32 devices in a mesh: grid: 8 (over z, x), dom: 4 (over y, core).
Axes of the slice: x: 2, y: 2, z: 4, core: 2. Of those that a mesh axis runs over, the one named last changes fastest.
Arguments:
- nodal_values: float32 [8, 64, 64, 256], P('grid', 'dom'), may hold values from -6 to 6
- level_vectors: int32 [8, 4], replicated, may hold values from 1 to 5, as said below
- coefficients: int32 [8], replicated, may hold values from -2 to 2, as said below
- velocity: float32 [6], replicated, may hold values from 0.5 to 2
Outputs:
- combined_field: float32 [8, 64, 64, 256], P('grid', 'dom')
The draws below stay inside these ranges and needn't reach their ends.
Inputs may be any that keep to these rules, and one draw needn't show every extreme that they name: `level_vectors`: columns 0 and 1 sum to 6, columns 2 and 3 sum to 5. `coefficients`: never zero.
All inputs are finite; a program needn't handle non-finite values.
Results may differ from the reference program's by a relative error of at most 0.0003.
Values sent between devices are 32-bit elements; how exact they have to be, the bound alone decides.
A program may use at most 128 MiB of HBM per device.

```python
import math
import jax
import jax.numpy as jnp
import numpy as np
from jax import lax

MLEV = 6
KSUM = 5
L6 = 3
STEPS = 4
NGRIDS = 8
N1 = 64
M = 64
K = 256


def draw_level_vectors(key, part):
    outer_level = jax.random.randint(jax.random.fold_in(key, 11), (NGRIDS,), 1, MLEV)
    fourth_level = jax.random.randint(jax.random.fold_in(key, 12), (NGRIDS,), 1, KSUM)
    return jnp.stack([outer_level, MLEV - outer_level, fourth_level, KSUM - fourth_level], axis=1).astype(jnp.int32)


def draw_coefficients(key, part):
    magnitude = jax.random.randint(jax.random.fold_in(key, 21), (NGRIDS,), 1, 3)
    sign_bits = jax.random.randint(jax.random.fold_in(key, 22), (NGRIDS,), 0, 2)
    return (magnitude * (2 * sign_bits - 1)).astype(jnp.int32)


def shard_levels(key, shape, shards, least, top_value):
    def one(dim, parts):
        heights = jax.random.uniform(jax.random.fold_in(jax.random.fold_in(key, 6), dim), (parts,), jnp.float32, least / len(shards), top_value / len(shards))
        return jnp.repeat(jnp.exp(heights), shape[dim] // parts).reshape((-1,) + (1,) * (len(shape) - dim - 1))

    loudness = one(*shards[0])
    for cut in shards[1:]:
        loudness = loudness * one(*cut)
    return loudness


def scatter_about(stream_key, dims, scale, bound, pieces=(), kind=jnp.bfloat16):
    drawn = jax.random.normal(stream_key, dims, jnp.float32) * scale
    if len(pieces) > 0:
        drawn = shard_levels(stream_key, dims, pieces, -0.22, 0.18) * drawn
    return jnp.clip(drawn, min=-bound, max=bound).astype(kind)


def setup_inputs(seed: int = 0) -> dict:
    seeds = jax.random.split(jax.random.key(seed), 5)
    nodal_values = scatter_about(seeds[0], (NGRIDS, N1, M, K), 1.0, 6.0, ((0, 8), (1, 4)), jnp.float32)
    level_vectors = draw_level_vectors(jax.random.fold_in(seeds[4], 71), 0)
    coefficients = draw_coefficients(jax.random.fold_in(seeds[4], 71), 0)
    velocity = jnp.clip(jnp.exp(jax.random.uniform(seeds[3], (6,), jnp.float32, math.log(0.5), math.log(2.0))), 0.5, 2.0)
    return {"nodal_values": nodal_values, "level_vectors": level_vectors, "coefficients": coefficients, "velocity": velocity}


CFL_LIMIT = 0.9
exact_mode = lax.Precision.HIGHEST


def level_of(number, finest):
    if number == 0:
        return 0
    return finest - ((number & -number).bit_length() - 1)


def union_slots(level_sum):
    finest = level_sum - 1
    outer_list = []
    inner_list = []
    for outer_cell in range(2 ** finest):
        for inner_cell in range(2 ** finest):
            if level_of(outer_cell, finest) + level_of(inner_cell, finest) <= level_sum:
                outer_list.append(outer_cell)
                inner_list.append(inner_cell)
    return np.array(outer_list, np.int32), np.array(inner_list, np.int32)


def slot_lists_k():
    outer_slots, inner_slots = union_slots(KSUM)
    repeat_count = 2 ** L6
    return [np.repeat(outer_slots, repeat_count), np.repeat(inner_slots, repeat_count),
            np.tile(np.arange(repeat_count, dtype=np.int32), outer_slots.shape[0])]


def split_flat(length, levels):
    flat_index = jnp.arange(length, dtype=jnp.int32)
    coordinates = []
    offset = jnp.int32(0)
    for grid_level in reversed(levels):
        coordinates.append(jnp.right_shift(flat_index, offset) & (jnp.left_shift(1, grid_level) - 1))
        offset = offset + grid_level
    return coordinates[::-1]


def surplus_entry(source, target, grid_level):
    wrap_mask = jnp.left_shift(1, grid_level) - 1
    lowest = target & (-target)
    before_cell = (target - lowest) & wrap_mask
    after_cell = (target + lowest) & wrap_mask
    nearby = (source == before_cell).astype(jnp.float32) + (source == after_cell).astype(jnp.float32)
    return (source == target).astype(jnp.float32) - 0.5 * jnp.where(target != 0, nearby, 0.0)


def basis_entry(source, target, grid_level):
    extent = jnp.left_shift(1, grid_level)
    lowest = jnp.maximum(source & (-source), 1)
    distance = jnp.abs(target - source)
    distance = jnp.minimum(distance, extent - distance)
    tent_value = jnp.maximum(1.0 - distance.astype(jnp.float32) / lowest.astype(jnp.float32), 0.0)
    return jnp.where(source == 0, 1.0, tent_value)


def axis_matrix(length, levels, transformed, entry):
    positions = split_flat(length, levels)
    matrix = jnp.ones((length, length), jnp.float32)
    for position, grid_level, active in zip(positions, levels, transformed):
        if active:
            matrix = matrix * entry(position[:, None], position[None, :], grid_level)
        else:
            matrix = matrix * (position[:, None] == position[None, :]).astype(jnp.float32)
    return matrix


def transform_pair(levels_row, entry):
    matrix_m = axis_matrix(2 ** MLEV, [levels_row[0], levels_row[1]], [True, True], entry)
    matrix_k = axis_matrix(2 ** (KSUM + L6), [levels_row[2], levels_row[3], L6], [True, True, False], entry)
    return matrix_m, matrix_k


def apply_both(values, matrix_m, matrix_k):
    values = jnp.einsum("rmk,mn->rnk", values, matrix_m, precision=exact_mode)
    return jnp.einsum("rmk,kn->rmn", values, matrix_k, precision=exact_mode)


def fine_cells_m(levels_row):
    positions = split_flat(2 ** MLEV, [levels_row[0], levels_row[1]])
    return [jnp.left_shift(positions[0], MLEV - 1 - levels_row[0]),
            jnp.left_shift(positions[1], MLEV - 1 - levels_row[1])]


def fine_cells_k(levels_row):
    positions = split_flat(2 ** (KSUM + L6), [levels_row[2], levels_row[3], L6])
    return [jnp.left_shift(positions[0], KSUM - 1 - levels_row[2]),
            jnp.left_shift(positions[1], KSUM - 1 - levels_row[3]), positions[2]]


def match_matrix(row_cells, column_cells):
    matrix = jnp.ones((row_cells[0].shape[0], column_cells[0].shape[0]), jnp.float32)
    for row_part, column_part in zip(row_cells, column_cells):
        matrix = matrix * (row_part[:, None] == jnp.asarray(column_part)[None, :]).astype(jnp.float32)
    return matrix


def members(levels_row):
    slots_m = union_slots(MLEV)
    member_m = match_matrix(fine_cells_m(levels_row), [slots_m[0], slots_m[1]])
    member_k = match_matrix(fine_cells_k(levels_row), slot_lists_k())
    return member_m, member_k


def contains(fine_cells, columns, finest):
    inside = jnp.ones((columns[0].shape[0], fine_cells[0].shape[0]), jnp.float32)
    for fine_part, column in zip(fine_cells, columns):
        step_mask = jnp.left_shift(1, finest - column) - 1
        inside = inside * ((fine_part[None, :] & step_mask[:, None]) == 0).astype(jnp.float32)
    return inside


def weight_total(levels_row, level_vectors, coefficients):
    inside_m = contains(fine_cells_m(levels_row), [level_vectors[:, 0], level_vectors[:, 1]], MLEV - 1)
    inside_k = contains(fine_cells_k(levels_row)[:2], [level_vectors[:, 2], level_vectors[:, 3]], KSUM - 1)
    weights = jnp.abs(coefficients).astype(jnp.float32)
    return jnp.einsum("hm,hk->mk", inside_m * weights[:, None], inside_k, precision=exact_mode)


def courant_table(level_vectors, velocity, whole_rows):
    grid_count = level_vectors.shape[0]
    cell_counts = jnp.concatenate([
        jnp.full((grid_count, 1), whole_rows, dtype=jnp.int32),
        jnp.left_shift(1, level_vectors),
        jnp.full((grid_count, 1), 2 ** L6, dtype=jnp.int32)], axis=1).astype(jnp.float32)
    courant = cell_counts * velocity[None, :]
    step_size = CFL_LIMIT / jnp.max(jnp.sum(courant, axis=1))
    return courant * step_size


def rotate(values, offset, axis_dim):
    length = values.shape[axis_dim]
    doubled = jnp.concatenate([values, values], axis=axis_dim)
    start_cell = ((length - jnp.asarray(offset, jnp.int32)) % length).astype(jnp.int32)
    return lax.dynamic_slice_in_dim(doubled, start_cell, length, axis_dim)


def shifted(values, stride, block_len, axis_dim):
    cell_index = jnp.arange(values.shape[axis_dim], dtype=jnp.int32)
    if axis_dim == 1:
        cell_index = cell_index[:, None]
    inside = (cell_index % block_len) >= stride
    return jnp.where(inside, rotate(values, stride, axis_dim), rotate(values, stride - block_len, axis_dim))


def advect(values, below, courant, levels_row):
    width_m = values.shape[1]
    width_k = values.shape[2]
    inner_m = jnp.left_shift(1, levels_row[1])
    inner_k = jnp.left_shift(1, levels_row[3] + L6)
    cell_six = 2 ** L6
    result = values - courant[0] * (values - below)
    result = result - courant[1] * (values - shifted(values, inner_m, width_m, 1))
    result = result - courant[2] * (values - shifted(values, 1, inner_m, 1))
    result = result - courant[3] * (values - shifted(values, inner_k, width_k, 2))
    result = result - courant[4] * (values - shifted(values, cell_six, inner_k, 2))
    result = result - courant[5] * (values - shifted(values, 1, cell_six, 2))
    return result


def reference(nodal_values, level_vectors, coefficients, velocity):
    rates_all = courant_table(level_vectors, velocity, N1)

    def evolve(entries):
        values, levels_row, courant = entries
        for step_index in range(STEPS):
            values = advect(values, jnp.roll(values, 1, axis=0), courant, levels_row)
        matrix_m, matrix_k = transform_pair(levels_row, surplus_entry)
        return apply_both(values, matrix_m, matrix_k)

    surplus = lax.map(evolve, (nodal_values, level_vectors, rates_all))
    slot_count_m = union_slots(MLEV)[0].shape[0]
    slot_count_k = slot_lists_k()[0].shape[0]

    def accumulate(buffer, entries):
        values, levels_row, weight = entries
        member_m, member_k = members(levels_row)
        spread = jnp.einsum("rmk,ks->rms", values * weight, member_k, precision=exact_mode)
        spread = jnp.einsum("rms,mu->rus", spread, member_m, precision=exact_mode)
        return buffer + spread, None

    initial = jnp.zeros((nodal_values.shape[1], slot_count_m, slot_count_k), jnp.float32)
    buffer, unused = lax.scan(accumulate, initial, (surplus, level_vectors, coefficients.astype(jnp.float32)))

    def finish(levels_row):
        member_m, member_k = members(levels_row)
        gathered = jnp.einsum("rus,mu->rms", buffer, member_m, precision=exact_mode)
        gathered = jnp.einsum("rms,ks->rmk", gathered, member_k, precision=exact_mode)
        combined = gathered / weight_total(levels_row, level_vectors, coefficients)[None]
        matrix_m, matrix_k = transform_pair(levels_row, basis_entry)
        return apply_both(combined, matrix_m, matrix_k)

    return lax.map(finish, level_vectors)
```

```python
import functools
import math

import jax
import jax.numpy as jnp
import numpy as np
from jax import lax
from jax.experimental import pallas as pl
from jax.experimental.pallas import tpu as pltpu
from jax.sharding import PartitionSpec as P

MLEV = 6
KSUM = 5
L6 = 3
STEPS = 4
CFL_LIMIT = 0.9

MESH = pl.DeviceIdType.MESH
F32 = jnp.float32
BF16 = jnp.bfloat16


def level_of(number, finest):
    return 0 if number == 0 else finest - ((number & -number).bit_length() - 1)


def union_points(level_sum):
    finest = level_sum - 1
    return [
        (a, b)
        for a in range(2**finest)
        for b in range(2**finest)
        if level_of(a, finest) + level_of(b, finest) <= level_sum
    ]


def surplus_line(level):
    size = 2**level
    matrix = np.eye(size, dtype=np.float32)
    for target in range(1, size):
        lowest = target & -target
        matrix[(target - lowest) % size, target] -= 0.5
        matrix[(target + lowest) % size, target] -= 0.5
    return matrix


def basis_line(level):
    size = 2**level
    matrix = np.zeros((size, size), np.float32)
    matrix[0] = 1.0
    for source in range(1, size):
        lowest = source & -source
        for target in range(size):
            distance = abs(target - source)
            distance = min(distance, size - distance)
            matrix[source, target] = max(0.0, 1.0 - distance / lowest)
    return matrix


def grid_points(outer, inner, level_sum):
    finest = level_sum - 1
    return {
        (i << (finest - outer), j << (finest - inner)): i * 2**inner + j
        for i in range(2**outer)
        for j in range(2**inner)
    }


@functools.lru_cache(None)
def tables():
    slots = union_points(MLEV)
    cells = 2**MLEV
    classes_m = MLEV - 1
    surplus_m = np.zeros((classes_m, len(slots), cells), np.float32)
    basis_m = np.zeros((classes_m, cells, len(slots)), np.float32)
    inside_m = np.zeros((len(slots), 8), np.float32)
    for a in range(classes_m):
        outer, inner = a + 1, MLEV - a - 1
        lines = np.kron(surplus_line(outer), surplus_line(inner))
        tents = np.kron(basis_line(outer), basis_line(inner))
        points = grid_points(outer, inner, MLEV)
        for s, point in enumerate(slots):
            if point in points:
                surplus_m[a, s] = lines[:, points[point]]
                basis_m[a, :, s] = tents[points[point]]
                inside_m[s, a] = 1.0
    classes_k = KSUM - 1
    cells = 2**KSUM
    move_k = np.zeros((classes_k * cells, classes_k * cells), np.float32)
    basis_k = np.zeros((classes_k * cells, classes_k * cells), np.float32)
    inside_k = np.zeros((8, classes_k * cells * 2**L6), np.float32)
    for b in range(classes_k):
        outer, inner = b + 1, KSUM - b - 1
        lines = np.kron(surplus_line(outer), surplus_line(inner))
        tents = np.kron(basis_line(outer), basis_line(inner))
        block = slice(b * cells, (b + 1) * cells)
        basis_k[block, block] = tents
        points = grid_points(outer, inner, KSUM)
        for other in range(classes_k):
            for point, cell in grid_points(other + 1, KSUM - other - 1, KSUM).items():
                if point in points:
                    column = other * cells + cell
                    move_k[block, column] = lines[:, points[point]]
                    inside_k[b, column * 2**L6 : (column + 1) * 2**L6] = 1.0
    return surplus_m, basis_m, inside_m, move_k, basis_k, inside_k


def halves(x):
    high = x.astype(BF16)
    return high, (x - high.astype(F32)).astype(BF16)


def dot(a, b):
    return jnp.dot(a, b, preferred_element_type=F32)


def iota(shape, dim):
    return lax.broadcasted_iota(jnp.int32, shape, dim)


def direct_kernel(
    grids, doms, x_ref, level_ref, coef_ref, velocity_ref, sm_hbm, bm_hbm, im_hbm, mk_hbm, bk_hbm, ik_hbm,
    out_ref, power, adv, recv, res, mat_k, mat_m, spread, gather, move, basis, inverse,
    sm_ref, bm_ref, im_ref, mk_ref, bk_ref, ik_ref,
    load_sem, halo_sem, send_sem, recv_sem, back_send, back_recv,
):
    rows, cells_m, cells_k = x_ref.shape[1:]
    chunk = max(1, rows // grids)
    workers = rows // chunk
    slots = im_ref.shape[0]
    classes_m = sm_ref.shape[0]
    classes_k = mk_ref.shape[0] // 2**KSUM
    span = STEPS * cells_m
    groups = rows // STEPS + 1
    half = grids // 2
    me = lax.axis_index("grid")
    here = lax.axis_index("dom")
    above = lax.rem(here + 1, doms)
    below = lax.rem(here + doms - 1, doms)

    side, seat = lax.div(me, half), lax.rem(me, half)
    peers = [(1 - side) * half + lax.rem(seat + i, half) for i in range(half)]
    peers += [side * half + lax.rem(seat + i, half) for i in range(1, half)]

    loads = [pltpu.make_async_copy(x_ref.at[0], power.at[0, pl.ds(STEPS, rows)], load_sem.at[0])]
    for i, (source, target) in enumerate([
        (sm_hbm, sm_ref), (bm_hbm, bm_ref), (im_hbm, im_ref), (mk_hbm, mk_ref), (bk_hbm, bk_ref), (ik_hbm, ik_ref),
    ]):
        loads.append(pltpu.make_async_copy(source, target, load_sem.at[i + 1]))
    loads[0].start()

    barrier = pltpu.get_barrier_semaphore()
    for peer in peers:
        pl.semaphore_signal(barrier, inc=1, device_id={"grid": peer}, device_id_type=MESH)
    for other in (above, below):
        pl.semaphore_signal(barrier, inc=1, device_id={"dom": other}, device_id_type=MESH)
    for load in loads[1:]:
        load.start()

    def counts(g):
        return [jnp.float32(rows * doms)] + [
            lax.shift_left(jnp.int32(1), level_ref[i, g]).astype(F32) for i in range(4)
        ] + [jnp.float32(2**L6)]

    fastest = None
    for g in range(grids):
        total = None
        for d, n in enumerate(counts(g)):
            term = n * velocity_ref[d]
            total = term if total is None else total + term
        fastest = total if fastest is None else jnp.maximum(fastest, total)
    step_size = CFL_LIMIT / jnp.full((8, 128), fastest, F32)
    step_size = step_size[0:1, 0:1]
    rate = [n * velocity_ref[d] * step_size for d, n in enumerate(counts(me))]
    stay = 1.0 - rate[0] - rate[1] - rate[2] - rate[3] - rate[4] - rate[5]

    inner_k = lax.shift_left(jnp.int32(1), level_ref[3, me] + L6)
    source, target = iota((cells_k, cells_k), 0), iota((cells_k, cells_k), 1)
    matrix = jnp.where(source == target, stay, 0.0)
    matrix += jnp.where(source == ((target - inner_k) & (cells_k - 1)), rate[3], 0.0)
    low = inner_k - 1
    matrix += jnp.where(source == ((target & ~low) | ((target - 2**L6) & low)), rate[4], 0.0)
    low = 2**L6 - 1
    matrix += jnp.where(source == ((target & ~low) | ((target - 1) & low)), rate[5], 0.0)
    high, rest = halves(matrix)
    mat_k[0] = high
    mat_k[1] = rest
    inner_m = lax.shift_left(jnp.int32(1), level_ref[1, me])
    target, source = iota((span, span), 0), iota((span, span), 1)
    low = jnp.int32(cells_m - 1)
    matrix = jnp.where(source == ((target & ~low) | ((target - inner_m) & low)), rate[1], 0.0)
    low = inner_m - 1
    matrix += jnp.where(source == ((target & ~low) | ((target - 1) & low)), rate[2], 0.0)
    high, rest = halves(matrix)
    mat_m[0] = high
    mat_m[1] = rest

    def raise_group(q):
        now = power[0, pl.ds(q * STEPS, STEPS)].reshape(span, cells_k)
        for step in range(STEPS):
            high, rest = halves(now)
            now = dot(high, mat_k[0]) + dot(rest, mat_k[0]) + dot(high, mat_k[1])
            now += dot(mat_m[0], high) + dot(mat_m[0], rest) + dot(mat_m[1], high)
            power[step + 1, pl.ds(q * STEPS, STEPS)] = now.reshape(STEPS, cells_m, cells_k)

    def send(row, peer):
        return pltpu.make_async_remote_copy(
            src_ref=adv.at[peer * chunk + row],
            dst_ref=recv.at[row, me],
            send_sem=send_sem.at[row, peer],
            recv_sem=recv_sem.at[row, me],
            device_id={"grid": peer},
            device_id_type=MESH,
        )

    def arrival(row, peer):
        return pltpu.make_async_remote_copy(
            src_ref=adv.at[row],
            dst_ref=recv.at[row, peer],
            send_sem=send_sem.at[row, peer],
            recv_sem=recv_sem.at[row, peer],
            device_id={"grid": peer},
            device_id_type=MESH,
        )

    def start_send(row, peer, ready):
        if workers < grids:
            valid = peer < workers
            ready = valid if ready is None else ready & valid
        if ready is None:
            send(row, peer).start()
        else:
            pl.when(ready)(lambda: send(row, peer).start())

    def finish_group(q):
        value, factor = None, None
        for j in range(STEPS + 1):
            term = power[STEPS - j, pl.ds(q * STEPS - j, STEPS)]
            if j > 0:
                factor = rate[0] if j == 1 else factor * rate[0]
                term = term * (math.comb(STEPS, j) * factor)
            value = term if value is None else value + term
        adv[pl.ds((q - 1) * STEPS, STEPS)] = value
        for peer in peers:
            place = peer * chunk
            start_send(0, peer, (place >= (q - 1) * STEPS) & (place < q * STEPS))

    loads[0].wait()
    first = jnp.where(side == 0, groups // 2, 1)
    raise_group(first)
    pl.semaphore_wait(barrier, grids + 1)
    halo_copy = pltpu.make_async_remote_copy(
        src_ref=x_ref.at[0, pl.ds(rows - STEPS, STEPS)],
        dst_ref=power.at[0, pl.ds(0, STEPS)],
        send_sem=halo_sem.at[0],
        recv_sem=halo_sem.at[1],
        device_id={"dom": above},
        device_id_type=MESH,
    )
    halo_copy.start()

    def one(i, carry):
        q = lax.rem(first + i, groups)
        pl.when(q == 0)(halo_copy.wait)
        raise_group(q)
        pl.when(q > 0)(lambda: finish_group(q))
        return carry

    lax.fori_loop(1, groups, one, 0)
    finish_group(first)
    for row in range(1, chunk):
        for peer in peers:
            start_send(row, peer, None)

    def give_back(row, peer):
        return pltpu.make_async_remote_copy(
            src_ref=res.at[row, peer],
            dst_ref=out_ref.at[0, me * chunk + row],
            send_sem=back_send.at[row, peer],
            recv_sem=back_recv.at[row, me],
            device_id={"grid": peer},
            device_id_type=MESH,
        )

    def returned(row, peer):
        return pltpu.make_async_remote_copy(
            src_ref=res.at[row, peer],
            dst_ref=out_ref.at[0, peer * chunk + row],
            send_sem=back_send.at[row, peer],
            recv_sem=back_recv.at[row, peer],
            device_id={"grid": peer},
            device_id_type=MESH,
        )

    for load in loads[1:]:
        load.wait()

    def when_worker(body):
        if workers < grids:
            pl.when(me < workers)(body)
        else:
            body()

    @when_worker
    def _():
        for row in range(chunk):
            recv[row, me] = adv[me * chunk + row]

        weights = [[F32(0.0)] * classes_k for _ in range(classes_m)]
        for g in range(grids):
            level_m, level_k = level_ref[0, g], level_ref[2, g]
            weight = coef_ref[g].astype(F32)
            place = jnp.clip(level_m - 1, 0, classes_m - 1)
            lines = sm_ref[place]
            tents = bm_ref[place]
            for b in range(classes_k):
                match = level_k == b + 1
                spread[b * slots : (b + 1) * slots, g * cells_m : (g + 1) * cells_m] = (
                    lines * jnp.where(match, weight, 0.0)
                ).astype(BF16)
                gather[g * cells_m : (g + 1) * cells_m, b * slots : (b + 1) * slots] = (
                    tents * jnp.where(match, 1.0, 0.0)
                ).astype(BF16)
                size = jnp.where(match, jnp.abs(weight), 0.0)
                for a in range(classes_m):
                    weights[a][b] = weights[a][b] + jnp.where(level_m == a + 1, size, 0.0)
        total = None
        for b in range(classes_k):
            column = None
            for a in range(classes_m):
                term = weights[a][b] * im_ref[:, a : a + 1]
                column = term if column is None else column + term
            term = column * ik_ref[b : b + 1, :]
            total = term if total is None else total + term
        inverse[...] = 1.0 / jnp.maximum(total, 1.0)
        small = classes_k * 2**KSUM
        for b in range(classes_k):
            place = iota((cells_k, small), 0) + b * cells_k
            repeat = (lax.shift_right_logical(place, L6) == iota((cells_k, small), 1)).astype(F32)
            repeat = repeat.astype(BF16)
            left = dot(repeat, mk_ref[...]).astype(BF16)
            left_basis = dot(repeat, bk_ref[...]).astype(BF16)
            for c in range(classes_k):
                place = iota((small, cells_k), 1) + c * cells_k
                widen = (lax.shift_right_logical(place, L6) == iota((small, cells_k), 0)).astype(F32)
                widen = widen.astype(BF16)
                same = (iota((cells_k, cells_k), 0) & (2**L6 - 1)) == (
                    iota((cells_k, cells_k), 1) & (2**L6 - 1)
                )
                move[b, :, c * cells_k : (c + 1) * cells_k] = jnp.where(
                    same, dot(left, widen), 0.0
                ).astype(BF16)
                if b == c:
                    basis[b] = jnp.where(same, dot(left_basis, widen), 0.0).astype(BF16)

        for row in range(chunk):
            for peer in peers:
                arrival(row, peer).wait_recv()
            high, rest = halves(recv[row].reshape(grids * cells_m, cells_k))
            union = None
            for b in range(classes_k):
                part = spread[b * slots : (b + 1) * slots, :]
                high_b, rest_b = halves(dot(part, high) + dot(part, rest))
                term = dot(high_b, move[b]) + dot(rest_b, move[b])
                union = term if union is None else union + term
            union = union * inverse[...]
            field = None
            for b in range(classes_k):
                high_b, rest_b = halves(union[:, b * cells_k : (b + 1) * cells_k])
                high_b, rest_b = halves(dot(high_b, basis[b]) + dot(rest_b, basis[b]))
                part = gather[:, b * slots : (b + 1) * slots]
                term = dot(part, high_b) + dot(part, rest_b)
                field = term if field is None else field + term
            res[row] = field.reshape(grids, cells_m, cells_k)
            for peer in peers:
                give_back(row, peer).start()
            out_ref[0, me * chunk + row] = res[row, me]

    for row in range(chunk):
        for peer in peers:

            def finish_peer(row=row, peer=peer):
                send(row, peer).wait_send()
                returned(row, peer).wait_recv()

            if workers < grids:
                pl.when(peer < workers)(finish_peer)
            else:
                finish_peer()
            when_worker(lambda row=row, peer=peer: give_back(row, peer).wait_send())


ROUNDS_M = ((1, 1), (2, 2), (3, 3), (4, 4), (5, 5), (1, 2), (4, 5), (2, 3), (1, 3), (3, 4), (3, 5), (2, 4), (1, 4), (2, 5), (1, 5))
ROUNDS_K = ((1, 1), (4, 4), (2, 2), (1, 2), (3, 3), (3, 4), (2, 3), (1, 3), (2, 4), (1, 4))


def ordered_points(level_sum, order):
    finest = level_sum - 1
    found = {interval: [] for interval in order}
    for a, b in union_points(level_sum):
        interval = max(level_of(a, finest), 1), min(level_sum - level_of(b, finest), finest)
        found[interval].append((a, b))
    return [(point, interval) for interval in order for point in found[interval]]


def hull(intervals):
    return min(low for low, _ in intervals), max(high for _, high in intervals)


@functools.lru_cache(None)
def staged_tables():
    slots_m = ordered_points(MLEV, ROUNDS_M)
    slots_k = ordered_points(KSUM, ROUNDS_K)
    lanes = 2**L6
    count_m, count_k = len(slots_m), len(slots_k) * lanes
    surplus_m = np.zeros((MLEV - 1, count_m, 2**MLEV), np.float32)
    basis_m = np.zeros((MLEV - 1, 2**MLEV, count_m), np.float32)
    inside_m = np.zeros((count_m, 8), np.float32)
    for a in range(MLEV - 1):
        outer, inner = a + 1, MLEV - a - 1
        lines = np.kron(surplus_line(outer), surplus_line(inner))
        tents = np.kron(basis_line(outer), basis_line(inner))
        points = grid_points(outer, inner, MLEV)
        for s, (point, _) in enumerate(slots_m):
            if point in points:
                surplus_m[a, s] = lines[:, points[point]]
                basis_m[a, :, s] = tents[points[point]]
                inside_m[s, a] = 1.0
    same = np.eye(lanes, dtype=np.float32)
    cells_k = 2 ** (KSUM + L6)
    surplus_k = np.zeros((KSUM - 1, cells_k, count_k), np.float32)
    basis_k = np.zeros((KSUM - 1, count_k, cells_k), np.float32)
    inside_k = np.zeros((8, count_k), np.float32)
    for b in range(KSUM - 1):
        outer, inner = b + 1, KSUM - b - 1
        lines = np.kron(surplus_line(outer), surplus_line(inner))
        tents = np.kron(basis_line(outer), basis_line(inner))
        points = grid_points(outer, inner, KSUM)
        for s, (point, _) in enumerate(slots_k):
            if point in points:
                place = slice(s * lanes, (s + 1) * lanes)
                surplus_k[b, :, place] = np.kron(lines[:, points[point]][:, None], same)
                basis_k[b, place] = np.kron(tents[points[point]][None, :], same)
                inside_k[b, place] = 1.0
    blocks_m = [hull([slots_m[8 * t + i][1] for i in range(8)]) for t in range(count_m // 8)]
    pairs_m = [hull(blocks_m[2 * t : 2 * t + 2]) for t in range(count_m // 16)]
    per = 64 // lanes
    halves_k = [hull([slots_k[per * t + i][1] for i in range(per)]) for t in range(count_k // 64)]
    tiles = []
    for first in (0, 2):
        tiles += [(block, hull(halves_k[first : first + 2])) for block in blocks_m]
    for column in range(4, 8):
        tiles += [(pair, halves_k[column]) for pair in pairs_m]
    tiles += [(block, hull(halves_k[8:10])) for block in blocks_m]
    return surplus_m, basis_m, inside_m, surplus_k, basis_k, inside_k, tiles


def shared_tiles(level_vectors):
    tiles = staged_tables()[-1]
    bounds = jnp.asarray(np.array([[*m, *k] for m, k in tiles], np.int32).T)
    level_m, level_k = level_vectors[:, 0:1], level_vectors[:, 2:3]
    touch = (bounds[0] <= level_m) & (level_m <= bounds[1]) & (bounds[2] <= level_k) & (level_k <= bounds[3])
    half = touch.shape[0] // 2
    return jnp.sum((jnp.any(touch[:half], axis=0) & jnp.any(touch[half:], axis=0)).astype(jnp.int32))


def shares(rows, half):
    chunk = rows // half
    outer = max(1, chunk // 2)
    return outer, 2 * chunk - outer


def staged_kernel(
    grids, doms, cap, x_ref, level_ref, coef_ref, velocity_ref, sm_hbm, bm_hbm, im_hbm, ek_hbm, tk_hbm, ik_hbm,
    out_ref, power, adv, recv, res, parts, pack, landed, taken, total, mat_k, mat_m, spread, gather, inverse,
    sm_ref, bm_ref, im_ref, ek_ref, tk_ref, ik_ref, after, place, chosen,
    load_sem, halo_sem, send_sem, recv_sem, cross_send, cross_recv, back_send, back_recv,
):
    rows, cells_m, cells_k = x_ref.shape[1:]
    slots_m, columns = im_ref.shape[0], ik_ref.shape[1]
    classes_m, classes_k = sm_ref.shape[0], ek_ref.shape[0]
    tiles = staged_tables()[-1]
    blocks = slots_m // 8
    span = STEPS * cells_m
    groups = rows // STEPS + 1
    half = grids // 2
    quarter = half // 2
    outer_rows, inner_rows = shares(rows, half)
    me = lax.axis_index("grid")
    here = lax.axis_index("dom")
    above = lax.rem(here + 1, doms)
    below = lax.rem(here + doms - 1, doms)
    side = lax.div(me, half)
    mine = lax.rem(me - side * half + side * quarter, half)
    my_rows = jnp.where(mine < quarter, outer_rows, inner_rows)

    def grid_of(seat, which):
        return which * half + lax.rem(seat + which * quarter, half)

    def owner_of(order):
        late = order - half * outer_rows
        early = order < half * outer_rows
        owner = jnp.where(early, lax.rem(order, half), quarter + lax.rem(late + half * rows, quarter))
        slot = jnp.where(early, lax.div(order, half), outer_rows + lax.div(jnp.maximum(late, 0), quarter))
        return owner, slot

    def row_of(slot):
        early = slot < outer_rows
        order = jnp.where(early, slot * half + mine, half * outer_rows + (slot - outer_rows) * quarter + mine - quarter)
        return lax.rem(order + STEPS, rows)

    peers = [lax.rem(mine + i, half) for i in range(1, half)]
    across = grid_of(mine, 1 - side)

    loads = [pltpu.make_async_copy(x_ref.at[0], power.at[0, pl.ds(STEPS, rows)], load_sem.at[0])]
    for i, (source, target) in enumerate([
        (sm_hbm, sm_ref), (bm_hbm, bm_ref), (im_hbm, im_ref), (ek_hbm, ek_ref), (tk_hbm, tk_ref), (ik_hbm, ik_ref),
    ]):
        loads.append(pltpu.make_async_copy(source, target, load_sem.at[i + 1]))
    loads[0].start()

    barrier = pltpu.get_barrier_semaphore()
    for peer in peers:
        pl.semaphore_signal(barrier, inc=1, device_id={"grid": grid_of(peer, side)}, device_id_type=MESH)
    pl.semaphore_signal(barrier, inc=1, device_id={"grid": across}, device_id_type=MESH)
    for other in (above, below):
        pl.semaphore_signal(barrier, inc=1, device_id={"dom": other}, device_id_type=MESH)
    for load in loads[1:]:
        load.start()

    def counts(g):
        return [jnp.float32(rows * doms)] + [
            lax.shift_left(jnp.int32(1), level_ref[i, g]).astype(F32) for i in range(4)
        ] + [jnp.float32(2**L6)]

    fastest = None
    for g in range(grids):
        size = None
        for d, n in enumerate(counts(g)):
            term = n * velocity_ref[d]
            size = term if size is None else size + term
        fastest = size if fastest is None else jnp.maximum(fastest, size)
    step_size = CFL_LIMIT / jnp.full((8, 128), fastest, F32)
    step_size = step_size[0:1, 0:1]
    rate = [n * velocity_ref[d] * step_size for d, n in enumerate(counts(me))]
    stay = 1.0 - rate[0] - rate[1] - rate[2] - rate[3] - rate[4] - rate[5]

    inner_k = lax.shift_left(jnp.int32(1), level_ref[3, me] + L6)
    source, target = iota((cells_k, cells_k), 0), iota((cells_k, cells_k), 1)
    matrix = jnp.where(source == target, stay, 0.0)
    matrix += jnp.where(source == ((target - inner_k) & (cells_k - 1)), rate[3], 0.0)
    low = inner_k - 1
    matrix += jnp.where(source == ((target & ~low) | ((target - 2**L6) & low)), rate[4], 0.0)
    low = 2**L6 - 1
    matrix += jnp.where(source == ((target & ~low) | ((target - 1) & low)), rate[5], 0.0)
    high, rest = halves(matrix)
    mat_k[0] = high
    mat_k[1] = rest
    inner_m = lax.shift_left(jnp.int32(1), level_ref[1, me])
    target, source = iota((span, span), 0), iota((span, span), 1)
    low = jnp.int32(cells_m - 1)
    matrix = jnp.where(source == ((target & ~low) | ((target - inner_m) & low)), rate[1], 0.0)
    low = inner_m - 1
    matrix += jnp.where(source == ((target & ~low) | ((target - 1) & low)), rate[2], 0.0)
    high, rest = halves(matrix)
    mat_m[0] = high
    mat_m[1] = rest

    def raise_group(q):
        now = power[0, pl.ds(q * STEPS, STEPS)].reshape(span, cells_k)
        for step in range(STEPS):
            high, rest = halves(now)
            now = dot(high, mat_k[0]) + dot(rest, mat_k[0]) + dot(high, mat_k[1])
            now += dot(mat_m[0], high) + dot(mat_m[0], rest) + dot(mat_m[1], high)
            power[step + 1, pl.ds(q * STEPS, STEPS)] = now.reshape(STEPS, cells_m, cells_k)

    def send(row, owner, slot):
        return pltpu.make_async_remote_copy(
            src_ref=adv.at[row],
            dst_ref=recv.at[slot, mine],
            send_sem=send_sem.at[row],
            recv_sem=recv_sem.at[slot, mine],
            device_id={"grid": grid_of(owner, side)},
            device_id_type=MESH,
        )

    def arrival(slot, peer):
        return pltpu.make_async_remote_copy(
            src_ref=adv.at[0],
            dst_ref=recv.at[slot, peer],
            send_sem=send_sem.at[0],
            recv_sem=recv_sem.at[slot, peer],
            device_id={"grid": grid_of(peer, side)},
            device_id_type=MESH,
        )

    def finish_group(q):
        value, factor = None, None
        for j in range(STEPS + 1):
            term = power[STEPS - j, pl.ds(q * STEPS - j, STEPS)]
            if j > 0:
                factor = rate[0] if j == 1 else factor * rate[0]
                term = term * (math.comb(STEPS, j) * factor)
            value = term if value is None else value + term
        adv[pl.ds((q - 1) * STEPS, STEPS)] = value
        for j in range(STEPS):
            row = (q - 1) * STEPS + j
            owner, slot = owner_of(lax.rem(row + rows - STEPS, rows))
            pl.when(owner != mine)(lambda row=row, owner=owner, slot=slot: send(row, owner, slot).start())

    loads[0].wait()
    first = 1
    raise_group(first)
    pl.semaphore_wait(barrier, half + 2)
    halo_copy = pltpu.make_async_remote_copy(
        src_ref=x_ref.at[0, pl.ds(rows - STEPS, STEPS)],
        dst_ref=power.at[0, pl.ds(0, STEPS)],
        send_sem=halo_sem.at[0],
        recv_sem=halo_sem.at[1],
        device_id={"dom": above},
        device_id_type=MESH,
    )
    halo_copy.start()

    def one(i, carry):
        q = lax.rem(first + i, groups)
        pl.when(q == 0)(halo_copy.wait)
        raise_group(q)
        pl.when(q > 0)(lambda: finish_group(q))
        return carry

    lax.fori_loop(1, groups, one, 0)
    finish_group(first)

    for load in loads[1:]:
        load.wait()

    if cap < len(tiles):
        zero = jnp.int32(0)
        with_m, with_k = [zero] * (classes_m + 1), [zero] * (classes_k + 1)
        for g in range(grids):
            bit = jnp.int32(1 << g)
            for a in range(1, classes_m + 1):
                with_m[a] = with_m[a] | jnp.where(level_ref[0, g] == a, bit, zero)
            for b in range(1, classes_k + 1):
                with_k[b] = with_k[b] | jnp.where(level_ref[2, g] == b, bit, zero)

        def mask_of(table, interval):
            mask = zero
            for level in range(interval[0], interval[1] + 1):
                mask = mask | table[level]
            return mask

        masks_m = {m: mask_of(with_m, m) for m in sorted({m for m, _ in tiles})}
        masks_k = {k: mask_of(with_k, k) for k in sorted({k for _, k in tiles})}
        lower = jnp.int32((1 << half) - 1)
        count = zero
        for t, (m, k) in enumerate(tiles):
            both = masks_m[m] & masks_k[k]
            needed = ((both & lower) != 0) & ((both & ~lower) != 0)
            place[t] = jnp.where(needed, jnp.minimum(count, cap), cap)
            after[t] = needed.astype(jnp.int32)
            count = count + needed.astype(jnp.int32)
        following = jnp.int32(len(tiles) - 1)
        for t in reversed(range(len(tiles))):
            following = jnp.where(after[t] != 0, t, following)
            after[t] = following
        last = jnp.int32(-1)
        for i in range(cap):
            last = after[jnp.minimum(last + 1, len(tiles) - 1)]
            chosen[i] = last
        taken[cap] = jnp.zeros(taken.shape[1:], F32)

    weights = [[F32(0.0)] * classes_k for _ in range(classes_m)]
    for g in range(grids):
        level_m, level_k = level_ref[0, g], level_ref[2, g]
        weight = jnp.abs(coef_ref[g].astype(F32))
        for b in range(classes_k):
            size = jnp.where(level_k == b + 1, weight, 0.0)
            for a in range(classes_m):
                weights[a][b] = weights[a][b] + jnp.where(level_m == a + 1, size, 0.0)
    sums = None
    for b in range(classes_k):
        column = None
        for a in range(classes_m):
            term = weights[a][b] * im_ref[:, a : a + 1]
            column = term if column is None else column + term
        term = column * ik_ref[b : b + 1, :]
        sums = term if sums is None else sums + term

    def fold(values):
        lane = iota((slots_m // 2, 128), 1) < 64
        out = [values[:, :128], values[:, 128:256]]
        for first in (256, 384):
            pair = values[:, first : first + 128].reshape(blocks // 2, 2, 8, 128)
            even = pair[:, 0].reshape(slots_m // 2, 128)
            odd = pltpu.roll(pair[:, 1].reshape(slots_m // 2, 128), 64, 1)
            out += [jnp.where(lane, even, odd), jnp.where(lane, odd, even)]
        return out + [values[:, 512:640]]

    def store_folded(target, values):
        at = 0
        for part in fold(values):
            size = part.shape[0] // 8
            target[at : at + size] = part.reshape(size, 8, 128)
            at += size

    def load_unfolded(source):
        lane = iota((slots_m // 2, 128), 1) < 64
        wide = [source[i * blocks : (i + 1) * blocks].reshape(slots_m, 128) for i in (0, 1, 4)]
        out = wide[:2]
        for at in (2 * blocks, 3 * blocks):
            low = source[at : at + blocks // 2].reshape(slots_m // 2, 128)
            high = source[at + blocks // 2 : at + blocks].reshape(slots_m // 2, 128)
            even = jnp.where(lane, low, high).reshape(blocks // 2, 1, 8, 128)
            odd = pltpu.roll(jnp.where(lane, high, low), 64, 1).reshape(blocks // 2, 1, 8, 128)
            out.append(jnp.concatenate([even, odd], axis=1).reshape(slots_m, 128))
        return jnp.concatenate(out + wide[2:], axis=1)

    store_folded(inverse, 1.0 / jnp.maximum(sums, 1.0))

    seats = [grid_of(seat, side) for seat in range(half)]
    for seat, g in enumerate(seats):
        at = jnp.clip(level_ref[0, g] - 1, 0, classes_m - 1)
        lines = (sm_ref[at] * coef_ref[g].astype(F32)).astype(BF16)
        tents = bm_ref[at].astype(BF16)
        for copy in range(2):
            spread[:, (copy * half + seat) * cells_m : (copy * half + seat + 1) * cells_m] = lines
            gather[seat * cells_m : (seat + 1) * cells_m, copy * slots_m : (copy + 1) * slots_m] = tents

    def cross(slot):
        return pltpu.make_async_remote_copy(
            src_ref=pack.at[slot],
            dst_ref=landed.at[slot],
            send_sem=cross_send.at[slot],
            recv_sem=cross_recv.at[slot],
            device_id={"grid": across},
            device_id_type=MESH,
        )

    def give_back(slot, peer):
        return pltpu.make_async_remote_copy(
            src_ref=res.at[slot, peer],
            dst_ref=out_ref.at[0, row_of(slot)],
            send_sem=back_send.at[slot, peer],
            recv_sem=back_recv.at[row_of(slot)],
            device_id={"grid": grid_of(peer, side)},
            device_id_type=MESH,
        )

    def class_k(seat):
        return jnp.clip(level_ref[2, seats[seat]] - 1, 0, classes_k - 1)

    def collect(slot):
        recv[slot, mine] = adv[row_of(slot)]
        for peer in peers:
            arrival(slot, peer).wait_recv()
        wide = []
        for seat in range(half):
            both = dot(jnp.concatenate(halves(recv[slot, seat]), axis=0), ek_ref[class_k(seat)])
            wide.append(halves(both[:cells_m] + both[cells_m:]))
        wide = jnp.concatenate([high for high, _ in wide] + [rest for _, rest in wide], axis=0)
        store_folded(parts.at[slot], dot(spread[...], wide))
        for i in range(cap):
            pack[slot, i] = parts[slot, chosen[i] if cap < len(tiles) else i]
        cross(slot).start()

    def release(slot):
        cross(slot).wait_recv()
        taken[0:cap] = landed[slot]
        for t in range(len(tiles)):
            total[t] = (parts[slot, t] + taken[place[t] if cap < len(tiles) else t]) * inverse[t]
        both = jnp.concatenate(halves(load_unfolded(total)), axis=0)
        field = dot(gather[...], both)
        for seat in range(half):
            part = jnp.concatenate(halves(field[seat * cells_m : (seat + 1) * cells_m]), axis=0)
            both = dot(part, tk_ref[class_k(seat)])
            res[slot, seat] = both[:cells_m] + both[cells_m:]
        for peer in peers:
            give_back(slot, peer).start()
        out_ref[0, row_of(slot)] = res[slot, mine]

    def turn(slot, carry):
        pl.when(slot < my_rows)(lambda: collect(slot))
        pl.when((slot > 0) & (slot <= my_rows))(lambda: release(slot - 1))
        return carry

    lax.fori_loop(0, max(outer_rows, inner_rows) + 1, turn, 0)

    def finish_row(row, carry):
        owner, slot = owner_of(lax.rem(row + rows - STEPS, rows))

        @pl.when(owner != mine)
        def _():
            send(row, owner, slot).wait_send()
            pltpu.make_async_remote_copy(
                src_ref=res.at[0, 0],
                dst_ref=out_ref.at[0, row],
                send_sem=back_send.at[0, 0],
                recv_sem=back_recv.at[row],
                device_id={"grid": grid_of(owner, side)},
                device_id_type=MESH,
            ).wait_recv()

        return carry

    lax.fori_loop(0, rows, finish_row, 0)

    def finish_slot(slot, carry):
        cross(slot).wait_send()
        for peer in peers:
            give_back(slot, peer).wait_send()
        return carry

    lax.fori_loop(0, my_rows, finish_slot, 0)


def staged_call(grids, doms, cap, index, nodal_values, level_vectors, coefficients, velocity):
    rows, cells_m, cells_k = nodal_values.shape[1:]
    half = grids // 2
    most = max(shares(rows, half))
    surplus_m, basis_m, inside_m, surplus_k, basis_k, inside_k, tiles = staged_tables()
    slots_m, columns = inside_m.shape[0], inside_k.shape[1]
    vmem = pl.BlockSpec(memory_space=pltpu.VMEM)
    smem = pl.BlockSpec(memory_space=pltpu.SMEM)
    hbm = pl.BlockSpec(memory_space=pltpu.HBM)
    return pl.pallas_call(
        functools.partial(staged_kernel, grids, doms, cap),
        out_shape=pltpu.VMEM(nodal_values.shape, F32),
        in_specs=[hbm, smem, smem, smem] + [hbm] * 6,
        out_specs=vmem,
        scratch_shapes=[
            pltpu.VMEM((STEPS + 1, STEPS + rows, cells_m, cells_k), F32),
            pltpu.VMEM((rows, cells_m, cells_k), F32),
            pltpu.VMEM((most, half, cells_m, cells_k), F32),
            pltpu.VMEM((most, half, cells_m, cells_k), F32),
            pltpu.VMEM((most, len(tiles), 8, 128), F32),
            pltpu.VMEM((most, cap, 8, 128), F32),
            pltpu.VMEM((most, cap, 8, 128), F32),
            pltpu.VMEM((cap + 1, 8, 128), F32),
            pltpu.VMEM((len(tiles), 8, 128), F32),
            pltpu.VMEM((2, cells_k, cells_k), BF16),
            pltpu.VMEM((2, STEPS * cells_m, STEPS * cells_m), BF16),
            pltpu.VMEM((slots_m, 2 * half * cells_m), BF16),
            pltpu.VMEM((half * cells_m, 2 * slots_m), BF16),
            pltpu.VMEM((len(tiles), 8, 128), F32),
            pltpu.VMEM(surplus_m.shape, F32),
            pltpu.VMEM(basis_m.shape, F32),
            pltpu.VMEM(inside_m.shape, F32),
            pltpu.VMEM(surplus_k.shape, BF16),
            pltpu.VMEM(basis_k.shape, BF16),
            pltpu.VMEM(inside_k.shape, F32),
            pltpu.SMEM((len(tiles),), jnp.int32),
            pltpu.SMEM((len(tiles),), jnp.int32),
            pltpu.SMEM((cap,), jnp.int32),
            pltpu.SemaphoreType.DMA((7,)),
            pltpu.SemaphoreType.DMA((2,)),
            pltpu.SemaphoreType.DMA((rows,)),
            pltpu.SemaphoreType.DMA((most, half)),
            pltpu.SemaphoreType.DMA((most,)),
            pltpu.SemaphoreType.DMA((most,)),
            pltpu.SemaphoreType.DMA((most, half)),
            pltpu.SemaphoreType.DMA((rows,)),
        ],
        compiler_params=pltpu.CompilerParams(
            collective_id=index, has_side_effects=True, vmem_limit_bytes=62 * 2**20 + 2**19
        ),
        name="combine_staged",
    )(
        nodal_values,
        level_vectors.T,
        coefficients,
        velocity,
        jnp.asarray(surplus_m),
        jnp.asarray(basis_m),
        jnp.asarray(inside_m),
        jnp.asarray(surplus_k).astype(BF16),
        jnp.asarray(basis_k).astype(BF16),
        jnp.asarray(inside_k),
    )


def solution(mesh):
    grids, doms = mesh.shape["grid"], mesh.shape["dom"]

    def direct(nodal_values, level_vectors, coefficients, velocity):
        rows, cells_m, cells_k = nodal_values.shape[1:]
        chunk = max(1, rows // grids)
        surplus_m, basis_m, inside_m, move_k, basis_k, inside_k = tables()
        slots = inside_m.shape[0]
        classes_k = KSUM - 1
        vmem = pl.BlockSpec(memory_space=pltpu.VMEM)
        smem = pl.BlockSpec(memory_space=pltpu.SMEM)
        hbm = pl.BlockSpec(memory_space=pltpu.HBM)
        return pl.pallas_call(
            functools.partial(direct_kernel, grids, doms),
            out_shape=pltpu.VMEM(nodal_values.shape, F32),
            in_specs=[hbm, smem, smem, smem] + [hbm] * 6,
            out_specs=vmem,
            scratch_shapes=[
                pltpu.VMEM((STEPS + 1, STEPS + rows, cells_m, cells_k), F32),
                pltpu.VMEM((rows, cells_m, cells_k), F32),
                pltpu.VMEM((chunk, grids, cells_m, cells_k), F32),
                pltpu.VMEM((chunk, grids, cells_m, cells_k), F32),
                pltpu.VMEM((2, cells_k, cells_k), BF16),
                pltpu.VMEM((2, STEPS * cells_m, STEPS * cells_m), BF16),
                pltpu.VMEM((classes_k * slots, grids * cells_m), BF16),
                pltpu.VMEM((grids * cells_m, classes_k * slots), BF16),
                pltpu.VMEM((classes_k, cells_k, classes_k * cells_k), BF16),
                pltpu.VMEM((classes_k, cells_k, cells_k), BF16),
                pltpu.VMEM((slots, classes_k * cells_k), F32),
                pltpu.VMEM(surplus_m.shape, F32),
                pltpu.VMEM(basis_m.shape, F32),
                pltpu.VMEM(inside_m.shape, F32),
                pltpu.VMEM(move_k.shape, BF16),
                pltpu.VMEM(basis_k.shape, BF16),
                pltpu.VMEM(inside_k.shape, F32),
                pltpu.SemaphoreType.DMA((7,)),
                pltpu.SemaphoreType.DMA((2,)),
                pltpu.SemaphoreType.DMA((chunk, grids)),
                pltpu.SemaphoreType.DMA((chunk, grids)),
                pltpu.SemaphoreType.DMA((chunk, grids)),
                pltpu.SemaphoreType.DMA((chunk, grids)),
            ],
            compiler_params=pltpu.CompilerParams(
                collective_id=0, has_side_effects=True, vmem_limit_bytes=62 * 2**20 + 2**19
            ),
            name="combine",
        )(
            nodal_values,
            level_vectors.T,
            coefficients,
            velocity,
            jnp.asarray(surplus_m),
            jnp.asarray(basis_m),
            jnp.asarray(inside_m),
            jnp.asarray(move_k).astype(BF16),
            jnp.asarray(basis_k).astype(BF16),
            jnp.asarray(inside_k),
        )

    def shards(nodal_values, level_vectors, coefficients, velocity):
        arrays = nodal_values, level_vectors, coefficients, velocity
        rows = nodal_values.shape[1]
        half = grids // 2
        if grids % 4 or rows % half or rows % STEPS:
            return direct(*arrays)
        count = len(staged_tables()[-1])
        cap = min(count, half * 2 ** (MLEV + KSUM + L6) // 1024 * 5 // 8)
        staged = functools.partial(staged_call, grids, doms, cap, 1)
        if cap == count:
            return staged(*arrays)
        return lax.cond(shared_tiles(level_vectors) <= cap, staged, direct, *arrays)

    in_specs = (P("grid", "dom", None, None), P(), P(), P())
    out_specs = P("grid", "dom", None, None)
    return jax.shard_map(shards, mesh=mesh, in_specs=in_specs, out_specs=out_specs, check_vma=False)
```

```python
import functools
import math

import jax
import jax.numpy as jnp
import numpy as np
from jax import lax
from jax.experimental import pallas as pl
from jax.experimental.pallas import tpu as pltpu
from jax.sharding import PartitionSpec as P

MLEV = 6
KSUM = 5
L6 = 3
STEPS = 4
CFL_LIMIT = 0.9
LAG = 2
PARTS = (5, 6, 7, 8, 9, 10, 12)

MESH = pl.DeviceIdType.MESH
F32 = jnp.float32
BF16 = jnp.bfloat16


def level_of(number, finest):
    return 0 if number == 0 else finest - ((number & -number).bit_length() - 1)


def union_points(level_sum):
    finest = level_sum - 1
    return [
        (a, b)
        for a in range(2**finest)
        for b in range(2**finest)
        if level_of(a, finest) + level_of(b, finest) <= level_sum
    ]


def surplus_line(level):
    size = 2**level
    matrix = np.eye(size, dtype=np.float32)
    for target in range(1, size):
        lowest = target & -target
        matrix[(target - lowest) % size, target] -= 0.5
        matrix[(target + lowest) % size, target] -= 0.5
    return matrix


def basis_line(level):
    size = 2**level
    matrix = np.zeros((size, size), np.float32)
    matrix[0] = 1.0
    for source in range(1, size):
        lowest = source & -source
        for target in range(size):
            distance = abs(target - source)
            distance = min(distance, size - distance)
            matrix[source, target] = max(0.0, 1.0 - distance / lowest)
    return matrix


def grid_points(outer, inner, level_sum):
    finest = level_sum - 1
    return {
        (i << (finest - outer), j << (finest - inner)): i * 2**inner + j
        for i in range(2**outer)
        for j in range(2**inner)
    }


@functools.lru_cache(None)
def tables():
    slots = union_points(MLEV)
    cells = 2**MLEV
    classes_m = MLEV - 1
    surplus_m = np.zeros((classes_m, len(slots), cells), np.float32)
    basis_m = np.zeros((classes_m, cells, len(slots)), np.float32)
    inside_m = np.zeros((len(slots), 8), np.float32)
    for a in range(classes_m):
        outer, inner = a + 1, MLEV - a - 1
        lines = np.kron(surplus_line(outer), surplus_line(inner))
        tents = np.kron(basis_line(outer), basis_line(inner))
        points = grid_points(outer, inner, MLEV)
        for s, point in enumerate(slots):
            if point in points:
                surplus_m[a, s] = lines[:, points[point]]
                basis_m[a, :, s] = tents[points[point]]
                inside_m[s, a] = 1.0
    classes_k = KSUM - 1
    cells = 2**KSUM
    move_k = np.zeros((classes_k * cells, classes_k * cells), np.float32)
    basis_k = np.zeros((classes_k * cells, classes_k * cells), np.float32)
    inside_k = np.zeros((8, classes_k * cells * 2**L6), np.float32)
    for b in range(classes_k):
        outer, inner = b + 1, KSUM - b - 1
        lines = np.kron(surplus_line(outer), surplus_line(inner))
        tents = np.kron(basis_line(outer), basis_line(inner))
        block = slice(b * cells, (b + 1) * cells)
        basis_k[block, block] = tents
        points = grid_points(outer, inner, KSUM)
        for other in range(classes_k):
            for point, cell in grid_points(other + 1, KSUM - other - 1, KSUM).items():
                if point in points:
                    column = other * cells + cell
                    move_k[block, column] = lines[:, points[point]]
                    inside_k[b, column * 2**L6 : (column + 1) * 2**L6] = 1.0
    return surplus_m, basis_m, inside_m, move_k, basis_k, inside_k


def halves(x):
    high = x.astype(BF16)
    return high, (x - high.astype(F32)).astype(BF16)


def dot(a, b):
    return jnp.dot(a, b, preferred_element_type=F32)


def iota(shape, dim):
    return lax.broadcasted_iota(jnp.int32, shape, dim)


def direct_kernel(
    grids, doms, x_ref, level_ref, coef_ref, velocity_ref, sm_hbm, bm_hbm, im_hbm, mk_hbm, bk_hbm, ik_hbm,
    out_ref, power, adv, recv, res, mat_k, mat_m, spread, gather, move, basis, inverse,
    sm_ref, bm_ref, im_ref, mk_ref, bk_ref, ik_ref,
    load_sem, halo_sem, send_sem, recv_sem, back_send, back_recv,
):
    rows, cells_m, cells_k = x_ref.shape[1:]
    chunk = max(1, rows // grids)
    workers = rows // chunk
    slots = im_ref.shape[0]
    classes_m = sm_ref.shape[0]
    classes_k = mk_ref.shape[0] // 2**KSUM
    span = STEPS * cells_m
    groups = rows // STEPS + 1
    half = grids // 2
    me = lax.axis_index("grid")
    here = lax.axis_index("dom")
    above = lax.rem(here + 1, doms)
    below = lax.rem(here + doms - 1, doms)

    side, seat = lax.div(me, half), lax.rem(me, half)
    peers = [(1 - side) * half + lax.rem(seat + i, half) for i in range(half)]
    peers += [side * half + lax.rem(seat + i, half) for i in range(1, half)]

    loads = [pltpu.make_async_copy(x_ref.at[0], power.at[0, pl.ds(STEPS, rows)], load_sem.at[0])]
    for i, (source, target) in enumerate([
        (sm_hbm, sm_ref), (bm_hbm, bm_ref), (im_hbm, im_ref), (mk_hbm, mk_ref), (bk_hbm, bk_ref), (ik_hbm, ik_ref),
    ]):
        loads.append(pltpu.make_async_copy(source, target, load_sem.at[i + 1]))
    loads[0].start()

    barrier = pltpu.get_barrier_semaphore()
    for peer in peers:
        pl.semaphore_signal(barrier, inc=1, device_id={"grid": peer}, device_id_type=MESH)
    for other in (above, below):
        pl.semaphore_signal(barrier, inc=1, device_id={"dom": other}, device_id_type=MESH)
    for load in loads[1:]:
        load.start()

    def counts(g):
        return [jnp.float32(rows * doms)] + [
            lax.shift_left(jnp.int32(1), level_ref[i, g]).astype(F32) for i in range(4)
        ] + [jnp.float32(2**L6)]

    fastest = None
    for g in range(grids):
        total = None
        for d, n in enumerate(counts(g)):
            term = n * velocity_ref[d]
            total = term if total is None else total + term
        fastest = total if fastest is None else jnp.maximum(fastest, total)
    step_size = CFL_LIMIT / jnp.full((8, 128), fastest, F32)
    step_size = step_size[0:1, 0:1]
    rate = [n * velocity_ref[d] * step_size for d, n in enumerate(counts(me))]
    stay = 1.0 - rate[0] - rate[1] - rate[2] - rate[3] - rate[4] - rate[5]

    inner_k = lax.shift_left(jnp.int32(1), level_ref[3, me] + L6)
    source, target = iota((cells_k, cells_k), 0), iota((cells_k, cells_k), 1)
    matrix = jnp.where(source == target, stay, 0.0)
    matrix += jnp.where(source == ((target - inner_k) & (cells_k - 1)), rate[3], 0.0)
    low = inner_k - 1
    matrix += jnp.where(source == ((target & ~low) | ((target - 2**L6) & low)), rate[4], 0.0)
    low = 2**L6 - 1
    matrix += jnp.where(source == ((target & ~low) | ((target - 1) & low)), rate[5], 0.0)
    high, rest = halves(matrix)
    mat_k[0] = high
    mat_k[1] = rest
    inner_m = lax.shift_left(jnp.int32(1), level_ref[1, me])
    target, source = iota((span, span), 0), iota((span, span), 1)
    low = jnp.int32(cells_m - 1)
    matrix = jnp.where(source == ((target & ~low) | ((target - inner_m) & low)), rate[1], 0.0)
    low = inner_m - 1
    matrix += jnp.where(source == ((target & ~low) | ((target - 1) & low)), rate[2], 0.0)
    high, rest = halves(matrix)
    mat_m[0] = high
    mat_m[1] = rest

    def raise_group(q):
        now = power[0, pl.ds(q * STEPS, STEPS)].reshape(span, cells_k)
        for step in range(STEPS):
            high, rest = halves(now)
            now = dot(high, mat_k[0]) + dot(rest, mat_k[0]) + dot(high, mat_k[1])
            now += dot(mat_m[0], high) + dot(mat_m[0], rest) + dot(mat_m[1], high)
            power[step + 1, pl.ds(q * STEPS, STEPS)] = now.reshape(STEPS, cells_m, cells_k)

    def send(row, peer):
        return pltpu.make_async_remote_copy(
            src_ref=adv.at[peer * chunk + row],
            dst_ref=recv.at[row, me],
            send_sem=send_sem.at[row, peer],
            recv_sem=recv_sem.at[row, me],
            device_id={"grid": peer},
            device_id_type=MESH,
        )

    def arrival(row, peer):
        return pltpu.make_async_remote_copy(
            src_ref=adv.at[row],
            dst_ref=recv.at[row, peer],
            send_sem=send_sem.at[row, peer],
            recv_sem=recv_sem.at[row, peer],
            device_id={"grid": peer},
            device_id_type=MESH,
        )

    def start_send(row, peer, ready):
        if workers < grids:
            valid = peer < workers
            ready = valid if ready is None else ready & valid
        if ready is None:
            send(row, peer).start()
        else:
            pl.when(ready)(lambda: send(row, peer).start())

    def finish_group(q):
        value, factor = None, None
        for j in range(STEPS + 1):
            term = power[STEPS - j, pl.ds(q * STEPS - j, STEPS)]
            if j > 0:
                factor = rate[0] if j == 1 else factor * rate[0]
                term = term * (math.comb(STEPS, j) * factor)
            value = term if value is None else value + term
        adv[pl.ds((q - 1) * STEPS, STEPS)] = value
        for peer in peers:
            place = peer * chunk
            start_send(0, peer, (place >= (q - 1) * STEPS) & (place < q * STEPS))

    loads[0].wait()
    first = jnp.where(side == 0, groups // 2, 1)
    raise_group(first)
    pl.semaphore_wait(barrier, grids + 1)
    halo_copy = pltpu.make_async_remote_copy(
        src_ref=x_ref.at[0, pl.ds(rows - STEPS, STEPS)],
        dst_ref=power.at[0, pl.ds(0, STEPS)],
        send_sem=halo_sem.at[0],
        recv_sem=halo_sem.at[1],
        device_id={"dom": above},
        device_id_type=MESH,
    )
    halo_copy.start()

    def one(i, carry):
        q = lax.rem(first + i, groups)
        pl.when(q == 0)(halo_copy.wait)
        raise_group(q)
        pl.when(q > 0)(lambda: finish_group(q))
        return carry

    lax.fori_loop(1, groups, one, 0)
    finish_group(first)
    for row in range(1, chunk):
        for peer in peers:
            start_send(row, peer, None)

    def give_back(row, peer):
        return pltpu.make_async_remote_copy(
            src_ref=res.at[row, peer],
            dst_ref=out_ref.at[0, me * chunk + row],
            send_sem=back_send.at[row, peer],
            recv_sem=back_recv.at[row, me],
            device_id={"grid": peer},
            device_id_type=MESH,
        )

    def returned(row, peer):
        return pltpu.make_async_remote_copy(
            src_ref=res.at[row, peer],
            dst_ref=out_ref.at[0, peer * chunk + row],
            send_sem=back_send.at[row, peer],
            recv_sem=back_recv.at[row, peer],
            device_id={"grid": peer},
            device_id_type=MESH,
        )

    for load in loads[1:]:
        load.wait()

    def when_worker(body):
        if workers < grids:
            pl.when(me < workers)(body)
        else:
            body()

    @when_worker
    def _():
        for row in range(chunk):
            recv[row, me] = adv[me * chunk + row]

        weights = [[F32(0.0)] * classes_k for _ in range(classes_m)]
        for g in range(grids):
            level_m, level_k = level_ref[0, g], level_ref[2, g]
            weight = coef_ref[g].astype(F32)
            place = jnp.clip(level_m - 1, 0, classes_m - 1)
            lines = sm_ref[place]
            tents = bm_ref[place]
            for b in range(classes_k):
                match = level_k == b + 1
                spread[b * slots : (b + 1) * slots, g * cells_m : (g + 1) * cells_m] = (
                    lines * jnp.where(match, weight, 0.0)
                ).astype(BF16)
                gather[g * cells_m : (g + 1) * cells_m, b * slots : (b + 1) * slots] = (
                    tents * jnp.where(match, 1.0, 0.0)
                ).astype(BF16)
                size = jnp.where(match, jnp.abs(weight), 0.0)
                for a in range(classes_m):
                    weights[a][b] = weights[a][b] + jnp.where(level_m == a + 1, size, 0.0)
        total = None
        for b in range(classes_k):
            column = None
            for a in range(classes_m):
                term = weights[a][b] * im_ref[:, a : a + 1]
                column = term if column is None else column + term
            term = column * ik_ref[b : b + 1, :]
            total = term if total is None else total + term
        inverse[...] = 1.0 / jnp.maximum(total, 1.0)
        small = classes_k * 2**KSUM
        for b in range(classes_k):
            place = iota((cells_k, small), 0) + b * cells_k
            repeat = (lax.shift_right_logical(place, L6) == iota((cells_k, small), 1)).astype(F32)
            repeat = repeat.astype(BF16)
            left = dot(repeat, mk_ref[...]).astype(BF16)
            left_basis = dot(repeat, bk_ref[...]).astype(BF16)
            for c in range(classes_k):
                place = iota((small, cells_k), 1) + c * cells_k
                widen = (lax.shift_right_logical(place, L6) == iota((small, cells_k), 0)).astype(F32)
                widen = widen.astype(BF16)
                same = (iota((cells_k, cells_k), 0) & (2**L6 - 1)) == (
                    iota((cells_k, cells_k), 1) & (2**L6 - 1)
                )
                move[b, :, c * cells_k : (c + 1) * cells_k] = jnp.where(
                    same, dot(left, widen), 0.0
                ).astype(BF16)
                if b == c:
                    basis[b] = jnp.where(same, dot(left_basis, widen), 0.0).astype(BF16)

        for row in range(chunk):
            for peer in peers:
                arrival(row, peer).wait_recv()
            high, rest = halves(recv[row].reshape(grids * cells_m, cells_k))
            union = None
            for b in range(classes_k):
                part = spread[b * slots : (b + 1) * slots, :]
                high_b, rest_b = halves(dot(part, high) + dot(part, rest))
                term = dot(high_b, move[b]) + dot(rest_b, move[b])
                union = term if union is None else union + term
            union = union * inverse[...]
            field = None
            for b in range(classes_k):
                high_b, rest_b = halves(union[:, b * cells_k : (b + 1) * cells_k])
                high_b, rest_b = halves(dot(high_b, basis[b]) + dot(rest_b, basis[b]))
                part = gather[:, b * slots : (b + 1) * slots]
                term = dot(part, high_b) + dot(part, rest_b)
                field = term if field is None else field + term
            res[row] = field.reshape(grids, cells_m, cells_k)
            for peer in peers:
                give_back(row, peer).start()
            out_ref[0, me * chunk + row] = res[row, me]

    for row in range(chunk):
        for peer in peers:

            def finish_peer(row=row, peer=peer):
                send(row, peer).wait_send()
                returned(row, peer).wait_recv()

            if workers < grids:
                pl.when(peer < workers)(finish_peer)
            else:
                finish_peer()
            when_worker(lambda row=row, peer=peer: give_back(row, peer).wait_send())


ROUNDS_M = ((1, 1), (2, 2), (3, 3), (4, 4), (5, 5), (1, 2), (4, 5), (2, 3), (1, 3), (3, 4), (3, 5), (2, 4), (1, 4), (2, 5), (1, 5))
ROUNDS_K = ((1, 1), (4, 4), (2, 2), (1, 2), (3, 3), (3, 4), (2, 3), (1, 3), (2, 4), (1, 4))


def ordered_points(level_sum, order):
    finest = level_sum - 1
    found = {interval: [] for interval in order}
    for a, b in union_points(level_sum):
        interval = max(level_of(a, finest), 1), min(level_sum - level_of(b, finest), finest)
        found[interval].append((a, b))
    return [(point, interval) for interval in order for point in found[interval]]


def hull(intervals):
    return min(low for low, _ in intervals), max(high for _, high in intervals)


@functools.lru_cache(None)
def staged_tables():
    slots_m = ordered_points(MLEV, ROUNDS_M)
    slots_k = ordered_points(KSUM, ROUNDS_K)
    lanes = 2**L6
    count_m, count_k = len(slots_m), len(slots_k) * lanes
    surplus_m = np.zeros((MLEV - 1, count_m, 2**MLEV), np.float32)
    basis_m = np.zeros((MLEV - 1, 2**MLEV, count_m), np.float32)
    inside_m = np.zeros((count_m, 8), np.float32)
    for a in range(MLEV - 1):
        outer, inner = a + 1, MLEV - a - 1
        lines = np.kron(surplus_line(outer), surplus_line(inner))
        tents = np.kron(basis_line(outer), basis_line(inner))
        points = grid_points(outer, inner, MLEV)
        for s, (point, _) in enumerate(slots_m):
            if point in points:
                surplus_m[a, s] = lines[:, points[point]]
                basis_m[a, :, s] = tents[points[point]]
                inside_m[s, a] = 1.0
    same = np.eye(lanes, dtype=np.float32)
    cells_k = 2 ** (KSUM + L6)
    surplus_k = np.zeros((KSUM - 1, cells_k, count_k), np.float32)
    basis_k = np.zeros((KSUM - 1, count_k, cells_k), np.float32)
    inside_k = np.zeros((8, count_k), np.float32)
    for b in range(KSUM - 1):
        outer, inner = b + 1, KSUM - b - 1
        lines = np.kron(surplus_line(outer), surplus_line(inner))
        tents = np.kron(basis_line(outer), basis_line(inner))
        points = grid_points(outer, inner, KSUM)
        for s, (point, _) in enumerate(slots_k):
            if point in points:
                place = slice(s * lanes, (s + 1) * lanes)
                surplus_k[b, :, place] = np.kron(lines[:, points[point]][:, None], same)
                basis_k[b, place] = np.kron(tents[points[point]][None, :], same)
                inside_k[b, place] = 1.0
    blocks_m = [hull([slots_m[8 * t + i][1] for i in range(8)]) for t in range(count_m // 8)]
    pairs_m = [hull(blocks_m[2 * t : 2 * t + 2]) for t in range(count_m // 16)]
    per = 64 // lanes
    halves_k = [hull([slots_k[per * t + i][1] for i in range(per)]) for t in range(count_k // 64)]
    tiles = []
    for first in (0, 2):
        tiles += [(block, hull(halves_k[first : first + 2])) for block in blocks_m]
    for column in range(4, 8):
        tiles += [(pair, halves_k[column]) for pair in pairs_m]
    tiles += [(block, hull(halves_k[8:10])) for block in blocks_m]
    return surplus_m, basis_m, inside_m, surplus_k, basis_k, inside_k, tiles


def shared_by_halves(grids, level_ref):
    tiles = staged_tables()[-1]
    zero = jnp.int32(0)
    with_m, with_k = [zero] * MLEV, [zero] * KSUM
    for g in range(grids):
        bit = jnp.int32(1 << g)
        for a in range(1, MLEV):
            with_m[a] = with_m[a] | jnp.where(level_ref[0, g] == a, bit, zero)
        for b in range(1, KSUM):
            with_k[b] = with_k[b] | jnp.where(level_ref[2, g] == b, bit, zero)

    def mask_of(table, interval):
        return functools.reduce(jnp.bitwise_or, table[interval[0] : interval[1] + 1])

    masks_m = {m: mask_of(with_m, m) for m in sorted({m for m, _ in tiles})}
    masks_k = {k: mask_of(with_k, k) for k in sorted({k for _, k in tiles})}
    lower = jnp.int32((1 << grids // 2) - 1)
    shared = {}
    for tile in tiles:
        if tile not in shared:
            both = masks_m[tile[0]] & masks_k[tile[1]]
            shared[tile] = (((both & lower) != 0) & ((both & ~lower) != 0)).astype(jnp.int32)
    return [shared[tile] for tile in tiles]


def choice_kernel(grids, caps, level_ref, out_ref):
    count = sum(shared_by_halves(grids, level_ref))
    out_ref[0] = sum((count > cap).astype(jnp.int32) for cap in caps)


def choose(grids, caps, levels):
    smem = pl.BlockSpec(memory_space=pltpu.SMEM)
    return pl.pallas_call(
        functools.partial(choice_kernel, grids, caps),
        out_shape=jax.ShapeDtypeStruct((1,), jnp.int32),
        in_specs=[smem],
        out_specs=smem,
        name="choose",
    )(levels)[0]


def staged_kernel(
    grids, doms, cap, x_ref, level_ref, coef_ref, velocity_ref, sm_hbm, bm_hbm, im_hbm, ek_hbm, tk_hbm, ik_hbm,
    out_ref, power, adv, recv, res, parts, pack, landed, taken, total, mat_k, mat_m, spread, gather, inverse,
    sm_ref, bm_ref, im_ref, ek_ref, tk_ref, ik_ref, after, place, chosen,
    load_sem, halo_sem, send_sem, recv_sem, cross_send, cross_recv, back_send, back_recv,
):
    rows, cells_m, cells_k = x_ref.shape[1:]
    slots_m, columns = im_ref.shape[0], ik_ref.shape[1]
    classes_m, classes_k = sm_ref.shape[0], ek_ref.shape[0]
    tiles = staged_tables()[-1]
    blocks = slots_m // 8
    span = STEPS * cells_m
    groups = rows // STEPS + 1
    half = grids // 2
    quarter = half // 2
    chunk = rows // half
    me = lax.axis_index("grid")
    here = lax.axis_index("dom")
    above = lax.rem(here + 1, doms)
    below = lax.rem(here + doms - 1, doms)
    side = lax.div(me, half)
    mine = lax.rem(me - side * half + side * quarter, half)

    def grid_of(seat, which):
        return which * half + lax.rem(seat + which * quarter, half)

    def owner_of(order):
        return lax.rem(order, half), lax.div(order, half)

    def row_of(slot):
        return lax.rem(slot * half + mine + STEPS, rows)

    peers = [lax.rem(mine + i, half) for i in range(1, half)]
    across = grid_of(mine, 1 - side)

    loads = [pltpu.make_async_copy(x_ref.at[0], power.at[0, pl.ds(STEPS, rows)], load_sem.at[0])]
    for i, (source, target) in enumerate([
        (sm_hbm, sm_ref), (bm_hbm, bm_ref), (im_hbm, im_ref), (ek_hbm, ek_ref), (tk_hbm, tk_ref), (ik_hbm, ik_ref),
    ]):
        loads.append(pltpu.make_async_copy(source, target, load_sem.at[i + 1]))
    loads[0].start()

    barrier = pltpu.get_barrier_semaphore()
    for peer in peers:
        pl.semaphore_signal(barrier, inc=1, device_id={"grid": grid_of(peer, side)}, device_id_type=MESH)
    pl.semaphore_signal(barrier, inc=1, device_id={"grid": across}, device_id_type=MESH)
    for other in (above, below):
        pl.semaphore_signal(barrier, inc=1, device_id={"dom": other}, device_id_type=MESH)
    for load in loads[1:]:
        load.start()

    def counts(g):
        return [jnp.float32(rows * doms)] + [
            lax.shift_left(jnp.int32(1), level_ref[i, g]).astype(F32) for i in range(4)
        ] + [jnp.float32(2**L6)]

    fastest = None
    for g in range(grids):
        size = None
        for d, n in enumerate(counts(g)):
            term = n * velocity_ref[d]
            size = term if size is None else size + term
        fastest = size if fastest is None else jnp.maximum(fastest, size)
    step_size = CFL_LIMIT / jnp.full((8, 128), fastest, F32)
    step_size = step_size[0:1, 0:1]
    rate = [n * velocity_ref[d] * step_size for d, n in enumerate(counts(me))]
    stay = 1.0 - rate[0] - rate[1] - rate[2] - rate[3] - rate[4] - rate[5]

    inner_k = lax.shift_left(jnp.int32(1), level_ref[3, me] + L6)
    source, target = iota((cells_k, cells_k), 0), iota((cells_k, cells_k), 1)
    matrix = jnp.where(source == target, stay, 0.0)
    matrix += jnp.where(source == ((target - inner_k) & (cells_k - 1)), rate[3], 0.0)
    low = inner_k - 1
    matrix += jnp.where(source == ((target & ~low) | ((target - 2**L6) & low)), rate[4], 0.0)
    low = 2**L6 - 1
    matrix += jnp.where(source == ((target & ~low) | ((target - 1) & low)), rate[5], 0.0)
    high, rest = halves(matrix)
    mat_k[0] = high
    mat_k[1] = rest
    inner_m = lax.shift_left(jnp.int32(1), level_ref[1, me])
    target, source = iota((span, span), 0), iota((span, span), 1)
    low = jnp.int32(cells_m - 1)
    matrix = jnp.where(source == ((target & ~low) | ((target - inner_m) & low)), rate[1], 0.0)
    low = inner_m - 1
    matrix += jnp.where(source == ((target & ~low) | ((target - 1) & low)), rate[2], 0.0)
    high, rest = halves(matrix)
    mat_m[0] = high
    mat_m[1] = rest

    def raise_group(q, carry=None):
        now = power[0, pl.ds(q * STEPS, STEPS)].reshape(span, cells_k)
        for step in range(STEPS):
            high, rest = halves(now)
            now = dot(high, mat_k[0]) + dot(rest, mat_k[0]) + dot(high, mat_k[1])
            now += dot(mat_m[0], high) + dot(mat_m[0], rest) + dot(mat_m[1], high)
            power[step + 1, pl.ds(q * STEPS, STEPS)] = now.reshape(STEPS, cells_m, cells_k)
        return carry

    def send(row, owner, slot):
        return pltpu.make_async_remote_copy(
            src_ref=adv.at[row],
            dst_ref=recv.at[slot, mine],
            send_sem=send_sem.at[row],
            recv_sem=recv_sem.at[slot, mine],
            device_id={"grid": grid_of(owner, side)},
            device_id_type=MESH,
        )

    def arrival(slot, peer):
        return pltpu.make_async_remote_copy(
            src_ref=adv.at[0],
            dst_ref=recv.at[slot, peer],
            send_sem=send_sem.at[0],
            recv_sem=recv_sem.at[slot, peer],
            device_id={"grid": grid_of(peer, side)},
            device_id_type=MESH,
        )

    def finish_group(q):
        value, factor = None, None
        for j in range(STEPS + 1):
            term = power[STEPS - j, pl.ds(q * STEPS - j, STEPS)]
            if j > 0:
                factor = rate[0] if j == 1 else factor * rate[0]
                term = term * (math.comb(STEPS, j) * factor)
            value = term if value is None else value + term
        adv[pl.ds((q - 1) * STEPS, STEPS)] = value
        for j in range(STEPS):
            row = (q - 1) * STEPS + j
            owner, slot = owner_of(lax.rem(row + rows - STEPS, rows))
            pl.when(owner != mine)(lambda row=row, owner=owner, slot=slot: send(row, owner, slot).start())

    loads[0].wait()
    first = 1
    lax.fori_loop(first, first + 2, raise_group, None)
    pl.semaphore_wait(barrier, half + 2)
    halo_copy = pltpu.make_async_remote_copy(
        src_ref=x_ref.at[0, pl.ds(rows - STEPS, STEPS)],
        dst_ref=power.at[0, pl.ds(0, STEPS)],
        send_sem=halo_sem.at[0],
        recv_sem=halo_sem.at[1],
        device_id={"dom": above},
        device_id_type=MESH,
    )
    halo_copy.start()

    def evolve(i):
        q = lax.rem(first + 1 + i, groups)
        pl.when(q == 0)(halo_copy.wait)
        pl.when(i > 0)(lambda: raise_group(q))
        finish_group(jnp.where(q == 0, first, q))

    def fold(values):
        lane = iota((slots_m // 2, 128), 1) < 64
        out = [values[:, :128], values[:, 128:256]]
        for first in (256, 384):
            pair = values[:, first : first + 128].reshape(blocks // 2, 2, 8, 128)
            even = pair[:, 0].reshape(slots_m // 2, 128)
            odd = pltpu.roll(pair[:, 1].reshape(slots_m // 2, 128), 64, 1)
            out += [jnp.where(lane, even, odd), jnp.where(lane, odd, even)]
        return out + [values[:, 512:640]]

    def store_folded(target, values):
        at = 0
        for part in fold(values):
            size = part.shape[0] // 8
            target[at : at + size] = part.reshape(size, 8, 128)
            at += size

    def load_unfolded(source):
        lane = iota((slots_m // 2, 128), 1) < 64
        wide = [source[i * blocks : (i + 1) * blocks].reshape(slots_m, 128) for i in (0, 1, 4)]
        out = wide[:2]
        for at in (2 * blocks, 3 * blocks):
            low = source[at : at + blocks // 2].reshape(slots_m // 2, 128)
            high = source[at + blocks // 2 : at + blocks].reshape(slots_m // 2, 128)
            even = jnp.where(lane, low, high).reshape(blocks // 2, 1, 8, 128)
            odd = pltpu.roll(jnp.where(lane, high, low), 64, 1).reshape(blocks // 2, 1, 8, 128)
            out.append(jnp.concatenate([even, odd], axis=1).reshape(slots_m, 128))
        return jnp.concatenate(out + wide[2:], axis=1)

    seats = [grid_of(seat, side) for seat in range(half)]

    def prepare():
        for load in loads[1:]:
            load.wait()

        if cap < len(tiles):
            count = jnp.int32(0)
            for t, needed in enumerate(shared_by_halves(grids, level_ref)):
                place[t] = jnp.where(needed != 0, jnp.minimum(count, cap), cap)
                after[t] = needed
                count = count + needed
            following = jnp.int32(len(tiles) - 1)
            for t in reversed(range(len(tiles))):
                following = jnp.where(after[t] != 0, t, following)
                after[t] = following
            last = jnp.int32(-1)
            for i in range(cap):
                last = after[jnp.minimum(last + 1, len(tiles) - 1)]
                chosen[i] = last
            taken[cap] = jnp.zeros(taken.shape[1:], F32)

        weights = [[F32(0.0)] * classes_k for _ in range(classes_m)]
        for g in range(grids):
            level_m, level_k = level_ref[0, g], level_ref[2, g]
            weight = jnp.abs(coef_ref[g].astype(F32))
            for b in range(classes_k):
                size = jnp.where(level_k == b + 1, weight, 0.0)
                for a in range(classes_m):
                    weights[a][b] = weights[a][b] + jnp.where(level_m == a + 1, size, 0.0)
        sums = None
        for b in range(classes_k):
            column = None
            for a in range(classes_m):
                term = weights[a][b] * im_ref[:, a : a + 1]
                column = term if column is None else column + term
            term = column * ik_ref[b : b + 1, :]
            sums = term if sums is None else sums + term

        store_folded(inverse, 1.0 / jnp.maximum(sums, 1.0))

        for seat, g in enumerate(seats):
            at = jnp.clip(level_ref[0, g] - 1, 0, classes_m - 1)
            lines = (sm_ref[at] * coef_ref[g].astype(F32)).astype(BF16)
            tents = bm_ref[at].astype(BF16)
            for copy in range(2):
                spread[:, (copy * half + seat) * cells_m : (copy * half + seat + 1) * cells_m] = lines
                gather[seat * cells_m : (seat + 1) * cells_m, copy * slots_m : (copy + 1) * slots_m] = tents

    def cross(slot):
        return pltpu.make_async_remote_copy(
            src_ref=pack.at[slot],
            dst_ref=landed.at[slot],
            send_sem=cross_send.at[slot],
            recv_sem=cross_recv.at[slot],
            device_id={"grid": across},
            device_id_type=MESH,
        )

    def give_back(slot, peer):
        return pltpu.make_async_remote_copy(
            src_ref=res.at[slot, peer],
            dst_ref=out_ref.at[0, row_of(slot)],
            send_sem=back_send.at[slot, peer],
            recv_sem=back_recv.at[row_of(slot)],
            device_id={"grid": grid_of(peer, side)},
            device_id_type=MESH,
        )

    def class_k(seat):
        return jnp.clip(level_ref[2, seats[seat]] - 1, 0, classes_k - 1)

    def collect(slot):
        recv[slot, mine] = adv[row_of(slot)]
        for peer in peers:
            arrival(slot, peer).wait_recv()
        wide = []
        for seat in range(half):
            both = dot(jnp.concatenate(halves(recv[slot, seat]), axis=0), ek_ref[class_k(seat)])
            wide.append(halves(both[:cells_m] + both[cells_m:]))
        wide = jnp.concatenate([high for high, _ in wide] + [rest for _, rest in wide], axis=0)
        store_folded(parts.at[slot], dot(spread[...], wide))
        for i in range(cap):
            pack[slot, i] = parts[slot, chosen[i] if cap < len(tiles) else i]
        cross(slot).start()

    def release(slot):
        cross(slot).wait_recv()
        taken[0:cap] = landed[slot]
        for t in range(len(tiles)):
            total[t] = (parts[slot, t] + taken[place[t] if cap < len(tiles) else t]) * inverse[t]
        both = jnp.concatenate(halves(load_unfolded(total)), axis=0)
        field = dot(gather[...], both)
        for seat in range(half):
            part = jnp.concatenate(halves(field[seat * cells_m : (seat + 1) * cells_m]), axis=0)
            both = dot(part, tk_ref[class_k(seat)])
            res[slot, seat] = both[:cells_m] + both[cells_m:]
        for peer in peers:
            give_back(slot, peer).start()
        out_ref[0, row_of(slot)] = res[slot, mine]

    lead = 1 if half == STEPS else groups - 1
    lag = lead + LAG

    def turn(i, carry):
        pl.when(i < groups - 1)(lambda: evolve(i))
        pl.when(i == 0)(prepare)
        pl.when((i >= lead) & (i < lead + chunk))(lambda: collect(i - lead))
        pl.when((i >= lag) & (i < lag + chunk))(lambda: release(i - lag))
        return carry

    lax.fori_loop(0, max(groups - 1, lag + chunk), turn, 0)

    def finish_row(row, carry):
        owner, slot = owner_of(lax.rem(row + rows - STEPS, rows))

        @pl.when(owner != mine)
        def _():
            send(row, owner, slot).wait_send()
            pltpu.make_async_remote_copy(
                src_ref=res.at[0, 0],
                dst_ref=out_ref.at[0, row],
                send_sem=back_send.at[0, 0],
                recv_sem=back_recv.at[row],
                device_id={"grid": grid_of(owner, side)},
                device_id_type=MESH,
            ).wait_recv()

        return carry

    lax.fori_loop(0, rows, finish_row, 0)

    def finish_slot(slot, carry):
        cross(slot).wait_send()
        for peer in peers:
            give_back(slot, peer).wait_send()
        return carry

    lax.fori_loop(0, chunk, finish_slot, 0)


def staged_call(grids, doms, cap, index, nodal_values, level_vectors, coefficients, velocity):
    rows, cells_m, cells_k = nodal_values.shape[1:]
    half = grids // 2
    chunk = rows // half
    surplus_m, basis_m, inside_m, surplus_k, basis_k, inside_k, tiles = staged_tables()
    slots_m, columns = inside_m.shape[0], inside_k.shape[1]
    vmem = pl.BlockSpec(memory_space=pltpu.VMEM)
    smem = pl.BlockSpec(memory_space=pltpu.SMEM)
    hbm = pl.BlockSpec(memory_space=pltpu.HBM)
    return pl.pallas_call(
        functools.partial(staged_kernel, grids, doms, cap),
        out_shape=pltpu.VMEM(nodal_values.shape, F32),
        in_specs=[hbm, smem, smem, smem] + [hbm] * 6,
        out_specs=vmem,
        scratch_shapes=[
            pltpu.VMEM((STEPS + 1, STEPS + rows, cells_m, cells_k), F32),
            pltpu.VMEM((rows, cells_m, cells_k), F32),
            pltpu.VMEM((chunk, half, cells_m, cells_k), F32),
            pltpu.VMEM((chunk, half, cells_m, cells_k), F32),
            pltpu.VMEM((chunk, len(tiles), 8, 128), F32),
            pltpu.VMEM((chunk, cap, 8, 128), F32),
            pltpu.VMEM((chunk, cap, 8, 128), F32),
            pltpu.VMEM((cap + 1, 8, 128), F32),
            pltpu.VMEM((len(tiles), 8, 128), F32),
            pltpu.VMEM((2, cells_k, cells_k), BF16),
            pltpu.VMEM((2, STEPS * cells_m, STEPS * cells_m), BF16),
            pltpu.VMEM((slots_m, 2 * half * cells_m), BF16),
            pltpu.VMEM((half * cells_m, 2 * slots_m), BF16),
            pltpu.VMEM((len(tiles), 8, 128), F32),
            pltpu.VMEM(surplus_m.shape, F32),
            pltpu.VMEM(basis_m.shape, F32),
            pltpu.VMEM(inside_m.shape, F32),
            pltpu.VMEM(surplus_k.shape, BF16),
            pltpu.VMEM(basis_k.shape, BF16),
            pltpu.VMEM(inside_k.shape, F32),
            pltpu.SMEM((len(tiles),), jnp.int32),
            pltpu.SMEM((len(tiles),), jnp.int32),
            pltpu.SMEM((cap,), jnp.int32),
            pltpu.SemaphoreType.DMA((7,)),
            pltpu.SemaphoreType.DMA((2,)),
            pltpu.SemaphoreType.DMA((rows,)),
            pltpu.SemaphoreType.DMA((chunk, half)),
            pltpu.SemaphoreType.DMA((chunk,)),
            pltpu.SemaphoreType.DMA((chunk,)),
            pltpu.SemaphoreType.DMA((chunk, half)),
            pltpu.SemaphoreType.DMA((rows,)),
        ],
        compiler_params=pltpu.CompilerParams(
            collective_id=index, has_side_effects=True, vmem_limit_bytes=62 * 2**20 + 2**19
        ),
        name="combine_staged",
    )(
        nodal_values,
        level_vectors.T,
        coefficients,
        velocity,
        jnp.asarray(surplus_m),
        jnp.asarray(basis_m),
        jnp.asarray(inside_m),
        jnp.asarray(surplus_k).astype(BF16),
        jnp.asarray(basis_k).astype(BF16),
        jnp.asarray(inside_k),
    )


def solution(mesh):
    grids, doms = mesh.shape["grid"], mesh.shape["dom"]

    def direct(nodal_values, level_vectors, coefficients, velocity):
        rows, cells_m, cells_k = nodal_values.shape[1:]
        chunk = max(1, rows // grids)
        surplus_m, basis_m, inside_m, move_k, basis_k, inside_k = tables()
        slots = inside_m.shape[0]
        classes_k = KSUM - 1
        vmem = pl.BlockSpec(memory_space=pltpu.VMEM)
        smem = pl.BlockSpec(memory_space=pltpu.SMEM)
        hbm = pl.BlockSpec(memory_space=pltpu.HBM)
        return pl.pallas_call(
            functools.partial(direct_kernel, grids, doms),
            out_shape=pltpu.VMEM(nodal_values.shape, F32),
            in_specs=[hbm, smem, smem, smem] + [hbm] * 6,
            out_specs=vmem,
            scratch_shapes=[
                pltpu.VMEM((STEPS + 1, STEPS + rows, cells_m, cells_k), F32),
                pltpu.VMEM((rows, cells_m, cells_k), F32),
                pltpu.VMEM((chunk, grids, cells_m, cells_k), F32),
                pltpu.VMEM((chunk, grids, cells_m, cells_k), F32),
                pltpu.VMEM((2, cells_k, cells_k), BF16),
                pltpu.VMEM((2, STEPS * cells_m, STEPS * cells_m), BF16),
                pltpu.VMEM((classes_k * slots, grids * cells_m), BF16),
                pltpu.VMEM((grids * cells_m, classes_k * slots), BF16),
                pltpu.VMEM((classes_k, cells_k, classes_k * cells_k), BF16),
                pltpu.VMEM((classes_k, cells_k, cells_k), BF16),
                pltpu.VMEM((slots, classes_k * cells_k), F32),
                pltpu.VMEM(surplus_m.shape, F32),
                pltpu.VMEM(basis_m.shape, F32),
                pltpu.VMEM(inside_m.shape, F32),
                pltpu.VMEM(move_k.shape, BF16),
                pltpu.VMEM(basis_k.shape, BF16),
                pltpu.VMEM(inside_k.shape, F32),
                pltpu.SemaphoreType.DMA((7,)),
                pltpu.SemaphoreType.DMA((2,)),
                pltpu.SemaphoreType.DMA((chunk, grids)),
                pltpu.SemaphoreType.DMA((chunk, grids)),
                pltpu.SemaphoreType.DMA((chunk, grids)),
                pltpu.SemaphoreType.DMA((chunk, grids)),
            ],
            compiler_params=pltpu.CompilerParams(
                collective_id=0, has_side_effects=True, vmem_limit_bytes=62 * 2**20 + 2**19
            ),
            name="combine",
        )(
            nodal_values,
            level_vectors.T,
            coefficients,
            velocity,
            jnp.asarray(surplus_m),
            jnp.asarray(basis_m),
            jnp.asarray(inside_m),
            jnp.asarray(move_k).astype(BF16),
            jnp.asarray(basis_k).astype(BF16),
            jnp.asarray(inside_k),
        )

    def shards(nodal_values, level_vectors, coefficients, velocity):
        arrays = nodal_values, level_vectors, coefficients, velocity
        rows = nodal_values.shape[1]
        half = grids // 2
        if grids % 4 or rows % half or rows % STEPS:
            return direct(*arrays)
        count = len(staged_tables()[-1])
        raw = half * 2 ** (MLEV + KSUM + L6) // 1024
        if count < raw:
            return staged_call(grids, doms, count, 1, *arrays)
        caps = [raw * part // 16 for part in PARTS]
        branches = [functools.partial(staged_call, grids, doms, cap, 1 + i) for i, cap in enumerate(caps)]
        return lax.switch(choose(grids, caps, level_vectors.T), branches + [direct], *arrays)

    in_specs = (P("grid", "dom", None, None), P(), P(), P())
    out_specs = P("grid", "dom", None, None)
    return jax.shard_map(shards, mesh=mesh, in_specs=in_specs, out_specs=out_specs, check_vma=False)
```

```python
import functools
import math

import jax
import jax.numpy as jnp
import numpy as np
from jax import lax
from jax.experimental import pallas as pl
from jax.experimental.pallas import tpu as pltpu
from jax.sharding import PartitionSpec as P

MLEV = 6
KSUM = 5
L6 = 3
STEPS = 4
CFL_LIMIT = 0.9
LAG = 2
PARTS = (6, 7, 8, 10)

MESH = pl.DeviceIdType.MESH
F32 = jnp.float32
BF16 = jnp.bfloat16


def level_of(number, finest):
    return 0 if number == 0 else finest - ((number & -number).bit_length() - 1)


def union_points(level_sum):
    finest = level_sum - 1
    return [
        (a, b)
        for a in range(2**finest)
        for b in range(2**finest)
        if level_of(a, finest) + level_of(b, finest) <= level_sum
    ]


def surplus_line(level):
    size = 2**level
    matrix = np.eye(size, dtype=np.float32)
    for target in range(1, size):
        lowest = target & -target
        matrix[(target - lowest) % size, target] -= 0.5
        matrix[(target + lowest) % size, target] -= 0.5
    return matrix


def basis_line(level):
    size = 2**level
    matrix = np.zeros((size, size), np.float32)
    matrix[0] = 1.0
    for source in range(1, size):
        lowest = source & -source
        for target in range(size):
            distance = abs(target - source)
            distance = min(distance, size - distance)
            matrix[source, target] = max(0.0, 1.0 - distance / lowest)
    return matrix


def grid_points(outer, inner, level_sum):
    finest = level_sum - 1
    return {
        (i << (finest - outer), j << (finest - inner)): i * 2**inner + j
        for i in range(2**outer)
        for j in range(2**inner)
    }


@functools.lru_cache(None)
def tables():
    slots = union_points(MLEV)
    cells = 2**MLEV
    classes_m = MLEV - 1
    surplus_m = np.zeros((classes_m, len(slots), cells), np.float32)
    basis_m = np.zeros((classes_m, cells, len(slots)), np.float32)
    inside_m = np.zeros((len(slots), 8), np.float32)
    for a in range(classes_m):
        outer, inner = a + 1, MLEV - a - 1
        lines = np.kron(surplus_line(outer), surplus_line(inner))
        tents = np.kron(basis_line(outer), basis_line(inner))
        points = grid_points(outer, inner, MLEV)
        for s, point in enumerate(slots):
            if point in points:
                surplus_m[a, s] = lines[:, points[point]]
                basis_m[a, :, s] = tents[points[point]]
                inside_m[s, a] = 1.0
    classes_k = KSUM - 1
    cells = 2**KSUM
    move_k = np.zeros((classes_k * cells, classes_k * cells), np.float32)
    basis_k = np.zeros((classes_k * cells, classes_k * cells), np.float32)
    inside_k = np.zeros((8, classes_k * cells * 2**L6), np.float32)
    for b in range(classes_k):
        outer, inner = b + 1, KSUM - b - 1
        lines = np.kron(surplus_line(outer), surplus_line(inner))
        tents = np.kron(basis_line(outer), basis_line(inner))
        block = slice(b * cells, (b + 1) * cells)
        basis_k[block, block] = tents
        points = grid_points(outer, inner, KSUM)
        for other in range(classes_k):
            for point, cell in grid_points(other + 1, KSUM - other - 1, KSUM).items():
                if point in points:
                    column = other * cells + cell
                    move_k[block, column] = lines[:, points[point]]
                    inside_k[b, column * 2**L6 : (column + 1) * 2**L6] = 1.0
    return surplus_m, basis_m, inside_m, move_k, basis_k, inside_k


def halves(x):
    high = x.astype(BF16)
    return high, (x - high.astype(F32)).astype(BF16)


def dot(a, b):
    return jnp.dot(a, b, preferred_element_type=F32)


def iota(shape, dim):
    return lax.broadcasted_iota(jnp.int32, shape, dim)


def direct_kernel(
    grids, doms, x_ref, level_ref, coef_ref, velocity_ref, sm_hbm, bm_hbm, im_hbm, mk_hbm, bk_hbm, ik_hbm,
    out_ref, power, adv, recv, res, mat_k, mat_m, spread, gather, move, basis, inverse,
    sm_ref, bm_ref, im_ref, mk_ref, bk_ref, ik_ref,
    load_sem, halo_sem, send_sem, recv_sem, back_send, back_recv,
):
    rows, cells_m, cells_k = x_ref.shape[1:]
    chunk = max(1, rows // grids)
    workers = rows // chunk
    slots = im_ref.shape[0]
    classes_m = sm_ref.shape[0]
    classes_k = mk_ref.shape[0] // 2**KSUM
    span = STEPS * cells_m
    groups = rows // STEPS + 1
    half = grids // 2
    me = lax.axis_index("grid")
    here = lax.axis_index("dom")
    above = lax.rem(here + 1, doms)
    below = lax.rem(here + doms - 1, doms)

    side, seat = lax.div(me, half), lax.rem(me, half)
    peers = [(1 - side) * half + lax.rem(seat + i, half) for i in range(half)]
    peers += [side * half + lax.rem(seat + i, half) for i in range(1, half)]

    loads = [pltpu.make_async_copy(x_ref.at[0], power.at[0, pl.ds(STEPS, rows)], load_sem.at[0])]
    for i, (source, target) in enumerate([
        (sm_hbm, sm_ref), (bm_hbm, bm_ref), (im_hbm, im_ref), (mk_hbm, mk_ref), (bk_hbm, bk_ref), (ik_hbm, ik_ref),
    ]):
        loads.append(pltpu.make_async_copy(source, target, load_sem.at[i + 1]))
    loads[0].start()

    barrier = pltpu.get_barrier_semaphore()
    for peer in peers:
        pl.semaphore_signal(barrier, inc=1, device_id={"grid": peer}, device_id_type=MESH)
    for other in (above, below):
        pl.semaphore_signal(barrier, inc=1, device_id={"dom": other}, device_id_type=MESH)
    for load in loads[1:]:
        load.start()

    def counts(g):
        return [jnp.float32(rows * doms)] + [
            lax.shift_left(jnp.int32(1), level_ref[i, g]).astype(F32) for i in range(4)
        ] + [jnp.float32(2**L6)]

    fastest = None
    for g in range(grids):
        total = None
        for d, n in enumerate(counts(g)):
            term = n * velocity_ref[d]
            total = term if total is None else total + term
        fastest = total if fastest is None else jnp.maximum(fastest, total)
    step_size = CFL_LIMIT / jnp.full((8, 128), fastest, F32)
    step_size = step_size[0:1, 0:1]
    rate = [n * velocity_ref[d] * step_size for d, n in enumerate(counts(me))]
    stay = 1.0 - rate[0] - rate[1] - rate[2] - rate[3] - rate[4] - rate[5]

    inner_k = lax.shift_left(jnp.int32(1), level_ref[3, me] + L6)
    source, target = iota((cells_k, cells_k), 0), iota((cells_k, cells_k), 1)
    matrix = jnp.where(source == target, stay, 0.0)
    matrix += jnp.where(source == ((target - inner_k) & (cells_k - 1)), rate[3], 0.0)
    low = inner_k - 1
    matrix += jnp.where(source == ((target & ~low) | ((target - 2**L6) & low)), rate[4], 0.0)
    low = 2**L6 - 1
    matrix += jnp.where(source == ((target & ~low) | ((target - 1) & low)), rate[5], 0.0)
    high, rest = halves(matrix)
    mat_k[0] = high
    mat_k[1] = rest
    inner_m = lax.shift_left(jnp.int32(1), level_ref[1, me])
    target, source = iota((span, span), 0), iota((span, span), 1)
    low = jnp.int32(cells_m - 1)
    matrix = jnp.where(source == ((target & ~low) | ((target - inner_m) & low)), rate[1], 0.0)
    low = inner_m - 1
    matrix += jnp.where(source == ((target & ~low) | ((target - 1) & low)), rate[2], 0.0)
    high, rest = halves(matrix)
    mat_m[0] = high
    mat_m[1] = rest

    def raise_group(q):
        now = power[0, pl.ds(q * STEPS, STEPS)].reshape(span, cells_k)
        for step in range(STEPS):
            high, rest = halves(now)
            now = dot(high, mat_k[0]) + dot(rest, mat_k[0]) + dot(high, mat_k[1])
            now += dot(mat_m[0], high) + dot(mat_m[0], rest) + dot(mat_m[1], high)
            power[step + 1, pl.ds(q * STEPS, STEPS)] = now.reshape(STEPS, cells_m, cells_k)

    def send(row, peer):
        return pltpu.make_async_remote_copy(
            src_ref=adv.at[peer * chunk + row],
            dst_ref=recv.at[row, me],
            send_sem=send_sem.at[row, peer],
            recv_sem=recv_sem.at[row, me],
            device_id={"grid": peer},
            device_id_type=MESH,
        )

    def arrival(row, peer):
        return pltpu.make_async_remote_copy(
            src_ref=adv.at[row],
            dst_ref=recv.at[row, peer],
            send_sem=send_sem.at[row, peer],
            recv_sem=recv_sem.at[row, peer],
            device_id={"grid": peer},
            device_id_type=MESH,
        )

    def start_send(row, peer, ready):
        if workers < grids:
            valid = peer < workers
            ready = valid if ready is None else ready & valid
        if ready is None:
            send(row, peer).start()
        else:
            pl.when(ready)(lambda: send(row, peer).start())

    def finish_group(q):
        value, factor = None, None
        for j in range(STEPS + 1):
            term = power[STEPS - j, pl.ds(q * STEPS - j, STEPS)]
            if j > 0:
                factor = rate[0] if j == 1 else factor * rate[0]
                term = term * (math.comb(STEPS, j) * factor)
            value = term if value is None else value + term
        adv[pl.ds((q - 1) * STEPS, STEPS)] = value
        for peer in peers:
            place = peer * chunk
            start_send(0, peer, (place >= (q - 1) * STEPS) & (place < q * STEPS))

    loads[0].wait()
    first = jnp.where(side == 0, groups // 2, 1)
    raise_group(first)
    pl.semaphore_wait(barrier, grids + 1)
    halo_copy = pltpu.make_async_remote_copy(
        src_ref=x_ref.at[0, pl.ds(rows - STEPS, STEPS)],
        dst_ref=power.at[0, pl.ds(0, STEPS)],
        send_sem=halo_sem.at[0],
        recv_sem=halo_sem.at[1],
        device_id={"dom": above},
        device_id_type=MESH,
    )
    halo_copy.start()

    def one(i, carry):
        q = lax.rem(first + i, groups)
        pl.when(q == 0)(halo_copy.wait)
        raise_group(q)
        pl.when(q > 0)(lambda: finish_group(q))
        return carry

    lax.fori_loop(1, groups, one, 0)
    finish_group(first)
    for row in range(1, chunk):
        for peer in peers:
            start_send(row, peer, None)

    def give_back(row, peer):
        return pltpu.make_async_remote_copy(
            src_ref=res.at[row, peer],
            dst_ref=out_ref.at[0, me * chunk + row],
            send_sem=back_send.at[row, peer],
            recv_sem=back_recv.at[row, me],
            device_id={"grid": peer},
            device_id_type=MESH,
        )

    def returned(row, peer):
        return pltpu.make_async_remote_copy(
            src_ref=res.at[row, peer],
            dst_ref=out_ref.at[0, peer * chunk + row],
            send_sem=back_send.at[row, peer],
            recv_sem=back_recv.at[row, peer],
            device_id={"grid": peer},
            device_id_type=MESH,
        )

    for load in loads[1:]:
        load.wait()

    def when_worker(body):
        if workers < grids:
            pl.when(me < workers)(body)
        else:
            body()

    @when_worker
    def _():
        for row in range(chunk):
            recv[row, me] = adv[me * chunk + row]

        weights = [[F32(0.0)] * classes_k for _ in range(classes_m)]
        for g in range(grids):
            level_m, level_k = level_ref[0, g], level_ref[2, g]
            weight = coef_ref[g].astype(F32)
            place = jnp.clip(level_m - 1, 0, classes_m - 1)
            lines = sm_ref[place]
            tents = bm_ref[place]
            for b in range(classes_k):
                match = level_k == b + 1
                spread[b * slots : (b + 1) * slots, g * cells_m : (g + 1) * cells_m] = (
                    lines * jnp.where(match, weight, 0.0)
                ).astype(BF16)
                gather[g * cells_m : (g + 1) * cells_m, b * slots : (b + 1) * slots] = (
                    tents * jnp.where(match, 1.0, 0.0)
                ).astype(BF16)
                size = jnp.where(match, jnp.abs(weight), 0.0)
                for a in range(classes_m):
                    weights[a][b] = weights[a][b] + jnp.where(level_m == a + 1, size, 0.0)
        total = None
        for b in range(classes_k):
            column = None
            for a in range(classes_m):
                term = weights[a][b] * im_ref[:, a : a + 1]
                column = term if column is None else column + term
            term = column * ik_ref[b : b + 1, :]
            total = term if total is None else total + term
        inverse[...] = 1.0 / jnp.maximum(total, 1.0)
        small = classes_k * 2**KSUM
        for b in range(classes_k):
            place = iota((cells_k, small), 0) + b * cells_k
            repeat = (lax.shift_right_logical(place, L6) == iota((cells_k, small), 1)).astype(F32)
            repeat = repeat.astype(BF16)
            left = dot(repeat, mk_ref[...]).astype(BF16)
            left_basis = dot(repeat, bk_ref[...]).astype(BF16)
            for c in range(classes_k):
                place = iota((small, cells_k), 1) + c * cells_k
                widen = (lax.shift_right_logical(place, L6) == iota((small, cells_k), 0)).astype(F32)
                widen = widen.astype(BF16)
                same = (iota((cells_k, cells_k), 0) & (2**L6 - 1)) == (
                    iota((cells_k, cells_k), 1) & (2**L6 - 1)
                )
                move[b, :, c * cells_k : (c + 1) * cells_k] = jnp.where(
                    same, dot(left, widen), 0.0
                ).astype(BF16)
                if b == c:
                    basis[b] = jnp.where(same, dot(left_basis, widen), 0.0).astype(BF16)

        for row in range(chunk):
            for peer in peers:
                arrival(row, peer).wait_recv()
            high, rest = halves(recv[row].reshape(grids * cells_m, cells_k))
            union = None
            for b in range(classes_k):
                part = spread[b * slots : (b + 1) * slots, :]
                high_b, rest_b = halves(dot(part, high) + dot(part, rest))
                term = dot(high_b, move[b]) + dot(rest_b, move[b])
                union = term if union is None else union + term
            union = union * inverse[...]
            field = None
            for b in range(classes_k):
                high_b, rest_b = halves(union[:, b * cells_k : (b + 1) * cells_k])
                high_b, rest_b = halves(dot(high_b, basis[b]) + dot(rest_b, basis[b]))
                part = gather[:, b * slots : (b + 1) * slots]
                term = dot(part, high_b) + dot(part, rest_b)
                field = term if field is None else field + term
            res[row] = field.reshape(grids, cells_m, cells_k)
            for peer in peers:
                give_back(row, peer).start()
            out_ref[0, me * chunk + row] = res[row, me]

    for row in range(chunk):
        for peer in peers:

            def finish_peer(row=row, peer=peer):
                send(row, peer).wait_send()
                returned(row, peer).wait_recv()

            if workers < grids:
                pl.when(peer < workers)(finish_peer)
            else:
                finish_peer()
            when_worker(lambda row=row, peer=peer: give_back(row, peer).wait_send())


ROUNDS_M = ((1, 1), (2, 2), (3, 3), (4, 4), (5, 5), (1, 2), (4, 5), (2, 3), (1, 3), (3, 4), (3, 5), (2, 4), (1, 4), (2, 5), (1, 5))
ROUNDS_K = ((1, 1), (4, 4), (2, 2), (1, 2), (3, 3), (3, 4), (2, 3), (1, 3), (2, 4), (1, 4))


def ordered_points(level_sum, order):
    finest = level_sum - 1
    found = {interval: [] for interval in order}
    for a, b in union_points(level_sum):
        interval = max(level_of(a, finest), 1), min(level_sum - level_of(b, finest), finest)
        found[interval].append((a, b))
    return [(point, interval) for interval in order for point in found[interval]]


def hull(intervals):
    return min(low for low, _ in intervals), max(high for _, high in intervals)


@functools.lru_cache(None)
def staged_tables():
    slots_m = ordered_points(MLEV, ROUNDS_M)
    slots_k = ordered_points(KSUM, ROUNDS_K)
    lanes = 2**L6
    count_m, count_k = len(slots_m), len(slots_k) * lanes
    surplus_m = np.zeros((MLEV - 1, count_m, 2**MLEV), np.float32)
    basis_m = np.zeros((MLEV - 1, 2**MLEV, count_m), np.float32)
    inside_m = np.zeros((count_m, 8), np.float32)
    for a in range(MLEV - 1):
        outer, inner = a + 1, MLEV - a - 1
        lines = np.kron(surplus_line(outer), surplus_line(inner))
        tents = np.kron(basis_line(outer), basis_line(inner))
        points = grid_points(outer, inner, MLEV)
        for s, (point, _) in enumerate(slots_m):
            if point in points:
                surplus_m[a, s] = lines[:, points[point]]
                basis_m[a, :, s] = tents[points[point]]
                inside_m[s, a] = 1.0
    same = np.eye(lanes, dtype=np.float32)
    cells_k = 2 ** (KSUM + L6)
    surplus_k = np.zeros((KSUM - 1, cells_k, count_k), np.float32)
    basis_k = np.zeros((KSUM - 1, count_k, cells_k), np.float32)
    inside_k = np.zeros((8, count_k), np.float32)
    for b in range(KSUM - 1):
        outer, inner = b + 1, KSUM - b - 1
        lines = np.kron(surplus_line(outer), surplus_line(inner))
        tents = np.kron(basis_line(outer), basis_line(inner))
        points = grid_points(outer, inner, KSUM)
        for s, (point, _) in enumerate(slots_k):
            if point in points:
                place = slice(s * lanes, (s + 1) * lanes)
                surplus_k[b, :, place] = np.kron(lines[:, points[point]][:, None], same)
                basis_k[b, place] = np.kron(tents[points[point]][None, :], same)
                inside_k[b, place] = 1.0
    blocks_m = [hull([slots_m[8 * t + i][1] for i in range(8)]) for t in range(count_m // 8)]
    pairs_m = [hull(blocks_m[2 * t : 2 * t + 2]) for t in range(count_m // 16)]
    per = 64 // lanes
    halves_k = [hull([slots_k[per * t + i][1] for i in range(per)]) for t in range(count_k // 64)]
    tiles = []
    for first in (0, 2):
        tiles += [(block, hull(halves_k[first : first + 2])) for block in blocks_m]
    for column in range(4, 8):
        tiles += [(pair, halves_k[column]) for pair in pairs_m]
    tiles += [(block, hull(halves_k[8:10])) for block in blocks_m]
    return surplus_m, basis_m, inside_m, surplus_k, basis_k, inside_k, tiles


def shared_by_halves(grids, level_ref):
    tiles = staged_tables()[-1]
    zero = jnp.int32(0)
    with_m, with_k = [zero] * MLEV, [zero] * KSUM
    for g in range(grids):
        bit = jnp.int32(1 << g)
        for a in range(1, MLEV):
            with_m[a] = with_m[a] | jnp.where(level_ref[0, g] == a, bit, zero)
        for b in range(1, KSUM):
            with_k[b] = with_k[b] | jnp.where(level_ref[2, g] == b, bit, zero)

    def mask_of(table, interval):
        return functools.reduce(jnp.bitwise_or, table[interval[0] : interval[1] + 1])

    masks_m = {m: mask_of(with_m, m) for m in sorted({m for m, _ in tiles})}
    masks_k = {k: mask_of(with_k, k) for k in sorted({k for _, k in tiles})}
    lower = jnp.int32((1 << grids // 2) - 1)
    shared = {}
    for tile in tiles:
        if tile not in shared:
            both = masks_m[tile[0]] & masks_k[tile[1]]
            shared[tile] = (((both & lower) != 0) & ((both & ~lower) != 0)).astype(jnp.int32)
    return [shared[tile] for tile in tiles]


def choice_kernel(grids, caps, level_ref, out_ref):
    count = sum(shared_by_halves(grids, level_ref))
    out_ref[0] = sum((count > cap).astype(jnp.int32) for cap in caps)


def choose(grids, caps, levels):
    smem = pl.BlockSpec(memory_space=pltpu.SMEM)
    return pl.pallas_call(
        functools.partial(choice_kernel, grids, caps),
        out_shape=jax.ShapeDtypeStruct((1,), jnp.int32),
        in_specs=[smem],
        out_specs=smem,
        name="choose",
    )(levels)[0]


def staged_kernel(
    grids, doms, cap, x_ref, level_ref, coef_ref, velocity_ref, sm_hbm, bm_hbm, im_hbm, ek_hbm, tk_hbm, ik_hbm,
    out_ref, power, adv, recv, res, parts, pack, landed, taken, total, mat_k, mat_m, spread, gather, inverse,
    sm_ref, bm_ref, im_ref, ek_ref, tk_ref, ik_ref, after, place, chosen,
    load_sem, halo_sem, send_sem, recv_sem, cross_send, cross_recv, back_send, back_recv,
):
    rows, cells_m, cells_k = x_ref.shape[1:]
    slots_m, columns = im_ref.shape[0], ik_ref.shape[1]
    classes_m, classes_k = sm_ref.shape[0], ek_ref.shape[0]
    tiles = staged_tables()[-1]
    blocks = slots_m // 8
    span = STEPS * cells_m
    groups = rows // STEPS + 1
    half = grids // 2
    quarter = half // 2
    chunk = rows // half
    me = lax.axis_index("grid")
    here = lax.axis_index("dom")
    above = lax.rem(here + 1, doms)
    below = lax.rem(here + doms - 1, doms)
    side = lax.div(me, half)
    mine = lax.rem(me - side * half + side * quarter, half)

    def grid_of(seat, which):
        return which * half + lax.rem(seat + which * quarter, half)

    def owner_of(order):
        return lax.rem(order, half), lax.div(order, half)

    def row_of(slot):
        return lax.rem(slot * half + mine + STEPS, rows)

    peers = [lax.rem(mine + i, half) for i in range(1, half)]
    across = grid_of(mine, 1 - side)

    loads = [pltpu.make_async_copy(x_ref.at[0], power.at[0, pl.ds(STEPS, rows)], load_sem.at[0])]
    for i, (source, target) in enumerate([
        (sm_hbm, sm_ref), (bm_hbm, bm_ref), (im_hbm, im_ref), (ek_hbm, ek_ref), (tk_hbm, tk_ref), (ik_hbm, ik_ref),
    ]):
        loads.append(pltpu.make_async_copy(source, target, load_sem.at[i + 1]))
    loads[0].start()

    barrier = pltpu.get_barrier_semaphore()
    for peer in peers:
        pl.semaphore_signal(barrier, inc=1, device_id={"grid": grid_of(peer, side)}, device_id_type=MESH)
    pl.semaphore_signal(barrier, inc=1, device_id={"grid": across}, device_id_type=MESH)
    for other in (above, below):
        pl.semaphore_signal(barrier, inc=1, device_id={"dom": other}, device_id_type=MESH)
    for load in loads[1:]:
        load.start()

    def counts(g):
        return [jnp.float32(rows * doms)] + [
            lax.shift_left(jnp.int32(1), level_ref[i, g]).astype(F32) for i in range(4)
        ] + [jnp.float32(2**L6)]

    fastest = None
    for g in range(grids):
        size = None
        for d, n in enumerate(counts(g)):
            term = n * velocity_ref[d]
            size = term if size is None else size + term
        fastest = size if fastest is None else jnp.maximum(fastest, size)
    step_size = CFL_LIMIT / jnp.full((8, 128), fastest, F32)
    step_size = step_size[0:1, 0:1]
    rate = [n * velocity_ref[d] * step_size for d, n in enumerate(counts(me))]
    stay = 1.0 - rate[0] - rate[1] - rate[2] - rate[3] - rate[4] - rate[5]

    inner_k = lax.shift_left(jnp.int32(1), level_ref[3, me] + L6)
    source, target = iota((cells_k, cells_k), 0), iota((cells_k, cells_k), 1)
    matrix = jnp.where(source == target, stay, 0.0)
    matrix += jnp.where(source == ((target - inner_k) & (cells_k - 1)), rate[3], 0.0)
    low = inner_k - 1
    matrix += jnp.where(source == ((target & ~low) | ((target - 2**L6) & low)), rate[4], 0.0)
    low = 2**L6 - 1
    matrix += jnp.where(source == ((target & ~low) | ((target - 1) & low)), rate[5], 0.0)
    high, rest = halves(matrix)
    mat_k[0] = high
    mat_k[1] = rest
    inner_m = lax.shift_left(jnp.int32(1), level_ref[1, me])
    target, source = iota((span, span), 0), iota((span, span), 1)
    low = jnp.int32(cells_m - 1)
    matrix = jnp.where(source == ((target & ~low) | ((target - inner_m) & low)), rate[1], 0.0)
    low = inner_m - 1
    matrix += jnp.where(source == ((target & ~low) | ((target - 1) & low)), rate[2], 0.0)
    high, rest = halves(matrix)
    mat_m[0] = high
    mat_m[1] = rest

    def raise_group(q, carry=None):
        now = power[0, pl.ds(q * STEPS, STEPS)].reshape(span, cells_k)
        for step in range(STEPS):
            high, rest = halves(now)
            now = dot(high, mat_k[0]) + dot(rest, mat_k[0]) + dot(high, mat_k[1])
            now += dot(mat_m[0], high) + dot(mat_m[0], rest) + dot(mat_m[1], high)
            power[step + 1, pl.ds(q * STEPS, STEPS)] = now.reshape(STEPS, cells_m, cells_k)
        return carry

    def send(row, owner, slot):
        return pltpu.make_async_remote_copy(
            src_ref=adv.at[row],
            dst_ref=recv.at[slot, mine],
            send_sem=send_sem.at[row],
            recv_sem=recv_sem.at[slot, mine],
            device_id={"grid": grid_of(owner, side)},
            device_id_type=MESH,
        )

    def arrival(slot, peer):
        return pltpu.make_async_remote_copy(
            src_ref=adv.at[0],
            dst_ref=recv.at[slot, peer],
            send_sem=send_sem.at[0],
            recv_sem=recv_sem.at[slot, peer],
            device_id={"grid": grid_of(peer, side)},
            device_id_type=MESH,
        )

    def finish_group(q):
        value, factor = None, None
        for j in range(STEPS + 1):
            term = power[STEPS - j, pl.ds(q * STEPS - j, STEPS)]
            if j > 0:
                factor = rate[0] if j == 1 else factor * rate[0]
                term = term * (math.comb(STEPS, j) * factor)
            value = term if value is None else value + term
        adv[pl.ds((q - 1) * STEPS, STEPS)] = value
        for j in range(STEPS):
            row = (q - 1) * STEPS + j
            owner, slot = owner_of(lax.rem(row + rows - STEPS, rows))
            pl.when(owner != mine)(lambda row=row, owner=owner, slot=slot: send(row, owner, slot).start())

    loads[0].wait()
    first = 1
    lax.fori_loop(first, first + 2, raise_group, None)
    pl.semaphore_wait(barrier, half + 2)
    halo_copy = pltpu.make_async_remote_copy(
        src_ref=x_ref.at[0, pl.ds(rows - STEPS, STEPS)],
        dst_ref=power.at[0, pl.ds(0, STEPS)],
        send_sem=halo_sem.at[0],
        recv_sem=halo_sem.at[1],
        device_id={"dom": above},
        device_id_type=MESH,
    )
    halo_copy.start()

    def evolve(i):
        q = lax.rem(first + 1 + i, groups)
        pl.when(q == 0)(halo_copy.wait)
        pl.when(i > 0)(lambda: raise_group(q))
        finish_group(jnp.where(q == 0, first, q))

    def fold(values):
        lane = iota((slots_m // 2, 128), 1) < 64
        out = [values[:, :128], values[:, 128:256]]
        for first in (256, 384):
            pair = values[:, first : first + 128].reshape(blocks // 2, 2, 8, 128)
            even = pair[:, 0].reshape(slots_m // 2, 128)
            odd = pltpu.roll(pair[:, 1].reshape(slots_m // 2, 128), 64, 1)
            out += [jnp.where(lane, even, odd), jnp.where(lane, odd, even)]
        return out + [values[:, 512:640]]

    def store_folded(target, values):
        at = 0
        for part in fold(values):
            size = part.shape[0] // 8
            target[at : at + size] = part.reshape(size, 8, 128)
            at += size

    def load_unfolded(source):
        lane = iota((slots_m // 2, 128), 1) < 64
        wide = [source[i * blocks : (i + 1) * blocks].reshape(slots_m, 128) for i in (0, 1, 4)]
        out = wide[:2]
        for at in (2 * blocks, 3 * blocks):
            low = source[at : at + blocks // 2].reshape(slots_m // 2, 128)
            high = source[at + blocks // 2 : at + blocks].reshape(slots_m // 2, 128)
            even = jnp.where(lane, low, high).reshape(blocks // 2, 1, 8, 128)
            odd = pltpu.roll(jnp.where(lane, high, low), 64, 1).reshape(blocks // 2, 1, 8, 128)
            out.append(jnp.concatenate([even, odd], axis=1).reshape(slots_m, 128))
        return jnp.concatenate(out + wide[2:], axis=1)

    seats = [grid_of(seat, side) for seat in range(half)]

    def prepare():
        for load in loads[1:]:
            load.wait()

        if cap < len(tiles):
            count = jnp.int32(0)
            for t, needed in enumerate(shared_by_halves(grids, level_ref)):
                place[t] = jnp.where(needed != 0, jnp.minimum(count, cap), cap)
                after[t] = needed
                count = count + needed
            following = jnp.int32(len(tiles) - 1)
            for t in reversed(range(len(tiles))):
                following = jnp.where(after[t] != 0, t, following)
                after[t] = following
            last = jnp.int32(-1)
            for i in range(cap):
                last = after[jnp.minimum(last + 1, len(tiles) - 1)]
                chosen[i] = last
            taken[cap] = jnp.zeros(taken.shape[1:], F32)

        weights = [[F32(0.0)] * classes_k for _ in range(classes_m)]
        for g in range(grids):
            level_m, level_k = level_ref[0, g], level_ref[2, g]
            weight = jnp.abs(coef_ref[g].astype(F32))
            for b in range(classes_k):
                size = jnp.where(level_k == b + 1, weight, 0.0)
                for a in range(classes_m):
                    weights[a][b] = weights[a][b] + jnp.where(level_m == a + 1, size, 0.0)
        sums = None
        for b in range(classes_k):
            column = None
            for a in range(classes_m):
                term = weights[a][b] * im_ref[:, a : a + 1]
                column = term if column is None else column + term
            term = column * ik_ref[b : b + 1, :]
            sums = term if sums is None else sums + term

        store_folded(inverse, 1.0 / jnp.maximum(sums, 1.0))

        for seat, g in enumerate(seats):
            at = jnp.clip(level_ref[0, g] - 1, 0, classes_m - 1)
            lines = (sm_ref[at] * coef_ref[g].astype(F32)).astype(BF16)
            tents = bm_ref[at].astype(BF16)
            for copy in range(2):
                spread[:, (copy * half + seat) * cells_m : (copy * half + seat + 1) * cells_m] = lines
                gather[seat * cells_m : (seat + 1) * cells_m, copy * slots_m : (copy + 1) * slots_m] = tents

    def cross(slot):
        return pltpu.make_async_remote_copy(
            src_ref=pack.at[slot],
            dst_ref=landed.at[slot],
            send_sem=cross_send.at[slot],
            recv_sem=cross_recv.at[slot],
            device_id={"grid": across},
            device_id_type=MESH,
        )

    def give_back(slot, peer):
        return pltpu.make_async_remote_copy(
            src_ref=res.at[slot, peer],
            dst_ref=out_ref.at[0, row_of(slot)],
            send_sem=back_send.at[slot, peer],
            recv_sem=back_recv.at[row_of(slot)],
            device_id={"grid": grid_of(peer, side)},
            device_id_type=MESH,
        )

    def class_k(seat):
        return jnp.clip(level_ref[2, seats[seat]] - 1, 0, classes_k - 1)

    def collect(slot):
        recv[slot, mine] = adv[row_of(slot)]
        for peer in peers:
            arrival(slot, peer).wait_recv()
        wide = []
        for seat in range(half):
            both = dot(jnp.concatenate(halves(recv[slot, seat]), axis=0), ek_ref[class_k(seat)])
            wide.append(halves(both[:cells_m] + both[cells_m:]))
        wide = jnp.concatenate([high for high, _ in wide] + [rest for _, rest in wide], axis=0)
        store_folded(parts.at[slot], dot(spread[...], wide))
        for i in range(cap):
            pack[slot, i] = parts[slot, chosen[i] if cap < len(tiles) else i]
        cross(slot).start()

    def release(slot):
        cross(slot).wait_recv()
        taken[0:cap] = landed[slot]
        for t in range(len(tiles)):
            total[t] = (parts[slot, t] + taken[place[t] if cap < len(tiles) else t]) * inverse[t]
        both = jnp.concatenate(halves(load_unfolded(total)), axis=0)
        field = dot(gather[...], both)
        for seat in range(half):
            part = jnp.concatenate(halves(field[seat * cells_m : (seat + 1) * cells_m]), axis=0)
            both = dot(part, tk_ref[class_k(seat)])
            res[slot, seat] = both[:cells_m] + both[cells_m:]
        for peer in peers:
            give_back(slot, peer).start()
        out_ref[0, row_of(slot)] = res[slot, mine]

    lead = 1 if half == STEPS else groups - 1
    lag = lead + LAG

    def turn(i, carry):
        pl.when(i < groups - 1)(lambda: evolve(i))
        pl.when(i == 0)(prepare)
        pl.when((i >= lead) & (i < lead + chunk))(lambda: collect(i - lead))
        pl.when((i >= lag) & (i < lag + chunk))(lambda: release(i - lag))
        return carry

    lax.fori_loop(0, max(groups - 1, lag + chunk), turn, 0)

    def finish_row(row, carry):
        owner, slot = owner_of(lax.rem(row + rows - STEPS, rows))

        @pl.when(owner != mine)
        def _():
            send(row, owner, slot).wait_send()
            pltpu.make_async_remote_copy(
                src_ref=res.at[0, 0],
                dst_ref=out_ref.at[0, row],
                send_sem=back_send.at[0, 0],
                recv_sem=back_recv.at[row],
                device_id={"grid": grid_of(owner, side)},
                device_id_type=MESH,
            ).wait_recv()

        return carry

    lax.fori_loop(0, rows, finish_row, 0)

    def finish_slot(slot, carry):
        cross(slot).wait_send()
        for peer in peers:
            give_back(slot, peer).wait_send()
        return carry

    lax.fori_loop(0, chunk, finish_slot, 0)


def staged_constants():
    surplus_m, basis_m, inside_m, surplus_k, basis_k, inside_k, _ = staged_tables()
    kinds = (F32, F32, F32, BF16, BF16, F32)
    return [jnp.asarray(a.astype(kind)) for a, kind in zip((surplus_m, basis_m, inside_m, surplus_k, basis_k, inside_k), kinds)]


def staged_call(grids, doms, cap, index, nodal_values, level_vectors, coefficients, velocity, constants):
    rows, cells_m, cells_k = nodal_values.shape[1:]
    half = grids // 2
    chunk = rows // half
    surplus_m, basis_m, inside_m, surplus_k, basis_k, inside_k, tiles = staged_tables()
    slots_m, columns = inside_m.shape[0], inside_k.shape[1]
    vmem = pl.BlockSpec(memory_space=pltpu.VMEM)
    smem = pl.BlockSpec(memory_space=pltpu.SMEM)
    hbm = pl.BlockSpec(memory_space=pltpu.HBM)
    return pl.pallas_call(
        functools.partial(staged_kernel, grids, doms, cap),
        out_shape=pltpu.VMEM(nodal_values.shape, F32),
        in_specs=[hbm, smem, smem, smem] + [hbm] * 6,
        out_specs=vmem,
        scratch_shapes=[
            pltpu.VMEM((STEPS + 1, STEPS + rows, cells_m, cells_k), F32),
            pltpu.VMEM((rows, cells_m, cells_k), F32),
            pltpu.VMEM((chunk, half, cells_m, cells_k), F32),
            pltpu.VMEM((chunk, half, cells_m, cells_k), F32),
            pltpu.VMEM((chunk, len(tiles), 8, 128), F32),
            pltpu.VMEM((chunk, cap, 8, 128), F32),
            pltpu.VMEM((chunk, cap, 8, 128), F32),
            pltpu.VMEM((cap + 1, 8, 128), F32),
            pltpu.VMEM((len(tiles), 8, 128), F32),
            pltpu.VMEM((2, cells_k, cells_k), BF16),
            pltpu.VMEM((2, STEPS * cells_m, STEPS * cells_m), BF16),
            pltpu.VMEM((slots_m, 2 * half * cells_m), BF16),
            pltpu.VMEM((half * cells_m, 2 * slots_m), BF16),
            pltpu.VMEM((len(tiles), 8, 128), F32),
            pltpu.VMEM(surplus_m.shape, F32),
            pltpu.VMEM(basis_m.shape, F32),
            pltpu.VMEM(inside_m.shape, F32),
            pltpu.VMEM(surplus_k.shape, BF16),
            pltpu.VMEM(basis_k.shape, BF16),
            pltpu.VMEM(inside_k.shape, F32),
            pltpu.SMEM((len(tiles),), jnp.int32),
            pltpu.SMEM((len(tiles),), jnp.int32),
            pltpu.SMEM((cap,), jnp.int32),
            pltpu.SemaphoreType.DMA((7,)),
            pltpu.SemaphoreType.DMA((2,)),
            pltpu.SemaphoreType.DMA((rows,)),
            pltpu.SemaphoreType.DMA((chunk, half)),
            pltpu.SemaphoreType.DMA((chunk,)),
            pltpu.SemaphoreType.DMA((chunk,)),
            pltpu.SemaphoreType.DMA((chunk, half)),
            pltpu.SemaphoreType.DMA((rows,)),
        ],
        compiler_params=pltpu.CompilerParams(
            collective_id=index, has_side_effects=True, vmem_limit_bytes=62 * 2**20 + 2**19
        ),
        name="combine_staged",
    )(
        nodal_values,
        level_vectors.T,
        coefficients,
        velocity,
        *constants,
    )


def solution(mesh):
    grids, doms = mesh.shape["grid"], mesh.shape["dom"]

    def direct(nodal_values, level_vectors, coefficients, velocity):
        rows, cells_m, cells_k = nodal_values.shape[1:]
        chunk = max(1, rows // grids)
        surplus_m, basis_m, inside_m, move_k, basis_k, inside_k = tables()
        slots = inside_m.shape[0]
        classes_k = KSUM - 1
        vmem = pl.BlockSpec(memory_space=pltpu.VMEM)
        smem = pl.BlockSpec(memory_space=pltpu.SMEM)
        hbm = pl.BlockSpec(memory_space=pltpu.HBM)
        return pl.pallas_call(
            functools.partial(direct_kernel, grids, doms),
            out_shape=pltpu.VMEM(nodal_values.shape, F32),
            in_specs=[hbm, smem, smem, smem] + [hbm] * 6,
            out_specs=vmem,
            scratch_shapes=[
                pltpu.VMEM((STEPS + 1, STEPS + rows, cells_m, cells_k), F32),
                pltpu.VMEM((rows, cells_m, cells_k), F32),
                pltpu.VMEM((chunk, grids, cells_m, cells_k), F32),
                pltpu.VMEM((chunk, grids, cells_m, cells_k), F32),
                pltpu.VMEM((2, cells_k, cells_k), BF16),
                pltpu.VMEM((2, STEPS * cells_m, STEPS * cells_m), BF16),
                pltpu.VMEM((classes_k * slots, grids * cells_m), BF16),
                pltpu.VMEM((grids * cells_m, classes_k * slots), BF16),
                pltpu.VMEM((classes_k, cells_k, classes_k * cells_k), BF16),
                pltpu.VMEM((classes_k, cells_k, cells_k), BF16),
                pltpu.VMEM((slots, classes_k * cells_k), F32),
                pltpu.VMEM(surplus_m.shape, F32),
                pltpu.VMEM(basis_m.shape, F32),
                pltpu.VMEM(inside_m.shape, F32),
                pltpu.VMEM(move_k.shape, BF16),
                pltpu.VMEM(basis_k.shape, BF16),
                pltpu.VMEM(inside_k.shape, F32),
                pltpu.SemaphoreType.DMA((7,)),
                pltpu.SemaphoreType.DMA((2,)),
                pltpu.SemaphoreType.DMA((chunk, grids)),
                pltpu.SemaphoreType.DMA((chunk, grids)),
                pltpu.SemaphoreType.DMA((chunk, grids)),
                pltpu.SemaphoreType.DMA((chunk, grids)),
            ],
            compiler_params=pltpu.CompilerParams(
                collective_id=0, has_side_effects=True, vmem_limit_bytes=62 * 2**20 + 2**19
            ),
            name="combine",
        )(
            nodal_values,
            level_vectors.T,
            coefficients,
            velocity,
            jnp.asarray(surplus_m),
            jnp.asarray(basis_m),
            jnp.asarray(inside_m),
            jnp.asarray(move_k).astype(BF16),
            jnp.asarray(basis_k).astype(BF16),
            jnp.asarray(inside_k),
        )

    def shards(nodal_values, level_vectors, coefficients, velocity):
        arrays = nodal_values, level_vectors, coefficients, velocity
        rows = nodal_values.shape[1]
        half = grids // 2
        if grids % 4 or rows % half or rows % STEPS:
            return direct(*arrays)
        count = len(staged_tables()[-1])
        raw = half * 2 ** (MLEV + KSUM + L6) // 1024
        if count < raw:
            return staged_call(grids, doms, count, 1, *arrays, staged_constants())
        caps = [raw * part // 16 for part in PARTS]
        branches = [functools.partial(staged_call, grids, doms, cap, 1 + i) for i, cap in enumerate(caps)]
        branches.append(lambda *given: direct(*given[:-1]))
        return lax.switch(choose(grids, caps, level_vectors.T), branches, *arrays, lax.optimization_barrier(staged_constants()))

    in_specs = (P("grid", "dom", None, None), P(), P(), P())
    out_specs = P("grid", "dom", None, None)
    return jax.shard_map(shards, mesh=mesh, in_specs=in_specs, out_specs=out_specs, check_vma=False)
```

```python
import functools
import math

import jax
import jax.numpy as jnp
import numpy as np
from jax import lax
from jax.experimental import pallas as pl
from jax.experimental.pallas import tpu as pltpu
from jax.sharding import PartitionSpec as P

MLEV = 6
KSUM = 5
L6 = 3
STEPS = 4
CFL_LIMIT = 0.9
LAG = 2
PARTS = (6, 7, 8, 10)

MESH = pl.DeviceIdType.MESH
F32 = jnp.float32
BF16 = jnp.bfloat16


def level_of(number, finest):
    return 0 if number == 0 else finest - ((number & -number).bit_length() - 1)


def union_points(level_sum):
    finest = level_sum - 1
    return [
        (a, b)
        for a in range(2**finest)
        for b in range(2**finest)
        if level_of(a, finest) + level_of(b, finest) <= level_sum
    ]


def surplus_line(level):
    size = 2**level
    matrix = np.eye(size, dtype=np.float32)
    for target in range(1, size):
        lowest = target & -target
        matrix[(target - lowest) % size, target] -= 0.5
        matrix[(target + lowest) % size, target] -= 0.5
    return matrix


def basis_line(level):
    size = 2**level
    matrix = np.zeros((size, size), np.float32)
    matrix[0] = 1.0
    for source in range(1, size):
        lowest = source & -source
        for target in range(size):
            distance = abs(target - source)
            distance = min(distance, size - distance)
            matrix[source, target] = max(0.0, 1.0 - distance / lowest)
    return matrix


def grid_points(outer, inner, level_sum):
    finest = level_sum - 1
    return {
        (i << (finest - outer), j << (finest - inner)): i * 2**inner + j
        for i in range(2**outer)
        for j in range(2**inner)
    }


@functools.lru_cache(None)
def tables():
    slots = union_points(MLEV)
    cells = 2**MLEV
    classes_m = MLEV - 1
    surplus_m = np.zeros((classes_m, len(slots), cells), np.float32)
    basis_m = np.zeros((classes_m, cells, len(slots)), np.float32)
    inside_m = np.zeros((len(slots), 8), np.float32)
    for a in range(classes_m):
        outer, inner = a + 1, MLEV - a - 1
        lines = np.kron(surplus_line(outer), surplus_line(inner))
        tents = np.kron(basis_line(outer), basis_line(inner))
        points = grid_points(outer, inner, MLEV)
        for s, point in enumerate(slots):
            if point in points:
                surplus_m[a, s] = lines[:, points[point]]
                basis_m[a, :, s] = tents[points[point]]
                inside_m[s, a] = 1.0
    classes_k = KSUM - 1
    cells = 2**KSUM
    move_k = np.zeros((classes_k * cells, classes_k * cells), np.float32)
    basis_k = np.zeros((classes_k * cells, classes_k * cells), np.float32)
    inside_k = np.zeros((8, classes_k * cells * 2**L6), np.float32)
    for b in range(classes_k):
        outer, inner = b + 1, KSUM - b - 1
        lines = np.kron(surplus_line(outer), surplus_line(inner))
        tents = np.kron(basis_line(outer), basis_line(inner))
        block = slice(b * cells, (b + 1) * cells)
        basis_k[block, block] = tents
        points = grid_points(outer, inner, KSUM)
        for other in range(classes_k):
            for point, cell in grid_points(other + 1, KSUM - other - 1, KSUM).items():
                if point in points:
                    column = other * cells + cell
                    move_k[block, column] = lines[:, points[point]]
                    inside_k[b, column * 2**L6 : (column + 1) * 2**L6] = 1.0
    return surplus_m, basis_m, inside_m, move_k, basis_k, inside_k


def halves(x):
    high = x.astype(BF16)
    return high, (x - high.astype(F32)).astype(BF16)


def dot(a, b):
    return jnp.dot(a, b, preferred_element_type=F32)


def iota(shape, dim):
    return lax.broadcasted_iota(jnp.int32, shape, dim)


def direct_kernel(
    grids, doms, x_ref, level_ref, coef_ref, velocity_ref, sm_hbm, bm_hbm, im_hbm, mk_hbm, bk_hbm, ik_hbm,
    out_ref, power, adv, recv, res, mat_k, mat_m, spread, gather, move, basis, inverse,
    sm_ref, bm_ref, im_ref, mk_ref, bk_ref, ik_ref,
    load_sem, halo_sem, send_sem, recv_sem, back_send, back_recv,
):
    rows, cells_m, cells_k = x_ref.shape[1:]
    chunk = max(1, rows // grids)
    workers = rows // chunk
    slots = im_ref.shape[0]
    classes_m = sm_ref.shape[0]
    classes_k = mk_ref.shape[0] // 2**KSUM
    span = STEPS * cells_m
    groups = rows // STEPS + 1
    half = grids // 2
    me = lax.axis_index("grid")
    here = lax.axis_index("dom")
    above = lax.rem(here + 1, doms)
    below = lax.rem(here + doms - 1, doms)

    side, seat = lax.div(me, half), lax.rem(me, half)
    peers = [(1 - side) * half + lax.rem(seat + i, half) for i in range(half)]
    peers += [side * half + lax.rem(seat + i, half) for i in range(1, half)]

    loads = [pltpu.make_async_copy(x_ref.at[0], power.at[0, pl.ds(STEPS, rows)], load_sem.at[0])]
    for i, (source, target) in enumerate([
        (sm_hbm, sm_ref), (bm_hbm, bm_ref), (im_hbm, im_ref), (mk_hbm, mk_ref), (bk_hbm, bk_ref), (ik_hbm, ik_ref),
    ]):
        loads.append(pltpu.make_async_copy(source, target, load_sem.at[i + 1]))
    loads[0].start()

    barrier = pltpu.get_barrier_semaphore()
    for peer in peers:
        pl.semaphore_signal(barrier, inc=1, device_id={"grid": peer}, device_id_type=MESH)
    for other in (above, below):
        pl.semaphore_signal(barrier, inc=1, device_id={"dom": other}, device_id_type=MESH)
    for load in loads[1:]:
        load.start()

    def counts(g):
        return [jnp.float32(rows * doms)] + [
            lax.shift_left(jnp.int32(1), level_ref[i, g]).astype(F32) for i in range(4)
        ] + [jnp.float32(2**L6)]

    fastest = None
    for g in range(grids):
        total = None
        for d, n in enumerate(counts(g)):
            term = n * velocity_ref[d]
            total = term if total is None else total + term
        fastest = total if fastest is None else jnp.maximum(fastest, total)
    step_size = CFL_LIMIT / jnp.full((8, 128), fastest, F32)
    step_size = step_size[0:1, 0:1]
    rate = [n * velocity_ref[d] * step_size for d, n in enumerate(counts(me))]
    stay = 1.0 - rate[0] - rate[1] - rate[2] - rate[3] - rate[4] - rate[5]

    inner_k = lax.shift_left(jnp.int32(1), level_ref[3, me] + L6)
    source, target = iota((cells_k, cells_k), 0), iota((cells_k, cells_k), 1)
    matrix = jnp.where(source == target, stay, 0.0)
    matrix += jnp.where(source == ((target - inner_k) & (cells_k - 1)), rate[3], 0.0)
    low = inner_k - 1
    matrix += jnp.where(source == ((target & ~low) | ((target - 2**L6) & low)), rate[4], 0.0)
    low = 2**L6 - 1
    matrix += jnp.where(source == ((target & ~low) | ((target - 1) & low)), rate[5], 0.0)
    high, rest = halves(matrix)
    mat_k[0] = high
    mat_k[1] = rest
    inner_m = lax.shift_left(jnp.int32(1), level_ref[1, me])
    target, source = iota((span, span), 0), iota((span, span), 1)
    low = jnp.int32(cells_m - 1)
    matrix = jnp.where(source == ((target & ~low) | ((target - inner_m) & low)), rate[1], 0.0)
    low = inner_m - 1
    matrix += jnp.where(source == ((target & ~low) | ((target - 1) & low)), rate[2], 0.0)
    high, rest = halves(matrix)
    mat_m[0] = high
    mat_m[1] = rest

    def raise_group(q):
        now = power[0, pl.ds(q * STEPS, STEPS)].reshape(span, cells_k)
        for step in range(STEPS):
            high, rest = halves(now)
            now = dot(high, mat_k[0]) + dot(rest, mat_k[0]) + dot(high, mat_k[1])
            now += dot(mat_m[0], high) + dot(mat_m[0], rest) + dot(mat_m[1], high)
            power[step + 1, pl.ds(q * STEPS, STEPS)] = now.reshape(STEPS, cells_m, cells_k)

    def send(row, peer):
        return pltpu.make_async_remote_copy(
            src_ref=adv.at[peer * chunk + row],
            dst_ref=recv.at[row, me],
            send_sem=send_sem.at[row, peer],
            recv_sem=recv_sem.at[row, me],
            device_id={"grid": peer},
            device_id_type=MESH,
        )

    def arrival(row, peer):
        return pltpu.make_async_remote_copy(
            src_ref=adv.at[row],
            dst_ref=recv.at[row, peer],
            send_sem=send_sem.at[row, peer],
            recv_sem=recv_sem.at[row, peer],
            device_id={"grid": peer},
            device_id_type=MESH,
        )

    def start_send(row, peer, ready):
        if workers < grids:
            valid = peer < workers
            ready = valid if ready is None else ready & valid
        if ready is None:
            send(row, peer).start()
        else:
            pl.when(ready)(lambda: send(row, peer).start())

    def finish_group(q):
        value, factor = None, None
        for j in range(STEPS + 1):
            term = power[STEPS - j, pl.ds(q * STEPS - j, STEPS)]
            if j > 0:
                factor = rate[0] if j == 1 else factor * rate[0]
                term = term * (math.comb(STEPS, j) * factor)
            value = term if value is None else value + term
        adv[pl.ds((q - 1) * STEPS, STEPS)] = value
        for peer in peers:
            place = peer * chunk
            start_send(0, peer, (place >= (q - 1) * STEPS) & (place < q * STEPS))

    loads[0].wait()
    first = jnp.where(side == 0, groups // 2, 1)
    raise_group(first)
    pl.semaphore_wait(barrier, grids + 1)
    halo_copy = pltpu.make_async_remote_copy(
        src_ref=x_ref.at[0, pl.ds(rows - STEPS, STEPS)],
        dst_ref=power.at[0, pl.ds(0, STEPS)],
        send_sem=halo_sem.at[0],
        recv_sem=halo_sem.at[1],
        device_id={"dom": above},
        device_id_type=MESH,
    )
    halo_copy.start()

    def one(i, carry):
        q = lax.rem(first + i, groups)
        pl.when(q == 0)(halo_copy.wait)
        raise_group(q)
        pl.when(q > 0)(lambda: finish_group(q))
        return carry

    lax.fori_loop(1, groups, one, 0)
    finish_group(first)
    for row in range(1, chunk):
        for peer in peers:
            start_send(row, peer, None)

    def give_back(row, peer):
        return pltpu.make_async_remote_copy(
            src_ref=res.at[row, peer],
            dst_ref=out_ref.at[0, me * chunk + row],
            send_sem=back_send.at[row, peer],
            recv_sem=back_recv.at[row, me],
            device_id={"grid": peer},
            device_id_type=MESH,
        )

    def returned(row, peer):
        return pltpu.make_async_remote_copy(
            src_ref=res.at[row, peer],
            dst_ref=out_ref.at[0, peer * chunk + row],
            send_sem=back_send.at[row, peer],
            recv_sem=back_recv.at[row, peer],
            device_id={"grid": peer},
            device_id_type=MESH,
        )

    for load in loads[1:]:
        load.wait()

    def when_worker(body):
        if workers < grids:
            pl.when(me < workers)(body)
        else:
            body()

    @when_worker
    def _():
        for row in range(chunk):
            recv[row, me] = adv[me * chunk + row]

        weights = [[F32(0.0)] * classes_k for _ in range(classes_m)]
        for g in range(grids):
            level_m, level_k = level_ref[0, g], level_ref[2, g]
            weight = coef_ref[g].astype(F32)
            place = jnp.clip(level_m - 1, 0, classes_m - 1)
            lines = sm_ref[place]
            tents = bm_ref[place]
            for b in range(classes_k):
                match = level_k == b + 1
                spread[b * slots : (b + 1) * slots, g * cells_m : (g + 1) * cells_m] = (
                    lines * jnp.where(match, weight, 0.0)
                ).astype(BF16)
                gather[g * cells_m : (g + 1) * cells_m, b * slots : (b + 1) * slots] = (
                    tents * jnp.where(match, 1.0, 0.0)
                ).astype(BF16)
                size = jnp.where(match, jnp.abs(weight), 0.0)
                for a in range(classes_m):
                    weights[a][b] = weights[a][b] + jnp.where(level_m == a + 1, size, 0.0)
        total = None
        for b in range(classes_k):
            column = None
            for a in range(classes_m):
                term = weights[a][b] * im_ref[:, a : a + 1]
                column = term if column is None else column + term
            term = column * ik_ref[b : b + 1, :]
            total = term if total is None else total + term
        inverse[...] = 1.0 / jnp.maximum(total, 1.0)
        small = classes_k * 2**KSUM
        for b in range(classes_k):
            place = iota((cells_k, small), 0) + b * cells_k
            repeat = (lax.shift_right_logical(place, L6) == iota((cells_k, small), 1)).astype(F32)
            repeat = repeat.astype(BF16)
            left = dot(repeat, mk_ref[...]).astype(BF16)
            left_basis = dot(repeat, bk_ref[...]).astype(BF16)
            for c in range(classes_k):
                place = iota((small, cells_k), 1) + c * cells_k
                widen = (lax.shift_right_logical(place, L6) == iota((small, cells_k), 0)).astype(F32)
                widen = widen.astype(BF16)
                same = (iota((cells_k, cells_k), 0) & (2**L6 - 1)) == (
                    iota((cells_k, cells_k), 1) & (2**L6 - 1)
                )
                move[b, :, c * cells_k : (c + 1) * cells_k] = jnp.where(
                    same, dot(left, widen), 0.0
                ).astype(BF16)
                if b == c:
                    basis[b] = jnp.where(same, dot(left_basis, widen), 0.0).astype(BF16)

        for row in range(chunk):
            for peer in peers:
                arrival(row, peer).wait_recv()
            high, rest = halves(recv[row].reshape(grids * cells_m, cells_k))
            union = None
            for b in range(classes_k):
                part = spread[b * slots : (b + 1) * slots, :]
                high_b, rest_b = halves(dot(part, high) + dot(part, rest))
                term = dot(high_b, move[b]) + dot(rest_b, move[b])
                union = term if union is None else union + term
            union = union * inverse[...]
            field = None
            for b in range(classes_k):
                high_b, rest_b = halves(union[:, b * cells_k : (b + 1) * cells_k])
                high_b, rest_b = halves(dot(high_b, basis[b]) + dot(rest_b, basis[b]))
                part = gather[:, b * slots : (b + 1) * slots]
                term = dot(part, high_b) + dot(part, rest_b)
                field = term if field is None else field + term
            res[row] = field.reshape(grids, cells_m, cells_k)
            for peer in peers:
                give_back(row, peer).start()
            out_ref[0, me * chunk + row] = res[row, me]

    for row in range(chunk):
        for peer in peers:

            def finish_peer(row=row, peer=peer):
                send(row, peer).wait_send()
                returned(row, peer).wait_recv()

            if workers < grids:
                pl.when(peer < workers)(finish_peer)
            else:
                finish_peer()
            when_worker(lambda row=row, peer=peer: give_back(row, peer).wait_send())


ROUNDS_M = ((1, 1), (2, 2), (3, 3), (4, 4), (5, 5), (1, 2), (4, 5), (2, 3), (1, 3), (3, 4), (3, 5), (2, 4), (1, 4), (2, 5), (1, 5))
ROUNDS_K = ((1, 1), (4, 4), (2, 2), (1, 2), (3, 3), (3, 4), (2, 3), (1, 3), (2, 4), (1, 4))


def ordered_points(level_sum, order):
    finest = level_sum - 1
    found = {interval: [] for interval in order}
    for a, b in union_points(level_sum):
        interval = max(level_of(a, finest), 1), min(level_sum - level_of(b, finest), finest)
        found[interval].append((a, b))
    return [(point, interval) for interval in order for point in found[interval]]


def hull(intervals):
    return min(low for low, _ in intervals), max(high for _, high in intervals)


@functools.lru_cache(None)
def staged_tables():
    slots_m = ordered_points(MLEV, ROUNDS_M)
    slots_k = ordered_points(KSUM, ROUNDS_K)
    lanes = 2**L6
    count_m, count_k = len(slots_m), len(slots_k) * lanes
    surplus_m = np.zeros((MLEV - 1, count_m, 2**MLEV), np.float32)
    basis_m = np.zeros((MLEV - 1, 2**MLEV, count_m), np.float32)
    inside_m = np.zeros((count_m, 8), np.float32)
    for a in range(MLEV - 1):
        outer, inner = a + 1, MLEV - a - 1
        lines = np.kron(surplus_line(outer), surplus_line(inner))
        tents = np.kron(basis_line(outer), basis_line(inner))
        points = grid_points(outer, inner, MLEV)
        for s, (point, _) in enumerate(slots_m):
            if point in points:
                surplus_m[a, s] = lines[:, points[point]]
                basis_m[a, :, s] = tents[points[point]]
                inside_m[s, a] = 1.0
    same = np.eye(lanes, dtype=np.float32)
    cells_k = 2 ** (KSUM + L6)
    surplus_k = np.zeros((KSUM - 1, cells_k, count_k), np.float32)
    basis_k = np.zeros((KSUM - 1, count_k, cells_k), np.float32)
    inside_k = np.zeros((8, count_k), np.float32)
    for b in range(KSUM - 1):
        outer, inner = b + 1, KSUM - b - 1
        lines = np.kron(surplus_line(outer), surplus_line(inner))
        tents = np.kron(basis_line(outer), basis_line(inner))
        points = grid_points(outer, inner, KSUM)
        for s, (point, _) in enumerate(slots_k):
            if point in points:
                place = slice(s * lanes, (s + 1) * lanes)
                surplus_k[b, :, place] = np.kron(lines[:, points[point]][:, None], same)
                basis_k[b, place] = np.kron(tents[points[point]][None, :], same)
                inside_k[b, place] = 1.0
    blocks_m = [hull([slots_m[8 * t + i][1] for i in range(8)]) for t in range(count_m // 8)]
    pairs_m = [hull(blocks_m[2 * t : 2 * t + 2]) for t in range(count_m // 16)]
    per = 64 // lanes
    halves_k = [hull([slots_k[per * t + i][1] for i in range(per)]) for t in range(count_k // 64)]
    tiles = []
    for first in (0, 2):
        tiles += [(block, hull(halves_k[first : first + 2])) for block in blocks_m]
    for column in range(4, 10):
        tiles += [(pair, halves_k[column]) for pair in pairs_m]
    return surplus_m, basis_m, inside_m, surplus_k, basis_k, inside_k, tiles


def shared_by_halves(grids, level_ref):
    one = jnp.int32(1)
    present = [
        functools.reduce(
            jnp.bitwise_or,
            [lax.shift_left(one, level_ref[0, g] * KSUM + level_ref[2, g]) for g in range(first, first + grids // 2)],
        )
        for first in (0, grids // 2)
    ]
    shared = {}
    for m, k in staged_tables()[-1]:
        if (m, k) not in shared:
            inside = sum(1 << (a * KSUM + b) for a in range(m[0], m[1] + 1) for b in range(k[0], k[1] + 1))
            lower, upper = ((side & jnp.int32(inside)) != 0 for side in present)
            shared[m, k] = (lower & upper).astype(jnp.int32)
    return shared


def choice_kernel(grids, caps, level_ref, out_ref):
    tiles = staged_tables()[-1]
    count = sum(needed * tiles.count(tile) for tile, needed in shared_by_halves(grids, level_ref).items())
    out_ref[0] = sum((count > cap).astype(jnp.int32) for cap in caps)


def choose(grids, caps, levels):
    smem = pl.BlockSpec(memory_space=pltpu.SMEM)
    return pl.pallas_call(
        functools.partial(choice_kernel, grids, caps),
        out_shape=jax.ShapeDtypeStruct((1,), jnp.int32),
        in_specs=[smem],
        out_specs=smem,
        name="choose",
    )(levels)[0]


def staged_kernel(
    grids, doms, cap, x_ref, level_ref, coef_ref, velocity_ref, sm_hbm, bm_hbm, im_hbm, ek_hbm, tk_hbm, ik_hbm,
    out_ref, power, adv, recv, res, parts, pack, landed, taken, total, mat_k, mat_m, spread, gather, inverse,
    sm_ref, bm_ref, im_ref, ek_ref, tk_ref, ik_ref, after, place, chosen,
    load_sem, halo_sem, send_sem, recv_sem, cross_send, cross_recv, back_send, back_recv,
):
    rows, cells_m, cells_k = x_ref.shape[1:]
    slots_m, columns = im_ref.shape[0], ik_ref.shape[1]
    classes_m, classes_k = sm_ref.shape[0], ek_ref.shape[0]
    tiles = staged_tables()[-1]
    blocks = slots_m // 8
    span = STEPS * cells_m
    groups = rows // STEPS + 1
    half = grids // 2
    quarter = half // 2
    chunk = rows // half
    me = lax.axis_index("grid")
    here = lax.axis_index("dom")
    above = lax.rem(here + 1, doms)
    below = lax.rem(here + doms - 1, doms)
    side = lax.div(me, half)
    mine = lax.rem(me - side * half + side * quarter, half)

    def grid_of(seat, which):
        return which * half + lax.rem(seat + which * quarter, half)

    def owner_of(order):
        return lax.rem(order, half), lax.div(order, half)

    def row_of(slot):
        return lax.rem(slot * half + mine + STEPS, rows)

    peers = [lax.rem(mine + i, half) for i in range(1, half)]
    across = grid_of(mine, 1 - side)

    loads = [pltpu.make_async_copy(x_ref.at[0], power.at[0, pl.ds(STEPS, rows)], load_sem.at[0])]
    for i, (source, target) in enumerate([
        (sm_hbm, sm_ref), (bm_hbm, bm_ref), (im_hbm, im_ref), (ek_hbm, ek_ref), (tk_hbm, tk_ref), (ik_hbm, ik_ref),
    ]):
        loads.append(pltpu.make_async_copy(source, target, load_sem.at[i + 1]))
    loads[0].start()

    barrier = pltpu.get_barrier_semaphore()
    for peer in peers:
        pl.semaphore_signal(barrier, inc=1, device_id={"grid": grid_of(peer, side)}, device_id_type=MESH)
    pl.semaphore_signal(barrier, inc=1, device_id={"grid": across}, device_id_type=MESH)
    for other in (above, below):
        pl.semaphore_signal(barrier, inc=1, device_id={"dom": other}, device_id_type=MESH)
    for load in loads[1:]:
        load.start()

    def counts(g):
        return [jnp.float32(rows * doms)] + [
            lax.shift_left(jnp.int32(1), level_ref[i, g]).astype(F32) for i in range(4)
        ] + [jnp.float32(2**L6)]

    fastest = None
    for g in range(grids):
        size = None
        for d, n in enumerate(counts(g)):
            term = n * velocity_ref[d]
            size = term if size is None else size + term
        fastest = size if fastest is None else jnp.maximum(fastest, size)
    step_size = CFL_LIMIT / jnp.full((8, 128), fastest, F32)
    step_size = step_size[0:1, 0:1]
    rate = [n * velocity_ref[d] * step_size for d, n in enumerate(counts(me))]
    stay = 1.0 - rate[0] - rate[1] - rate[2] - rate[3] - rate[4] - rate[5]

    inner_k = lax.shift_left(jnp.int32(1), level_ref[3, me] + L6)
    source, target = iota((cells_k, cells_k), 0), iota((cells_k, cells_k), 1)
    matrix = jnp.where(source == target, stay, 0.0)
    matrix += jnp.where(source == ((target - inner_k) & (cells_k - 1)), rate[3], 0.0)
    low = inner_k - 1
    matrix += jnp.where(source == ((target & ~low) | ((target - 2**L6) & low)), rate[4], 0.0)
    low = 2**L6 - 1
    matrix += jnp.where(source == ((target & ~low) | ((target - 1) & low)), rate[5], 0.0)
    high, rest = halves(matrix)
    mat_k[0] = high
    mat_k[1] = rest
    inner_m = lax.shift_left(jnp.int32(1), level_ref[1, me])
    target, source = iota((span, span), 0), iota((span, span), 1)
    low = jnp.int32(cells_m - 1)
    matrix = jnp.where(source == ((target & ~low) | ((target - inner_m) & low)), rate[1], 0.0)
    low = inner_m - 1
    matrix += jnp.where(source == ((target & ~low) | ((target - 1) & low)), rate[2], 0.0)
    high, rest = halves(matrix)
    mat_m[0] = high
    mat_m[1] = rest

    def raise_group(q, carry=None):
        now = power[0, pl.ds(q * STEPS, STEPS)].reshape(span, cells_k)
        for step in range(STEPS):
            high, rest = halves(now)
            now = dot(high, mat_k[0]) + dot(rest, mat_k[0]) + dot(high, mat_k[1])
            now += dot(mat_m[0], high) + dot(mat_m[0], rest) + dot(mat_m[1], high)
            power[step + 1, pl.ds(q * STEPS, STEPS)] = now.reshape(STEPS, cells_m, cells_k)
        return carry

    def send(row, owner, slot):
        return pltpu.make_async_remote_copy(
            src_ref=adv.at[row],
            dst_ref=recv.at[slot, mine],
            send_sem=send_sem.at[row],
            recv_sem=recv_sem.at[slot, mine],
            device_id={"grid": grid_of(owner, side)},
            device_id_type=MESH,
        )

    def arrival(slot, peer):
        return pltpu.make_async_remote_copy(
            src_ref=adv.at[0],
            dst_ref=recv.at[slot, peer],
            send_sem=send_sem.at[0],
            recv_sem=recv_sem.at[slot, peer],
            device_id={"grid": grid_of(peer, side)},
            device_id_type=MESH,
        )

    def finish_group(q):
        value, factor = None, None
        for j in range(STEPS + 1):
            term = power[STEPS - j, pl.ds(q * STEPS - j, STEPS)]
            if j > 0:
                factor = rate[0] if j == 1 else factor * rate[0]
                term = term * (math.comb(STEPS, j) * factor)
            value = term if value is None else value + term
        adv[pl.ds((q - 1) * STEPS, STEPS)] = value
        for j in range(STEPS):
            row = (q - 1) * STEPS + j
            owner, slot = owner_of(lax.rem(row + rows - STEPS, rows))
            pl.when(owner != mine)(lambda row=row, owner=owner, slot=slot: send(row, owner, slot).start())

    loads[0].wait()
    first = 1
    lax.fori_loop(first, first + 2, raise_group, None)
    pl.semaphore_wait(barrier, half + 2)
    halo_copy = pltpu.make_async_remote_copy(
        src_ref=x_ref.at[0, pl.ds(rows - STEPS, STEPS)],
        dst_ref=power.at[0, pl.ds(0, STEPS)],
        send_sem=halo_sem.at[0],
        recv_sem=halo_sem.at[1],
        device_id={"dom": above},
        device_id_type=MESH,
    )
    halo_copy.start()

    def evolve(i):
        q = lax.rem(first + 1 + i, groups)
        pl.when(q == 0)(halo_copy.wait)
        pl.when(i > 0)(lambda: raise_group(q))
        finish_group(jnp.where(q == 0, first, q))

    def fold(values):
        lane = iota((slots_m // 2, 128), 1) < 64
        out = [values[:, :128], values[:, 128:256]]
        for first in (256, 384, 512):
            pair = values[:, first : first + 128].reshape(blocks // 2, 2, 8, 128)
            even = pair[:, 0].reshape(slots_m // 2, 128)
            odd = pltpu.roll(pair[:, 1].reshape(slots_m // 2, 128), 64, 1)
            out += [jnp.where(lane, even, odd), jnp.where(lane, odd, even)]
        return out

    def store_folded(target, values):
        at = 0
        for part in fold(values):
            size = part.shape[0] // 8
            target[at : at + size] = part.reshape(size, 8, 128)
            at += size

    def load_unfolded(source):
        lane = iota((slots_m // 2, 128), 1) < 64
        out = [source[i * blocks : (i + 1) * blocks].reshape(slots_m, 128) for i in (0, 1)]
        for at in (2 * blocks, 3 * blocks, 4 * blocks):
            low = source[at : at + blocks // 2].reshape(slots_m // 2, 128)
            high = source[at + blocks // 2 : at + blocks].reshape(slots_m // 2, 128)
            even = jnp.where(lane, low, high).reshape(blocks // 2, 1, 8, 128)
            odd = pltpu.roll(jnp.where(lane, high, low), 64, 1).reshape(blocks // 2, 1, 8, 128)
            out.append(jnp.concatenate([even, odd], axis=1).reshape(slots_m, 128))
        return jnp.concatenate(out, axis=1)

    seats = [grid_of(seat, side) for seat in range(half)]

    def prepare():
        for load in loads[1:]:
            load.wait()

        if cap < len(tiles):
            count = jnp.int32(0)
            shared = shared_by_halves(grids, level_ref)
            for t, tile in enumerate(tiles):
                needed = shared[tile]
                place[t] = jnp.where(needed != 0, jnp.minimum(count, cap), cap)
                after[t] = needed
                count = count + needed
            following = jnp.int32(len(tiles) - 1)
            for t in reversed(range(len(tiles))):
                following = jnp.where(after[t] != 0, t, following)
                after[t] = following
            last = jnp.int32(-1)
            for i in range(cap):
                last = after[jnp.minimum(last + 1, len(tiles) - 1)]
                chosen[i] = last
            taken[cap] = jnp.zeros(taken.shape[1:], F32)

        weights = [[F32(0.0)] * classes_k for _ in range(classes_m)]
        for g in range(grids):
            level_m, level_k = level_ref[0, g], level_ref[2, g]
            weight = jnp.abs(coef_ref[g].astype(F32))
            for b in range(classes_k):
                size = jnp.where(level_k == b + 1, weight, 0.0)
                for a in range(classes_m):
                    weights[a][b] = weights[a][b] + jnp.where(level_m == a + 1, size, 0.0)
        sums = None
        for b in range(classes_k):
            column = None
            for a in range(classes_m):
                term = weights[a][b] * im_ref[:, a : a + 1]
                column = term if column is None else column + term
            term = column * ik_ref[b : b + 1, :]
            sums = term if sums is None else sums + term

        store_folded(inverse, 1.0 / jnp.maximum(sums, 1.0))

        for seat, g in enumerate(seats):
            at = jnp.clip(level_ref[0, g] - 1, 0, classes_m - 1)
            lines = (sm_ref[at] * coef_ref[g].astype(F32)).astype(BF16)
            tents = bm_ref[at].astype(BF16)
            for copy in range(2):
                spread[:, (copy * half + seat) * cells_m : (copy * half + seat + 1) * cells_m] = lines
                gather[seat * cells_m : (seat + 1) * cells_m, copy * slots_m : (copy + 1) * slots_m] = tents

    def cross(slot):
        return pltpu.make_async_remote_copy(
            src_ref=pack.at[slot],
            dst_ref=landed.at[slot],
            send_sem=cross_send.at[slot],
            recv_sem=cross_recv.at[slot],
            device_id={"grid": across},
            device_id_type=MESH,
        )

    def give_back(slot, peer):
        return pltpu.make_async_remote_copy(
            src_ref=res.at[slot, peer],
            dst_ref=out_ref.at[0, row_of(slot)],
            send_sem=back_send.at[slot, peer],
            recv_sem=back_recv.at[row_of(slot)],
            device_id={"grid": grid_of(peer, side)},
            device_id_type=MESH,
        )

    def class_k(seat):
        return jnp.clip(level_ref[2, seats[seat]] - 1, 0, classes_k - 1)

    def collect(slot):
        recv[slot, mine] = adv[row_of(slot)]
        for peer in peers:
            arrival(slot, peer).wait_recv()
        wide = []
        for seat in range(half):
            both = dot(jnp.concatenate(halves(recv[slot, seat]), axis=0), ek_ref[class_k(seat)])
            wide.append(halves(both[:cells_m] + both[cells_m:]))
        wide = jnp.concatenate([high for high, _ in wide] + [rest for _, rest in wide], axis=0)
        store_folded(parts.at[slot], dot(spread[...], wide))
        for i in range(cap):
            pack[slot, i] = parts[slot, chosen[i] if cap < len(tiles) else i]
        cross(slot).start()

    def release(slot):
        cross(slot).wait_recv()
        taken[0:cap] = landed[slot]
        for t in range(len(tiles)):
            total[t] = (parts[slot, t] + taken[place[t] if cap < len(tiles) else t]) * inverse[t]
        both = jnp.concatenate(halves(load_unfolded(total)), axis=0)
        field = dot(gather[...], both)
        for seat in range(half):
            part = jnp.concatenate(halves(field[seat * cells_m : (seat + 1) * cells_m]), axis=0)
            both = dot(part, tk_ref[class_k(seat)])
            res[slot, seat] = both[:cells_m] + both[cells_m:]
        for peer in peers:
            give_back(slot, peer).start()
        out_ref[0, row_of(slot)] = res[slot, mine]

    lead = 1 if half == STEPS else groups - 1
    lag = lead + LAG

    def turn(i, carry):
        pl.when(i < groups - 1)(lambda: evolve(i))
        pl.when(i == 0)(prepare)
        pl.when((i >= lead) & (i < lead + chunk))(lambda: collect(i - lead))
        pl.when((i >= lag) & (i < lag + chunk))(lambda: release(i - lag))
        return carry

    lax.fori_loop(0, max(groups - 1, lag + chunk), turn, 0)

    def finish_row(row, carry):
        owner, slot = owner_of(lax.rem(row + rows - STEPS, rows))

        @pl.when(owner != mine)
        def _():
            send(row, owner, slot).wait_send()
            pltpu.make_async_remote_copy(
                src_ref=res.at[0, 0],
                dst_ref=out_ref.at[0, row],
                send_sem=back_send.at[0, 0],
                recv_sem=back_recv.at[row],
                device_id={"grid": grid_of(owner, side)},
                device_id_type=MESH,
            ).wait_recv()

        return carry

    lax.fori_loop(0, rows, finish_row, 0)

    def finish_slot(slot, carry):
        cross(slot).wait_send()
        for peer in peers:
            give_back(slot, peer).wait_send()
        return carry

    lax.fori_loop(0, chunk, finish_slot, 0)


def staged_constants():
    surplus_m, basis_m, inside_m, surplus_k, basis_k, inside_k, _ = staged_tables()
    kinds = (F32, F32, F32, BF16, BF16, F32)
    return [jnp.asarray(a.astype(kind)) for a, kind in zip((surplus_m, basis_m, inside_m, surplus_k, basis_k, inside_k), kinds)]


def staged_call(grids, doms, cap, index, nodal_values, level_vectors, coefficients, velocity, constants):
    rows, cells_m, cells_k = nodal_values.shape[1:]
    half = grids // 2
    chunk = rows // half
    surplus_m, basis_m, inside_m, surplus_k, basis_k, inside_k, tiles = staged_tables()
    slots_m, columns = inside_m.shape[0], inside_k.shape[1]
    vmem = pl.BlockSpec(memory_space=pltpu.VMEM)
    smem = pl.BlockSpec(memory_space=pltpu.SMEM)
    hbm = pl.BlockSpec(memory_space=pltpu.HBM)
    return pl.pallas_call(
        functools.partial(staged_kernel, grids, doms, cap),
        out_shape=pltpu.VMEM(nodal_values.shape, F32),
        in_specs=[hbm, smem, smem, smem] + [hbm] * 6,
        out_specs=vmem,
        scratch_shapes=[
            pltpu.VMEM((STEPS + 1, STEPS + rows, cells_m, cells_k), F32),
            pltpu.VMEM((rows, cells_m, cells_k), F32),
            pltpu.VMEM((chunk, half, cells_m, cells_k), F32),
            pltpu.VMEM((chunk, half, cells_m, cells_k), F32),
            pltpu.VMEM((chunk, len(tiles), 8, 128), F32),
            pltpu.VMEM((chunk, cap, 8, 128), F32),
            pltpu.VMEM((chunk, cap, 8, 128), F32),
            pltpu.VMEM((cap + 1, 8, 128), F32),
            pltpu.VMEM((len(tiles), 8, 128), F32),
            pltpu.VMEM((2, cells_k, cells_k), BF16),
            pltpu.VMEM((2, STEPS * cells_m, STEPS * cells_m), BF16),
            pltpu.VMEM((slots_m, 2 * half * cells_m), BF16),
            pltpu.VMEM((half * cells_m, 2 * slots_m), BF16),
            pltpu.VMEM((len(tiles), 8, 128), F32),
            pltpu.VMEM(surplus_m.shape, F32),
            pltpu.VMEM(basis_m.shape, F32),
            pltpu.VMEM(inside_m.shape, F32),
            pltpu.VMEM(surplus_k.shape, BF16),
            pltpu.VMEM(basis_k.shape, BF16),
            pltpu.VMEM(inside_k.shape, F32),
            pltpu.SMEM((len(tiles),), jnp.int32),
            pltpu.SMEM((len(tiles),), jnp.int32),
            pltpu.SMEM((cap,), jnp.int32),
            pltpu.SemaphoreType.DMA((7,)),
            pltpu.SemaphoreType.DMA((2,)),
            pltpu.SemaphoreType.DMA((rows,)),
            pltpu.SemaphoreType.DMA((chunk, half)),
            pltpu.SemaphoreType.DMA((chunk,)),
            pltpu.SemaphoreType.DMA((chunk,)),
            pltpu.SemaphoreType.DMA((chunk, half)),
            pltpu.SemaphoreType.DMA((rows,)),
        ],
        compiler_params=pltpu.CompilerParams(
            collective_id=index, has_side_effects=True, vmem_limit_bytes=62 * 2**20 + 2**19
        ),
        name="combine_staged",
    )(
        nodal_values,
        level_vectors.T,
        coefficients,
        velocity,
        *constants,
    )


def solution(mesh):
    grids, doms = mesh.shape["grid"], mesh.shape["dom"]

    def direct(nodal_values, level_vectors, coefficients, velocity):
        rows, cells_m, cells_k = nodal_values.shape[1:]
        chunk = max(1, rows // grids)
        surplus_m, basis_m, inside_m, move_k, basis_k, inside_k = tables()
        slots = inside_m.shape[0]
        classes_k = KSUM - 1
        vmem = pl.BlockSpec(memory_space=pltpu.VMEM)
        smem = pl.BlockSpec(memory_space=pltpu.SMEM)
        hbm = pl.BlockSpec(memory_space=pltpu.HBM)
        return pl.pallas_call(
            functools.partial(direct_kernel, grids, doms),
            out_shape=pltpu.VMEM(nodal_values.shape, F32),
            in_specs=[hbm, smem, smem, smem] + [hbm] * 6,
            out_specs=vmem,
            scratch_shapes=[
                pltpu.VMEM((STEPS + 1, STEPS + rows, cells_m, cells_k), F32),
                pltpu.VMEM((rows, cells_m, cells_k), F32),
                pltpu.VMEM((chunk, grids, cells_m, cells_k), F32),
                pltpu.VMEM((chunk, grids, cells_m, cells_k), F32),
                pltpu.VMEM((2, cells_k, cells_k), BF16),
                pltpu.VMEM((2, STEPS * cells_m, STEPS * cells_m), BF16),
                pltpu.VMEM((classes_k * slots, grids * cells_m), BF16),
                pltpu.VMEM((grids * cells_m, classes_k * slots), BF16),
                pltpu.VMEM((classes_k, cells_k, classes_k * cells_k), BF16),
                pltpu.VMEM((classes_k, cells_k, cells_k), BF16),
                pltpu.VMEM((slots, classes_k * cells_k), F32),
                pltpu.VMEM(surplus_m.shape, F32),
                pltpu.VMEM(basis_m.shape, F32),
                pltpu.VMEM(inside_m.shape, F32),
                pltpu.VMEM(move_k.shape, BF16),
                pltpu.VMEM(basis_k.shape, BF16),
                pltpu.VMEM(inside_k.shape, F32),
                pltpu.SemaphoreType.DMA((7,)),
                pltpu.SemaphoreType.DMA((2,)),
                pltpu.SemaphoreType.DMA((chunk, grids)),
                pltpu.SemaphoreType.DMA((chunk, grids)),
                pltpu.SemaphoreType.DMA((chunk, grids)),
                pltpu.SemaphoreType.DMA((chunk, grids)),
            ],
            compiler_params=pltpu.CompilerParams(
                collective_id=0, has_side_effects=True, vmem_limit_bytes=62 * 2**20 + 2**19
            ),
            name="combine",
        )(
            nodal_values,
            level_vectors.T,
            coefficients,
            velocity,
            jnp.asarray(surplus_m),
            jnp.asarray(basis_m),
            jnp.asarray(inside_m),
            jnp.asarray(move_k).astype(BF16),
            jnp.asarray(basis_k).astype(BF16),
            jnp.asarray(inside_k),
        )

    def shards(nodal_values, level_vectors, coefficients, velocity):
        arrays = nodal_values, level_vectors, coefficients, velocity
        rows = nodal_values.shape[1]
        half = grids // 2
        if grids % 4 or rows % half or rows % STEPS:
            return direct(*arrays)
        count = len(staged_tables()[-1])
        raw = half * 2 ** (MLEV + KSUM + L6) // 1024
        if count < raw:
            return staged_call(grids, doms, count, 1, *arrays, staged_constants())
        caps = [raw * part // 16 for part in PARTS]
        branches = [functools.partial(staged_call, grids, doms, cap, 1 + i) for i, cap in enumerate(caps)]
        branches.append(lambda *given: direct(*given[:-1]))
        return lax.switch(choose(grids, caps, level_vectors.T), branches, *arrays, lax.optimization_barrier(staged_constants()))

    in_specs = (P("grid", "dom", None, None), P(), P(), P())
    out_specs = P("grid", "dom", None, None)
    return jax.shard_map(shards, mesh=mesh, in_specs=in_specs, out_specs=out_specs, check_vma=False)
```

```python
import functools
import math

import jax
import jax.numpy as jnp
import numpy as np
from jax import lax
from jax.experimental import pallas as pl
from jax.experimental.pallas import tpu as pltpu
from jax.sharding import PartitionSpec as P

MLEV = 6
KSUM = 5
L6 = 3
STEPS = 4
CFL_LIMIT = 0.9
LAG = 2
PARTS = (6, 7, 8, 10, 13)

MESH = pl.DeviceIdType.MESH
F32 = jnp.float32
BF16 = jnp.bfloat16


def level_of(number, finest):
    return 0 if number == 0 else finest - ((number & -number).bit_length() - 1)


def union_points(level_sum):
    finest = level_sum - 1
    return [
        (a, b)
        for a in range(2**finest)
        for b in range(2**finest)
        if level_of(a, finest) + level_of(b, finest) <= level_sum
    ]


def surplus_line(level):
    size = 2**level
    matrix = np.eye(size, dtype=np.float32)
    for target in range(1, size):
        lowest = target & -target
        matrix[(target - lowest) % size, target] -= 0.5
        matrix[(target + lowest) % size, target] -= 0.5
    return matrix


def basis_line(level):
    size = 2**level
    matrix = np.zeros((size, size), np.float32)
    matrix[0] = 1.0
    for source in range(1, size):
        lowest = source & -source
        for target in range(size):
            distance = abs(target - source)
            distance = min(distance, size - distance)
            matrix[source, target] = max(0.0, 1.0 - distance / lowest)
    return matrix


def grid_points(outer, inner, level_sum):
    finest = level_sum - 1
    return {
        (i << (finest - outer), j << (finest - inner)): i * 2**inner + j
        for i in range(2**outer)
        for j in range(2**inner)
    }


@functools.lru_cache(None)
def tables():
    slots = union_points(MLEV)
    cells = 2**MLEV
    classes_m = MLEV - 1
    surplus_m = np.zeros((classes_m, len(slots), cells), np.float32)
    basis_m = np.zeros((classes_m, cells, len(slots)), np.float32)
    inside_m = np.zeros((len(slots), 8), np.float32)
    for a in range(classes_m):
        outer, inner = a + 1, MLEV - a - 1
        lines = np.kron(surplus_line(outer), surplus_line(inner))
        tents = np.kron(basis_line(outer), basis_line(inner))
        points = grid_points(outer, inner, MLEV)
        for s, point in enumerate(slots):
            if point in points:
                surplus_m[a, s] = lines[:, points[point]]
                basis_m[a, :, s] = tents[points[point]]
                inside_m[s, a] = 1.0
    classes_k = KSUM - 1
    cells = 2**KSUM
    move_k = np.zeros((classes_k * cells, classes_k * cells), np.float32)
    basis_k = np.zeros((classes_k * cells, classes_k * cells), np.float32)
    inside_k = np.zeros((8, classes_k * cells * 2**L6), np.float32)
    for b in range(classes_k):
        outer, inner = b + 1, KSUM - b - 1
        lines = np.kron(surplus_line(outer), surplus_line(inner))
        tents = np.kron(basis_line(outer), basis_line(inner))
        block = slice(b * cells, (b + 1) * cells)
        basis_k[block, block] = tents
        points = grid_points(outer, inner, KSUM)
        for other in range(classes_k):
            for point, cell in grid_points(other + 1, KSUM - other - 1, KSUM).items():
                if point in points:
                    column = other * cells + cell
                    move_k[block, column] = lines[:, points[point]]
                    inside_k[b, column * 2**L6 : (column + 1) * 2**L6] = 1.0
    return surplus_m, basis_m, inside_m, move_k, basis_k, inside_k


def halves(x):
    high = x.astype(BF16)
    return high, (x - high.astype(F32)).astype(BF16)


def dot(a, b):
    return jnp.dot(a, b, preferred_element_type=F32)


def iota(shape, dim):
    return lax.broadcasted_iota(jnp.int32, shape, dim)


def direct_kernel(
    grids, doms, x_ref, level_ref, coef_ref, velocity_ref, sm_hbm, bm_hbm, im_hbm, mk_hbm, bk_hbm, ik_hbm,
    out_ref, power, adv, recv, res, mat_k, mat_m, spread, gather, move, basis, inverse,
    sm_ref, bm_ref, im_ref, mk_ref, bk_ref, ik_ref,
    load_sem, halo_sem, send_sem, recv_sem, back_send, back_recv,
):
    rows, cells_m, cells_k = x_ref.shape[1:]
    chunk = max(1, rows // grids)
    workers = rows // chunk
    slots = im_ref.shape[0]
    classes_m = sm_ref.shape[0]
    classes_k = mk_ref.shape[0] // 2**KSUM
    span = STEPS * cells_m
    groups = rows // STEPS + 1
    half = grids // 2
    me = lax.axis_index("grid")
    here = lax.axis_index("dom")
    above = lax.rem(here + 1, doms)
    below = lax.rem(here + doms - 1, doms)

    side, seat = lax.div(me, half), lax.rem(me, half)
    peers = [(1 - side) * half + lax.rem(seat + i, half) for i in range(half)]
    peers += [side * half + lax.rem(seat + i, half) for i in range(1, half)]

    loads = [pltpu.make_async_copy(x_ref.at[0], power.at[0, pl.ds(STEPS, rows)], load_sem.at[0])]
    for i, (source, target) in enumerate([
        (sm_hbm, sm_ref), (bm_hbm, bm_ref), (im_hbm, im_ref), (mk_hbm, mk_ref), (bk_hbm, bk_ref), (ik_hbm, ik_ref),
    ]):
        loads.append(pltpu.make_async_copy(source, target, load_sem.at[i + 1]))
    loads[0].start()

    barrier = pltpu.get_barrier_semaphore()
    for peer in peers:
        pl.semaphore_signal(barrier, inc=1, device_id={"grid": peer}, device_id_type=MESH)
    for other in (above, below):
        pl.semaphore_signal(barrier, inc=1, device_id={"dom": other}, device_id_type=MESH)
    for load in loads[1:]:
        load.start()

    def counts(g):
        return [jnp.float32(rows * doms)] + [
            lax.shift_left(jnp.int32(1), level_ref[i, g]).astype(F32) for i in range(4)
        ] + [jnp.float32(2**L6)]

    fastest = None
    for g in range(grids):
        total = None
        for d, n in enumerate(counts(g)):
            term = n * velocity_ref[d]
            total = term if total is None else total + term
        fastest = total if fastest is None else jnp.maximum(fastest, total)
    step_size = CFL_LIMIT / jnp.full((8, 128), fastest, F32)
    step_size = step_size[0:1, 0:1]
    rate = [n * velocity_ref[d] * step_size for d, n in enumerate(counts(me))]
    stay = 1.0 - rate[0] - rate[1] - rate[2] - rate[3] - rate[4] - rate[5]

    inner_k = lax.shift_left(jnp.int32(1), level_ref[3, me] + L6)
    source, target = iota((cells_k, cells_k), 0), iota((cells_k, cells_k), 1)
    matrix = jnp.where(source == target, stay, 0.0)
    matrix += jnp.where(source == ((target - inner_k) & (cells_k - 1)), rate[3], 0.0)
    low = inner_k - 1
    matrix += jnp.where(source == ((target & ~low) | ((target - 2**L6) & low)), rate[4], 0.0)
    low = 2**L6 - 1
    matrix += jnp.where(source == ((target & ~low) | ((target - 1) & low)), rate[5], 0.0)
    high, rest = halves(matrix)
    mat_k[0] = high
    mat_k[1] = rest
    inner_m = lax.shift_left(jnp.int32(1), level_ref[1, me])
    target, source = iota((span, span), 0), iota((span, span), 1)
    low = jnp.int32(cells_m - 1)
    matrix = jnp.where(source == ((target & ~low) | ((target - inner_m) & low)), rate[1], 0.0)
    low = inner_m - 1
    matrix += jnp.where(source == ((target & ~low) | ((target - 1) & low)), rate[2], 0.0)
    high, rest = halves(matrix)
    mat_m[0] = high
    mat_m[1] = rest

    def raise_group(q):
        now = power[0, pl.ds(q * STEPS, STEPS)].reshape(span, cells_k)
        for step in range(STEPS):
            high, rest = halves(now)
            now = dot(high, mat_k[0]) + dot(rest, mat_k[0]) + dot(high, mat_k[1])
            now += dot(mat_m[0], high) + dot(mat_m[0], rest) + dot(mat_m[1], high)
            power[step + 1, pl.ds(q * STEPS, STEPS)] = now.reshape(STEPS, cells_m, cells_k)

    def send(row, peer):
        return pltpu.make_async_remote_copy(
            src_ref=adv.at[peer * chunk + row],
            dst_ref=recv.at[row, me],
            send_sem=send_sem.at[row, peer],
            recv_sem=recv_sem.at[row, me],
            device_id={"grid": peer},
            device_id_type=MESH,
        )

    def arrival(row, peer):
        return pltpu.make_async_remote_copy(
            src_ref=adv.at[row],
            dst_ref=recv.at[row, peer],
            send_sem=send_sem.at[row, peer],
            recv_sem=recv_sem.at[row, peer],
            device_id={"grid": peer},
            device_id_type=MESH,
        )

    def start_send(row, peer, ready):
        if workers < grids:
            valid = peer < workers
            ready = valid if ready is None else ready & valid
        if ready is None:
            send(row, peer).start()
        else:
            pl.when(ready)(lambda: send(row, peer).start())

    def finish_group(q):
        value, factor = None, None
        for j in range(STEPS + 1):
            term = power[STEPS - j, pl.ds(q * STEPS - j, STEPS)]
            if j > 0:
                factor = rate[0] if j == 1 else factor * rate[0]
                term = term * (math.comb(STEPS, j) * factor)
            value = term if value is None else value + term
        adv[pl.ds((q - 1) * STEPS, STEPS)] = value
        for peer in peers:
            place = peer * chunk
            start_send(0, peer, (place >= (q - 1) * STEPS) & (place < q * STEPS))

    loads[0].wait()
    first = jnp.where(side == 0, groups // 2, 1)
    raise_group(first)
    pl.semaphore_wait(barrier, grids + 1)
    halo_copy = pltpu.make_async_remote_copy(
        src_ref=x_ref.at[0, pl.ds(rows - STEPS, STEPS)],
        dst_ref=power.at[0, pl.ds(0, STEPS)],
        send_sem=halo_sem.at[0],
        recv_sem=halo_sem.at[1],
        device_id={"dom": above},
        device_id_type=MESH,
    )
    halo_copy.start()

    def one(i, carry):
        q = lax.rem(first + i, groups)
        pl.when(q == 0)(halo_copy.wait)
        raise_group(q)
        pl.when(q > 0)(lambda: finish_group(q))
        return carry

    lax.fori_loop(1, groups, one, 0)
    finish_group(first)
    for row in range(1, chunk):
        for peer in peers:
            start_send(row, peer, None)

    def give_back(row, peer):
        return pltpu.make_async_remote_copy(
            src_ref=res.at[row, peer],
            dst_ref=out_ref.at[0, me * chunk + row],
            send_sem=back_send.at[row, peer],
            recv_sem=back_recv.at[row, me],
            device_id={"grid": peer},
            device_id_type=MESH,
        )

    def returned(row, peer):
        return pltpu.make_async_remote_copy(
            src_ref=res.at[row, peer],
            dst_ref=out_ref.at[0, peer * chunk + row],
            send_sem=back_send.at[row, peer],
            recv_sem=back_recv.at[row, peer],
            device_id={"grid": peer},
            device_id_type=MESH,
        )

    for load in loads[1:]:
        load.wait()

    def when_worker(body):
        if workers < grids:
            pl.when(me < workers)(body)
        else:
            body()

    @when_worker
    def _():
        for row in range(chunk):
            recv[row, me] = adv[me * chunk + row]

        weights = [[F32(0.0)] * classes_k for _ in range(classes_m)]
        for g in range(grids):
            level_m, level_k = level_ref[0, g], level_ref[2, g]
            weight = coef_ref[g].astype(F32)
            place = jnp.clip(level_m - 1, 0, classes_m - 1)
            lines = sm_ref[place]
            tents = bm_ref[place]
            for b in range(classes_k):
                match = level_k == b + 1
                spread[b * slots : (b + 1) * slots, g * cells_m : (g + 1) * cells_m] = (
                    lines * jnp.where(match, weight, 0.0)
                ).astype(BF16)
                gather[g * cells_m : (g + 1) * cells_m, b * slots : (b + 1) * slots] = (
                    tents * jnp.where(match, 1.0, 0.0)
                ).astype(BF16)
                size = jnp.where(match, jnp.abs(weight), 0.0)
                for a in range(classes_m):
                    weights[a][b] = weights[a][b] + jnp.where(level_m == a + 1, size, 0.0)
        total = None
        for b in range(classes_k):
            column = None
            for a in range(classes_m):
                term = weights[a][b] * im_ref[:, a : a + 1]
                column = term if column is None else column + term
            term = column * ik_ref[b : b + 1, :]
            total = term if total is None else total + term
        inverse[...] = 1.0 / jnp.maximum(total, 1.0)
        small = classes_k * 2**KSUM
        for b in range(classes_k):
            place = iota((cells_k, small), 0) + b * cells_k
            repeat = (lax.shift_right_logical(place, L6) == iota((cells_k, small), 1)).astype(F32)
            repeat = repeat.astype(BF16)
            left = dot(repeat, mk_ref[...]).astype(BF16)
            left_basis = dot(repeat, bk_ref[...]).astype(BF16)
            for c in range(classes_k):
                place = iota((small, cells_k), 1) + c * cells_k
                widen = (lax.shift_right_logical(place, L6) == iota((small, cells_k), 0)).astype(F32)
                widen = widen.astype(BF16)
                same = (iota((cells_k, cells_k), 0) & (2**L6 - 1)) == (
                    iota((cells_k, cells_k), 1) & (2**L6 - 1)
                )
                move[b, :, c * cells_k : (c + 1) * cells_k] = jnp.where(
                    same, dot(left, widen), 0.0
                ).astype(BF16)
                if b == c:
                    basis[b] = jnp.where(same, dot(left_basis, widen), 0.0).astype(BF16)

        for row in range(chunk):
            for peer in peers:
                arrival(row, peer).wait_recv()
            high, rest = halves(recv[row].reshape(grids * cells_m, cells_k))
            union = None
            for b in range(classes_k):
                part = spread[b * slots : (b + 1) * slots, :]
                high_b, rest_b = halves(dot(part, high) + dot(part, rest))
                term = dot(high_b, move[b]) + dot(rest_b, move[b])
                union = term if union is None else union + term
            union = union * inverse[...]
            field = None
            for b in range(classes_k):
                high_b, rest_b = halves(union[:, b * cells_k : (b + 1) * cells_k])
                high_b, rest_b = halves(dot(high_b, basis[b]) + dot(rest_b, basis[b]))
                part = gather[:, b * slots : (b + 1) * slots]
                term = dot(part, high_b) + dot(part, rest_b)
                field = term if field is None else field + term
            res[row] = field.reshape(grids, cells_m, cells_k)
            for peer in peers:
                give_back(row, peer).start()
            out_ref[0, me * chunk + row] = res[row, me]

    for row in range(chunk):
        for peer in peers:

            def finish_peer(row=row, peer=peer):
                send(row, peer).wait_send()
                returned(row, peer).wait_recv()

            if workers < grids:
                pl.when(peer < workers)(finish_peer)
            else:
                finish_peer()
            when_worker(lambda row=row, peer=peer: give_back(row, peer).wait_send())


ROUNDS_M = ((1, 1), (2, 2), (3, 3), (4, 4), (5, 5), (1, 2), (4, 5), (2, 3), (1, 3), (3, 4), (3, 5), (2, 4), (1, 4), (2, 5), (1, 5))
ROUNDS_K = ((1, 1), (4, 4), (2, 2), (1, 2), (3, 3), (3, 4), (2, 3), (1, 3), (2, 4), (1, 4))


def ordered_points(level_sum, order):
    finest = level_sum - 1
    found = {interval: [] for interval in order}
    for a, b in union_points(level_sum):
        interval = max(level_of(a, finest), 1), min(level_sum - level_of(b, finest), finest)
        found[interval].append((a, b))
    return [(point, interval) for interval in order for point in found[interval]]


def hull(intervals):
    return min(low for low, _ in intervals), max(high for _, high in intervals)


@functools.lru_cache(None)
def staged_tables():
    slots_m = ordered_points(MLEV, ROUNDS_M)
    slots_k = ordered_points(KSUM, ROUNDS_K)
    lanes = 2**L6
    count_m, count_k = len(slots_m), len(slots_k) * lanes
    surplus_m = np.zeros((MLEV - 1, count_m, 2**MLEV), np.float32)
    basis_m = np.zeros((MLEV - 1, 2**MLEV, count_m), np.float32)
    inside_m = np.zeros((count_m, 8), np.float32)
    for a in range(MLEV - 1):
        outer, inner = a + 1, MLEV - a - 1
        lines = np.kron(surplus_line(outer), surplus_line(inner))
        tents = np.kron(basis_line(outer), basis_line(inner))
        points = grid_points(outer, inner, MLEV)
        for s, (point, _) in enumerate(slots_m):
            if point in points:
                surplus_m[a, s] = lines[:, points[point]]
                basis_m[a, :, s] = tents[points[point]]
                inside_m[s, a] = 1.0
    same = np.eye(lanes, dtype=np.float32)
    cells_k = 2 ** (KSUM + L6)
    surplus_k = np.zeros((KSUM - 1, cells_k, count_k), np.float32)
    basis_k = np.zeros((KSUM - 1, count_k, cells_k), np.float32)
    inside_k = np.zeros((8, count_k), np.float32)
    for b in range(KSUM - 1):
        outer, inner = b + 1, KSUM - b - 1
        lines = np.kron(surplus_line(outer), surplus_line(inner))
        tents = np.kron(basis_line(outer), basis_line(inner))
        points = grid_points(outer, inner, KSUM)
        for s, (point, _) in enumerate(slots_k):
            if point in points:
                place = slice(s * lanes, (s + 1) * lanes)
                surplus_k[b, :, place] = np.kron(lines[:, points[point]][:, None], same)
                basis_k[b, place] = np.kron(tents[points[point]][None, :], same)
                inside_k[b, place] = 1.0
    blocks_m = [hull([slots_m[8 * t + i][1] for i in range(8)]) for t in range(count_m // 8)]
    pairs_m = [hull(blocks_m[2 * t : 2 * t + 2]) for t in range(count_m // 16)]
    per = 64 // lanes
    halves_k = [hull([slots_k[per * t + i][1] for i in range(per)]) for t in range(count_k // 64)]
    tiles = []
    for first in (0, 2):
        tiles += [(block, hull(halves_k[first : first + 2])) for block in blocks_m]
    for column in range(4, 10):
        tiles += [(pair, halves_k[column]) for pair in pairs_m]
    return surplus_m, basis_m, inside_m, surplus_k, basis_k, inside_k, tiles


def shared_by_halves(grids, level_ref):
    one = jnp.int32(1)
    present = [
        functools.reduce(
            jnp.bitwise_or,
            [lax.shift_left(one, level_ref[0, g] * KSUM + level_ref[2, g]) for g in range(first, first + grids // 2)],
        )
        for first in (0, grids // 2)
    ]
    shared = {}
    for m, k in staged_tables()[-1]:
        if (m, k) not in shared:
            inside = sum(1 << (a * KSUM + b) for a in range(m[0], m[1] + 1) for b in range(k[0], k[1] + 1))
            lower, upper = ((side & jnp.int32(inside)) != 0 for side in present)
            shared[m, k] = (lower & upper).astype(jnp.int32)
    return shared


def choice_kernel(grids, caps, level_ref, out_ref):
    tiles = staged_tables()[-1]
    count = sum(needed * tiles.count(tile) for tile, needed in shared_by_halves(grids, level_ref).items())
    out_ref[0] = sum((count > cap).astype(jnp.int32) for cap in caps)


def choose(grids, caps, levels):
    smem = pl.BlockSpec(memory_space=pltpu.SMEM)
    return pl.pallas_call(
        functools.partial(choice_kernel, grids, caps),
        out_shape=jax.ShapeDtypeStruct((1,), jnp.int32),
        in_specs=[smem],
        out_specs=smem,
        name="choose",
    )(levels)[0]


def staged_kernel(
    grids, doms, cap, x_ref, level_ref, coef_ref, velocity_ref, sm_hbm, bm_hbm, im_hbm, ek_hbm, tk_hbm, ik_hbm,
    out_ref, power, adv, recv, res, parts, pack, landed, taken, total, mat_k, mat_m, spread, gather, inverse,
    sm_ref, bm_ref, im_ref, ek_ref, tk_ref, ik_ref, after, place, chosen,
    load_sem, halo_sem, send_sem, recv_sem, cross_send, cross_recv, back_send, back_recv,
):
    rows, cells_m, cells_k = x_ref.shape[1:]
    slots_m, columns = im_ref.shape[0], ik_ref.shape[1]
    classes_m, classes_k = sm_ref.shape[0], ek_ref.shape[0]
    tiles = staged_tables()[-1]
    blocks = slots_m // 8
    span = STEPS * cells_m
    groups = rows // STEPS + 1
    half = grids // 2
    quarter = half // 2
    chunk = rows // half
    me = lax.axis_index("grid")
    here = lax.axis_index("dom")
    above = lax.rem(here + 1, doms)
    below = lax.rem(here + doms - 1, doms)
    side = lax.div(me, half)
    mine = lax.rem(me - side * half + side * quarter, half)

    def grid_of(seat, which):
        return which * half + lax.rem(seat + which * quarter, half)

    def owner_of(order):
        return lax.rem(order, half), lax.div(order, half)

    def row_of(slot):
        return lax.rem(slot * half + mine + STEPS, rows)

    peers = [lax.rem(mine + i, half) for i in range(1, half)]
    across = grid_of(mine, 1 - side)

    loads = [pltpu.make_async_copy(x_ref.at[0], power.at[0, pl.ds(STEPS, rows)], load_sem.at[0])]
    for i, (source, target) in enumerate([
        (sm_hbm, sm_ref), (bm_hbm, bm_ref), (im_hbm, im_ref), (ek_hbm, ek_ref), (tk_hbm, tk_ref), (ik_hbm, ik_ref),
    ]):
        loads.append(pltpu.make_async_copy(source, target, load_sem.at[i + 1]))
    loads[0].start()

    barrier = pltpu.get_barrier_semaphore()
    for peer in peers:
        pl.semaphore_signal(barrier, inc=1, device_id={"grid": grid_of(peer, side)}, device_id_type=MESH)
    pl.semaphore_signal(barrier, inc=1, device_id={"grid": across}, device_id_type=MESH)
    for other in (above, below):
        pl.semaphore_signal(barrier, inc=1, device_id={"dom": other}, device_id_type=MESH)
    for load in loads[1:]:
        load.start()

    def counts(g):
        return [jnp.float32(rows * doms)] + [
            lax.shift_left(jnp.int32(1), level_ref[i, g]).astype(F32) for i in range(4)
        ] + [jnp.float32(2**L6)]

    fastest = None
    for g in range(grids):
        size = None
        for d, n in enumerate(counts(g)):
            term = n * velocity_ref[d]
            size = term if size is None else size + term
        fastest = size if fastest is None else jnp.maximum(fastest, size)
    step_size = CFL_LIMIT / jnp.full((8, 128), fastest, F32)
    step_size = step_size[0:1, 0:1]
    rate = [n * velocity_ref[d] * step_size for d, n in enumerate(counts(me))]
    stay = 1.0 - rate[0] - rate[1] - rate[2] - rate[3] - rate[4] - rate[5]

    inner_k = lax.shift_left(jnp.int32(1), level_ref[3, me] + L6)
    source, target = iota((cells_k, cells_k), 0), iota((cells_k, cells_k), 1)
    matrix = jnp.where(source == target, stay, 0.0)
    matrix += jnp.where(source == ((target - inner_k) & (cells_k - 1)), rate[3], 0.0)
    low = inner_k - 1
    matrix += jnp.where(source == ((target & ~low) | ((target - 2**L6) & low)), rate[4], 0.0)
    low = 2**L6 - 1
    matrix += jnp.where(source == ((target & ~low) | ((target - 1) & low)), rate[5], 0.0)
    high, rest = halves(matrix)
    mat_k[0] = high
    mat_k[1] = rest
    inner_m = lax.shift_left(jnp.int32(1), level_ref[1, me])
    target, source = iota((span, span), 0), iota((span, span), 1)
    low = jnp.int32(cells_m - 1)
    matrix = jnp.where(source == ((target & ~low) | ((target - inner_m) & low)), rate[1], 0.0)
    low = inner_m - 1
    matrix += jnp.where(source == ((target & ~low) | ((target - 1) & low)), rate[2], 0.0)
    high, rest = halves(matrix)
    mat_m[0] = high
    mat_m[1] = rest

    def raise_group(q, carry=None):
        now = power[0, pl.ds(q * STEPS, STEPS)].reshape(span, cells_k)
        for step in range(STEPS):
            high, rest = halves(now)
            now = dot(high, mat_k[0]) + dot(rest, mat_k[0]) + dot(high, mat_k[1])
            now += dot(mat_m[0], high) + dot(mat_m[0], rest) + dot(mat_m[1], high)
            power[step + 1, pl.ds(q * STEPS, STEPS)] = now.reshape(STEPS, cells_m, cells_k)
        return carry

    def send(row, owner, slot):
        return pltpu.make_async_remote_copy(
            src_ref=adv.at[row],
            dst_ref=recv.at[slot, mine],
            send_sem=send_sem.at[row],
            recv_sem=recv_sem.at[slot, mine],
            device_id={"grid": grid_of(owner, side)},
            device_id_type=MESH,
        )

    def arrival(slot, peer):
        return pltpu.make_async_remote_copy(
            src_ref=adv.at[0],
            dst_ref=recv.at[slot, peer],
            send_sem=send_sem.at[0],
            recv_sem=recv_sem.at[slot, peer],
            device_id={"grid": grid_of(peer, side)},
            device_id_type=MESH,
        )

    def finish_group(q):
        value, factor = None, None
        for j in range(STEPS + 1):
            term = power[STEPS - j, pl.ds(q * STEPS - j, STEPS)]
            if j > 0:
                factor = rate[0] if j == 1 else factor * rate[0]
                term = term * (math.comb(STEPS, j) * factor)
            value = term if value is None else value + term
        adv[pl.ds((q - 1) * STEPS, STEPS)] = value
        for j in range(STEPS):
            row = (q - 1) * STEPS + j
            owner, slot = owner_of(lax.rem(row + rows - STEPS, rows))
            pl.when(owner != mine)(lambda row=row, owner=owner, slot=slot: send(row, owner, slot).start())

    loads[0].wait()
    first = 1
    lax.fori_loop(first, first + 2, raise_group, None)
    pl.semaphore_wait(barrier, half + 2)
    halo_copy = pltpu.make_async_remote_copy(
        src_ref=x_ref.at[0, pl.ds(rows - STEPS, STEPS)],
        dst_ref=power.at[0, pl.ds(0, STEPS)],
        send_sem=halo_sem.at[0],
        recv_sem=halo_sem.at[1],
        device_id={"dom": above},
        device_id_type=MESH,
    )
    halo_copy.start()

    def evolve(i):
        q = lax.rem(first + 1 + i, groups)
        pl.when(q == 0)(halo_copy.wait)
        pl.when(i > 0)(lambda: raise_group(q))
        finish_group(jnp.where(q == 0, first, q))

    def fold(values):
        lane = iota((slots_m // 2, 128), 1) < 64
        out = [values[:, :128], values[:, 128:256]]
        for first in (256, 384, 512):
            pair = values[:, first : first + 128].reshape(blocks // 2, 2, 8, 128)
            even = pair[:, 0].reshape(slots_m // 2, 128)
            odd = pltpu.roll(pair[:, 1].reshape(slots_m // 2, 128), 64, 1)
            out += [jnp.where(lane, even, odd), jnp.where(lane, odd, even)]
        return out

    def store_folded(target, values):
        at = 0
        for part in fold(values):
            size = part.shape[0] // 8
            target[at : at + size] = part.reshape(size, 8, 128)
            at += size

    def load_unfolded(source):
        lane = iota((slots_m // 2, 128), 1) < 64
        out = [source[i * blocks : (i + 1) * blocks].reshape(slots_m, 128) for i in (0, 1)]
        for at in (2 * blocks, 3 * blocks, 4 * blocks):
            low = source[at : at + blocks // 2].reshape(slots_m // 2, 128)
            high = source[at + blocks // 2 : at + blocks].reshape(slots_m // 2, 128)
            even = jnp.where(lane, low, high).reshape(blocks // 2, 1, 8, 128)
            odd = pltpu.roll(jnp.where(lane, high, low), 64, 1).reshape(blocks // 2, 1, 8, 128)
            out.append(jnp.concatenate([even, odd], axis=1).reshape(slots_m, 128))
        return jnp.concatenate(out, axis=1)

    seats = [grid_of(seat, side) for seat in range(half)]

    def prepare():
        for load in loads[1:]:
            load.wait()

        if cap < len(tiles):
            count = jnp.int32(0)
            shared = shared_by_halves(grids, level_ref)
            for t, tile in enumerate(tiles):
                needed = shared[tile]
                place[t] = jnp.where(needed != 0, jnp.minimum(count, cap), cap)
                after[t] = needed
                count = count + needed
            following = jnp.int32(len(tiles) - 1)
            for t in reversed(range(len(tiles))):
                following = jnp.where(after[t] != 0, t, following)
                after[t] = following
            last = jnp.int32(-1)
            for i in range(cap):
                last = after[jnp.minimum(last + 1, len(tiles) - 1)]
                chosen[i] = last
            taken[cap] = jnp.zeros(taken.shape[1:], F32)

        weights = [[F32(0.0)] * classes_k for _ in range(classes_m)]
        for g in range(grids):
            level_m, level_k = level_ref[0, g], level_ref[2, g]
            weight = jnp.abs(coef_ref[g].astype(F32))
            for b in range(classes_k):
                size = jnp.where(level_k == b + 1, weight, 0.0)
                for a in range(classes_m):
                    weights[a][b] = weights[a][b] + jnp.where(level_m == a + 1, size, 0.0)
        sums = None
        for b in range(classes_k):
            column = None
            for a in range(classes_m):
                term = weights[a][b] * im_ref[:, a : a + 1]
                column = term if column is None else column + term
            term = column * ik_ref[b : b + 1, :]
            sums = term if sums is None else sums + term

        store_folded(inverse, 1.0 / jnp.maximum(sums, 1.0))

        for seat, g in enumerate(seats):
            at = jnp.clip(level_ref[0, g] - 1, 0, classes_m - 1)
            lines = (sm_ref[at] * coef_ref[g].astype(F32)).astype(BF16)
            tents = bm_ref[at].astype(BF16)
            for copy in range(2):
                spread[:, (copy * half + seat) * cells_m : (copy * half + seat + 1) * cells_m] = lines
                gather[seat * cells_m : (seat + 1) * cells_m, copy * slots_m : (copy + 1) * slots_m] = tents

    def cross(slot):
        return pltpu.make_async_remote_copy(
            src_ref=pack.at[slot],
            dst_ref=landed.at[slot],
            send_sem=cross_send.at[slot],
            recv_sem=cross_recv.at[slot],
            device_id={"grid": across},
            device_id_type=MESH,
        )

    def give_back(slot, peer):
        return pltpu.make_async_remote_copy(
            src_ref=res.at[slot, peer],
            dst_ref=out_ref.at[0, row_of(slot)],
            send_sem=back_send.at[slot, peer],
            recv_sem=back_recv.at[row_of(slot)],
            device_id={"grid": grid_of(peer, side)},
            device_id_type=MESH,
        )

    def class_k(seat):
        return jnp.clip(level_ref[2, seats[seat]] - 1, 0, classes_k - 1)

    def collect(slot):
        recv[slot, mine] = adv[row_of(slot)]
        for peer in peers:
            arrival(slot, peer).wait_recv()
        wide = []
        for seat in range(half):
            both = dot(jnp.concatenate(halves(recv[slot, seat]), axis=0), ek_ref[class_k(seat)])
            wide.append(halves(both[:cells_m] + both[cells_m:]))
        wide = jnp.concatenate([high for high, _ in wide] + [rest for _, rest in wide], axis=0)
        store_folded(parts.at[slot], dot(spread[...], wide))
        for i in range(cap):
            pack[slot, i] = parts[slot, chosen[i] if cap < len(tiles) else i]
        cross(slot).start()

    def release(slot):
        cross(slot).wait_recv()
        taken[0:cap] = landed[slot]
        for t in range(len(tiles)):
            total[t] = (parts[slot, t] + taken[place[t] if cap < len(tiles) else t]) * inverse[t]
        both = jnp.concatenate(halves(load_unfolded(total)), axis=0)
        field = dot(gather[...], both)
        for seat in range(half):
            part = jnp.concatenate(halves(field[seat * cells_m : (seat + 1) * cells_m]), axis=0)
            both = dot(part, tk_ref[class_k(seat)])
            res[slot, seat] = both[:cells_m] + both[cells_m:]
        for peer in peers:
            give_back(slot, peer).start()
        out_ref[0, row_of(slot)] = res[slot, mine]

    lead = 1 if half == STEPS else groups - 1
    lag = lead + LAG

    def turn(i, carry):
        pl.when(i < groups - 1)(lambda: evolve(i))
        pl.when(i == 0)(prepare)
        pl.when((i >= lead) & (i < lead + chunk))(lambda: collect(i - lead))
        pl.when((i >= lag) & (i < lag + chunk))(lambda: release(i - lag))
        return carry

    lax.fori_loop(0, max(groups - 1, lag + chunk), turn, 0)

    def finish_row(row, carry):
        owner, slot = owner_of(lax.rem(row + rows - STEPS, rows))

        @pl.when(owner != mine)
        def _():
            send(row, owner, slot).wait_send()
            pltpu.make_async_remote_copy(
                src_ref=res.at[0, 0],
                dst_ref=out_ref.at[0, row],
                send_sem=back_send.at[0, 0],
                recv_sem=back_recv.at[row],
                device_id={"grid": grid_of(owner, side)},
                device_id_type=MESH,
            ).wait_recv()

        return carry

    lax.fori_loop(0, rows, finish_row, 0)

    def finish_slot(slot, carry):
        cross(slot).wait_send()
        for peer in peers:
            give_back(slot, peer).wait_send()
        return carry

    lax.fori_loop(0, chunk, finish_slot, 0)


def staged_constants():
    surplus_m, basis_m, inside_m, surplus_k, basis_k, inside_k, _ = staged_tables()
    kinds = (F32, F32, F32, BF16, BF16, F32)
    return [jnp.asarray(a.astype(kind)) for a, kind in zip((surplus_m, basis_m, inside_m, surplus_k, basis_k, inside_k), kinds)]


def staged_call(grids, doms, cap, index, nodal_values, level_vectors, coefficients, velocity, constants):
    rows, cells_m, cells_k = nodal_values.shape[1:]
    half = grids // 2
    chunk = rows // half
    surplus_m, basis_m, inside_m, surplus_k, basis_k, inside_k, tiles = staged_tables()
    slots_m, columns = inside_m.shape[0], inside_k.shape[1]
    vmem = pl.BlockSpec(memory_space=pltpu.VMEM)
    smem = pl.BlockSpec(memory_space=pltpu.SMEM)
    hbm = pl.BlockSpec(memory_space=pltpu.HBM)
    return pl.pallas_call(
        functools.partial(staged_kernel, grids, doms, cap),
        out_shape=pltpu.VMEM(nodal_values.shape, F32),
        in_specs=[hbm, smem, smem, smem] + [hbm] * 6,
        out_specs=vmem,
        scratch_shapes=[
            pltpu.VMEM((STEPS + 1, STEPS + rows, cells_m, cells_k), F32),
            pltpu.VMEM((rows, cells_m, cells_k), F32),
            pltpu.VMEM((chunk, half, cells_m, cells_k), F32),
            pltpu.VMEM((chunk, half, cells_m, cells_k), F32),
            pltpu.VMEM((chunk, len(tiles), 8, 128), F32),
            pltpu.VMEM((chunk, cap, 8, 128), F32),
            pltpu.VMEM((chunk, cap, 8, 128), F32),
            pltpu.VMEM((cap + 1, 8, 128), F32),
            pltpu.VMEM((len(tiles), 8, 128), F32),
            pltpu.VMEM((2, cells_k, cells_k), BF16),
            pltpu.VMEM((2, STEPS * cells_m, STEPS * cells_m), BF16),
            pltpu.VMEM((slots_m, 2 * half * cells_m), BF16),
            pltpu.VMEM((half * cells_m, 2 * slots_m), BF16),
            pltpu.VMEM((len(tiles), 8, 128), F32),
            pltpu.VMEM(surplus_m.shape, F32),
            pltpu.VMEM(basis_m.shape, F32),
            pltpu.VMEM(inside_m.shape, F32),
            pltpu.VMEM(surplus_k.shape, BF16),
            pltpu.VMEM(basis_k.shape, BF16),
            pltpu.VMEM(inside_k.shape, F32),
            pltpu.SMEM((len(tiles),), jnp.int32),
            pltpu.SMEM((len(tiles),), jnp.int32),
            pltpu.SMEM((cap,), jnp.int32),
            pltpu.SemaphoreType.DMA((7,)),
            pltpu.SemaphoreType.DMA((2,)),
            pltpu.SemaphoreType.DMA((rows,)),
            pltpu.SemaphoreType.DMA((chunk, half)),
            pltpu.SemaphoreType.DMA((chunk,)),
            pltpu.SemaphoreType.DMA((chunk,)),
            pltpu.SemaphoreType.DMA((chunk, half)),
            pltpu.SemaphoreType.DMA((rows,)),
        ],
        compiler_params=pltpu.CompilerParams(
            collective_id=index, has_side_effects=True, vmem_limit_bytes=62 * 2**20 + 2**19
        ),
        name="combine_staged",
    )(
        nodal_values,
        level_vectors.T,
        coefficients,
        velocity,
        *constants,
    )


def solution(mesh):
    grids, doms = mesh.shape["grid"], mesh.shape["dom"]

    def direct(nodal_values, level_vectors, coefficients, velocity):
        rows, cells_m, cells_k = nodal_values.shape[1:]
        chunk = max(1, rows // grids)
        surplus_m, basis_m, inside_m, move_k, basis_k, inside_k = tables()
        slots = inside_m.shape[0]
        classes_k = KSUM - 1
        vmem = pl.BlockSpec(memory_space=pltpu.VMEM)
        smem = pl.BlockSpec(memory_space=pltpu.SMEM)
        hbm = pl.BlockSpec(memory_space=pltpu.HBM)
        return pl.pallas_call(
            functools.partial(direct_kernel, grids, doms),
            out_shape=pltpu.VMEM(nodal_values.shape, F32),
            in_specs=[hbm, smem, smem, smem] + [hbm] * 6,
            out_specs=vmem,
            scratch_shapes=[
                pltpu.VMEM((STEPS + 1, STEPS + rows, cells_m, cells_k), F32),
                pltpu.VMEM((rows, cells_m, cells_k), F32),
                pltpu.VMEM((chunk, grids, cells_m, cells_k), F32),
                pltpu.VMEM((chunk, grids, cells_m, cells_k), F32),
                pltpu.VMEM((2, cells_k, cells_k), BF16),
                pltpu.VMEM((2, STEPS * cells_m, STEPS * cells_m), BF16),
                pltpu.VMEM((classes_k * slots, grids * cells_m), BF16),
                pltpu.VMEM((grids * cells_m, classes_k * slots), BF16),
                pltpu.VMEM((classes_k, cells_k, classes_k * cells_k), BF16),
                pltpu.VMEM((classes_k, cells_k, cells_k), BF16),
                pltpu.VMEM((slots, classes_k * cells_k), F32),
                pltpu.VMEM(surplus_m.shape, F32),
                pltpu.VMEM(basis_m.shape, F32),
                pltpu.VMEM(inside_m.shape, F32),
                pltpu.VMEM(move_k.shape, BF16),
                pltpu.VMEM(basis_k.shape, BF16),
                pltpu.VMEM(inside_k.shape, F32),
                pltpu.SemaphoreType.DMA((7,)),
                pltpu.SemaphoreType.DMA((2,)),
                pltpu.SemaphoreType.DMA((chunk, grids)),
                pltpu.SemaphoreType.DMA((chunk, grids)),
                pltpu.SemaphoreType.DMA((chunk, grids)),
                pltpu.SemaphoreType.DMA((chunk, grids)),
            ],
            compiler_params=pltpu.CompilerParams(
                collective_id=0, has_side_effects=True, vmem_limit_bytes=62 * 2**20 + 2**19
            ),
            name="combine",
        )(
            nodal_values,
            level_vectors.T,
            coefficients,
            velocity,
            jnp.asarray(surplus_m),
            jnp.asarray(basis_m),
            jnp.asarray(inside_m),
            jnp.asarray(move_k).astype(BF16),
            jnp.asarray(basis_k).astype(BF16),
            jnp.asarray(inside_k),
        )

    def shards(nodal_values, level_vectors, coefficients, velocity):
        arrays = nodal_values, level_vectors, coefficients, velocity
        rows = nodal_values.shape[1]
        half = grids // 2
        if grids % 4 or rows % half or rows % STEPS:
            return direct(*arrays)
        count = len(staged_tables()[-1])
        raw = half * 2 ** (MLEV + KSUM + L6) // 1024
        if count < raw:
            return staged_call(grids, doms, count, 1, *arrays, staged_constants())
        caps = [raw * part // 16 for part in PARTS]
        branches = [functools.partial(staged_call, grids, doms, cap, 1 + i) for i, cap in enumerate(caps + [count])]
        choice = choose(grids, caps, level_vectors.T)
        return lax.switch(choice, branches, *arrays, lax.optimization_barrier(staged_constants()))

    in_specs = (P("grid", "dom", None, None), P(), P(), P())
    out_specs = P("grid", "dom", None, None)
    return jax.shard_map(shards, mesh=mesh, in_specs=in_specs, out_specs=out_specs, check_vma=False)
```
